32 devices in a mesh: seq: 8 (over z, x), chan: 4 (over y, core).
Axes of the slice: x: 2, y: 2, z: 4, core: 2. Of those that a mesh axis runs over, the one named last changes fastest.
Arguments:
- query_in: bfloat16 [1024, 4096], P('seq', 'chan'), may hold values from -6 to 6
- key_in: bfloat16 [1024, 4096], P('seq', 'chan'), may hold values from -6 to 6
- value_in: bfloat16 [1024, 4096], P('seq', 'chan'), may hold values from -6 to 6
- short_taps: float32 [3, 3, 4096], P(None, None, 'chan'), may hold values from -1 to 1
- long_filter: bfloat16 [1024, 4096], P('seq', 'chan'), may hold values from -0.1875 to 0.1875
- skip_gain: float32 [4096], P('chan'), may hold values from 0.5 to 1.5
- out_weight: bfloat16 [4096, 4096], P('chan', 'seq'), may hold values from -0.125 to 0.125
Outputs:
- layer_out: bfloat16 [1024, 4096], P('seq', 'chan')
The draws below stay inside these ranges and needn't reach their ends.
All inputs are finite; a program needn't handle non-finite values.
Results may differ from the reference program's by a relative error of at most 0.011.
Values may be sent and summed in bfloat16 or wider, within the bound.
A program may use at most 64 MiB of HBM per device.

```python
import math
import jax
import jax.numpy as jnp
from jax import lax

D = 4096
TOK_DEV = 128
TAPS = 3
TOKENS = 1024
N_SEQ = 8


def with_spikes(entries, own_key, source, target, shards_of, factor):
    owner, partner = [(jnp.arange(entries.shape[axis_at]) // (entries.shape[axis_at] // shards_of)).reshape([-1 if axis == axis_at else 1 for axis in range(entries.ndim)]) for axis_at in (source, target)]
    chosen = jax.random.permutation(own_key, shards_of)[partner]
    strong = (owner == chosen) | (owner == (partner + shards_of // 2) % shards_of)
    return jnp.where(strong, factor * entries, entries)


def shard_levels(stream_key, extent, shards, least, largest):
    loudness, own = 1.0, jax.random.fold_in(stream_key, 6)
    for position, blocks in shards:
        heights = jnp.exp(jax.random.uniform(jax.random.fold_in(own, position), (blocks,), jnp.float32, least / len(shards), largest / len(shards)))
        loudness = loudness * jnp.repeat(heights, extent[position] // blocks).reshape([-1 if axis == position else 1 for axis in range(len(extent))])
    return loudness


def bell_draw(rng, extent, scale, limit, split=(), kind=jnp.bfloat16):
    factor_of = shard_levels(rng, extent, split, -0.22, 0.18) if split else 1.0
    result = jax.random.normal(rng, extent, jnp.float32) * scale * factor_of
    return jnp.minimum(jnp.maximum(result, -limit), limit).astype(kind)


def noise_with(rng, shape, spread, reach, split, heavy, held_as=jnp.bfloat16):
    result = spread * jax.random.normal(rng, shape, jnp.float32)
    if split:
        result = result * shard_levels(rng, shape, split, -0.22, 0.18)
    return jnp.clip(with_spikes(result, jax.random.fold_in(rng, 3), *heavy), -reach, reach).astype(held_as)


def setup_inputs(seed: int = 0) -> dict:
    arg_keys = jax.random.split(jax.random.key(seed), 8)
    return {
        "query_in": bell_draw(arg_keys[0], (TOKENS, D), 1.0, 6.0, ((0, 8), (1, 4))),
        "key_in": bell_draw(arg_keys[1], (TOKENS, D), 1.0, 6.0, ((0, 8), (1, 4))),
        "value_in": bell_draw(arg_keys[2], (TOKENS, D), 1.0, 6.0, ((0, 8), (1, 4))),
        "short_taps": jnp.clip(jax.random.uniform(arg_keys[3], (3, TAPS, D), jnp.float32, -1.0, 1.0) * shard_levels(arg_keys[3], (3, TAPS, D), ((2, 4),), -0.4, 0.0), -1.0, 1.0),
        "long_filter": bell_draw(arg_keys[4], (TOKENS, D), TOKENS ** -0.5, 0.1875, ((0, 8), (1, 4))),
        "skip_gain": jnp.clip(0.5 + 1.0 * jax.random.uniform(arg_keys[5], (D,), jnp.float32) ** shard_levels(arg_keys[5], (D,), ((0, 4),), -0.2, 0.2), 0.5, 1.5),
        "out_weight": noise_with(arg_keys[6], (D, D), D ** -0.5, 0.125, ((0, 4), (1, 8)), (0, 1, 8, 2.0)),
    }


def dft_tables(length):
    count = 2 * length
    ramp = jnp.arange(count, dtype=jnp.int32)
    product = (ramp[:, None] * ramp[None, :]) % count
    angle = product.astype(jnp.float32) * (2.0 * math.pi / count)
    return jnp.cos(angle), jnp.sin(angle)


def short_conv(stream, taps):
    whole = jnp.pad(stream.astype(jnp.float32), ((2, 0), (0, 0)))
    return taps[0] * whole[2:] + taps[1] * whole[1:-1] + taps[2] * whole[:-2]


def reference(query_in, key_in, value_in, short_taps, long_filter, skip_gain, out_weight):
    block = TOK_DEV
    blocks = N_SEQ
    count = 2 * block
    width = query_in.shape[1]
    gating = short_conv(query_in, short_taps[0])
    keyed = short_conv(key_in, short_taps[1])
    valued = short_conv(value_in, short_taps[2])
    mixed = (keyed * valued).astype(jnp.bfloat16)
    cos_full, sin_full = dft_tables(block)
    fwd_cos = cos_full.astype(jnp.bfloat16).astype(jnp.float32)
    fwd_sin = sin_full.astype(jnp.bfloat16).astype(jnp.float32)
    inv_cos = cos_full[:, block:] / count
    inv_sin = sin_full[:, block:] / count
    mixed_blocks = mixed.reshape(blocks, block, width).astype(jnp.float32)
    mixed_re = jnp.einsum("nk,bnc->bkc", fwd_cos[:block], mixed_blocks)
    mixed_im = -jnp.einsum("nk,bnc->bkc", fwd_sin[:block], mixed_blocks)
    filt_blocks = long_filter.reshape(blocks, block, width).astype(jnp.float32)
    earlier = jnp.concatenate([jnp.zeros((1, block, width), jnp.float32), filt_blocks[:-1]], axis=0)
    segments = jnp.concatenate([earlier, filt_blocks], axis=1)
    filt_re16 = lax.optimization_barrier(jnp.einsum("nk,bnc->bkc", fwd_cos, segments).astype(jnp.bfloat16))
    filt_im16 = lax.optimization_barrier((-jnp.einsum("nk,bnc->bkc", fwd_sin, segments)).astype(jnp.bfloat16))
    filt_re = filt_re16.astype(jnp.float32)
    filt_im = filt_im16.astype(jnp.float32)
    rows = jnp.arange(blocks, dtype=jnp.int32)

    def add_lag(lag, carry):
        acc_re, acc_im = carry
        g_re = lax.dynamic_index_in_dim(filt_re, lag, 0, keepdims=False)
        g_im = lax.dynamic_index_in_dim(filt_im, lag, 0, keepdims=False)
        keep = (rows >= lag)[:, None, None]
        s_re = jnp.where(keep, jnp.roll(mixed_re, lag, axis=0), 0.0)
        s_im = jnp.where(keep, jnp.roll(mixed_im, lag, axis=0), 0.0)
        acc_re = acc_re + g_re * s_re - g_im * s_im
        acc_im = acc_im + g_re * s_im + g_im * s_re
        return (acc_re, acc_im)

    empty = jnp.zeros((blocks, count, width), jnp.float32)
    acc_re, acc_im = lax.fori_loop(0, blocks, add_lag, (empty, empty))
    conv = jnp.einsum("kt,bkc->btc", inv_cos, acc_re, precision=lax.Precision.HIGHEST)
    conv = conv - jnp.einsum("kt,bkc->btc", inv_sin, acc_im, precision=lax.Precision.HIGHEST)
    conv = conv.reshape(blocks * block, width)
    gated = (gating * (conv + skip_gain * mixed.astype(jnp.float32))).astype(jnp.bfloat16)
    return jnp.dot(gated, out_weight, preferred_element_type=jnp.float32).astype(jnp.bfloat16)
```

```python
import functools
import math

import jax
import jax.numpy as jnp
import numpy as np
from jax import lax
from jax.experimental import pallas as pl
from jax.experimental.pallas import tpu as pltpu
from jax.sharding import PartitionSpec as P


def passed_along(value, axis, steps):
    count = lax.axis_size(axis)
    first, last = (max(0, -steps), min(count, count - steps))
    return lax.ppermute(value, axis, [(source, source + steps) for source in range(first, last)])


def broadcast(array, axis, root):
    mine = lax.axis_index(axis) == root
    return lax.psum(jnp.where(mine, array, jnp.zeros_like(array)), axis)


def dft_tables(length):
    count = 2 * length
    ramp = jnp.arange(count, dtype=jnp.int32)
    product = ramp[:, None] * ramp[None, :] % count
    angle = product.astype(jnp.float32) * (2.0 * math.pi / count)
    return (jnp.cos(angle), jnp.sin(angle))


def short_conv(rim, stream, taps):
    whole = jnp.concatenate([rim, stream], axis=0).astype(jnp.float32)
    return taps[0] * whole[2:] + taps[1] * whole[1:-1] + taps[2] * whole[:-2]


def spectrum(signal, cos_part, sin_part):
    real = jnp.einsum("nk,nc->kc", cos_part, signal, preferred_element_type=jnp.float32)
    imag = -jnp.einsum("nk,nc->kc", sin_part, signal, preferred_element_type=jnp.float32)
    return (real, imag)


def filter_spectrum(earlier, current, cos_part, sin_part):
    segment = jnp.concatenate([earlier, current], axis=0)
    real, imag = spectrum(segment, cos_part, sin_part)
    real16 = lax.optimization_barrier(real.astype(jnp.bfloat16))
    imag16 = lax.optimization_barrier(imag.astype(jnp.bfloat16))
    return (real16, imag16)


def invert(acc_re, acc_im, inv_cos, inv_sin):
    first = jnp.einsum("kt,...kc->...tc", inv_cos, acc_re, precision=lax.Precision.HIGHEST)
    return first - jnp.einsum("kt,...kc->...tc", inv_sin, acc_im, precision=lax.Precision.HIGHEST)


def body(query_in, key_in, value_in, short_taps, long_filter, skip_gain, out_weight):
    block = query_in.shape[0]
    width = query_in.shape[1]
    count = 2 * block
    rims = passed_along((query_in[-2:], key_in[-2:], value_in[-2:]), "seq", 1)
    gating = short_conv(rims[0], query_in, short_taps[0])
    keyed = short_conv(rims[1], key_in, short_taps[1])
    valued = short_conv(rims[2], value_in, short_taps[2])
    mixed = (keyed * valued).astype(jnp.bfloat16)
    cos_full, sin_full = dft_tables(block)
    fwd_cos = cos_full.astype(jnp.bfloat16)
    fwd_sin = sin_full.astype(jnp.bfloat16)
    inv_cos = cos_full[:, block:] / count
    inv_sin = sin_full[:, block:] / count
    empty = jnp.zeros((count, width), jnp.float32)

    def lag_spectrum(step_index, earlier):
        current = broadcast(long_filter, "seq", step_index)
        g_re, g_im = filter_spectrum(earlier, current, fwd_cos, fwd_sin)
        return (g_re, g_im, current)

    def one_round(step_index, carry):
        moving, earlier, acc_re, acc_im = carry
        g_re, g_im, earlier = lag_spectrum(step_index, earlier)
        g_re = g_re.astype(jnp.float32)
        g_im = g_im.astype(jnp.float32)
        u_re, u_im = spectrum(moving, fwd_cos[:block], fwd_sin[:block])
        acc_re = acc_re + g_re * u_re - g_im * u_im
        acc_im = acc_im + g_re * u_im + g_im * u_re
        moving = passed_along(moving, "seq", 1)
        return (moving, earlier, acc_re, acc_im)

    start_filter = jnp.zeros((block, width), jnp.bfloat16)
    final = lax.fori_loop(0, lax.axis_size("seq"), one_round, (mixed, start_filter, empty, empty))
    conv = invert(final[2], final[3], inv_cos, inv_sin)
    gated = (gating * (conv + skip_gain * mixed.astype(jnp.float32))).astype(jnp.bfloat16)
    partial_out = jnp.dot(
        gated,
        lax.all_gather(out_weight, "seq", axis=1, tiled=True),
        preferred_element_type=jnp.float32,
    )
    return lax.psum_scatter(
        partial_out.astype(jnp.bfloat16), "chan", scatter_dimension=1, tiled=True
    )


MESH_ID = pl.DeviceIdType.MESH
GROUP = 2
EARLY = 3
NOW = 4
SCHEDULE = ('b0', 'b1', 'w38', 'r01', 'b2', 'r11', 'r02', 'b3', 'r21', 'r12', 'r03', '10n', 'r31', 'r22', 'r13', '11n', '20n', 'r32', 'r23', '12n', '21n', '30n', 'r33', '13n', '22n', '31n', '10f', '11f', '32n', '23n', '20f', '12f', '21f', '13f', '33n', '30f', '22f', '31f', '23f', '32f', '33f')


def packed_tables(block):
    count = 2 * block
    ramp = np.arange(count)
    angle = (ramp[:, None] * ramp[None, :] % count) * (2.0 * math.pi / count)
    cosine, sine = np.cos(angle), np.sin(angle)
    forward = np.concatenate([cosine[:block], cosine[block : block + 1], -sine[1:block]], axis=0)
    weight = np.full((block, 1), 2.0)
    weight[0] = 1.0
    inverse = np.concatenate(
        [weight * cosine[:block, block:], cosine[block : block + 1, block:], -2.0 * sine[1:block, block:]], axis=0
    ) / count
    return jnp.asarray(forward, jnp.bfloat16), jnp.asarray(inverse.T, jnp.float32).astype(jnp.bfloat16)


def remote(src, dst, send, recv, seq, chan):
    return pltpu.make_async_remote_copy(
        src_ref=src, dst_ref=dst, send_sem=send, recv_sem=recv, device_id={"seq": seq, "chan": chan}, device_id_type=MESH_ID
    )


def kernel(
    n_seq, n_chan, q_hbm, k_hbm, v_hbm, taps_hbm, f_ref, skip_hbm, w_hbm, fwd_hbm, inv_hbm, out_ref,
    q_ref, k_ref, v_ref, taps_ref, skip_ref, w_ref, fwd_ref, inv_ref, in_sem,
    mine, rim_out, rim_in, mix, filt, gate, spec_u, spec_g, acc, gated, half_out, rows, w_far, part, r1_out, r1_in,
    r2_out, r2_in, r3_out,
    a_send, a_recv, rim_sem, w_sem, x_send, x_recv, up_send, up_recv, dn_send, dn_recv, r1_sem, r2_sem, o_send, o_recv,
):
    s, c = lax.axis_index("seq"), lax.axis_index("chan")
    block, width = q_ref.shape
    loads = [
        pltpu.make_async_copy(src, dst, in_sem.at[i])
        for i, (src, dst) in enumerate((
            (q_hbm, q_ref), (k_hbm, k_ref), (v_hbm, v_ref), (taps_hbm, taps_ref), (skip_hbm, skip_ref),
            (fwd_hbm, fwd_ref), (inv_hbm, inv_ref), (w_hbm, w_ref),
        ))
    ]
    for load in loads:
        load.start()
    lines = n_seq // GROUP
    z, x = s // GROUP, s % GROUP
    y, core = c // 2, c % 2
    sub = width // n_seq
    wide = GROUP * sub
    cols = w_ref.shape[1]
    px, pc, py = z * GROUP + (1 - x), y * 2 + (1 - core), (1 - y) * 2 + core

    def lanes(index, size):
        return pl.ds(pl.multiple_of(index * size, size), size)

    barrier = pltpu.get_barrier_semaphore()
    for d in range(1, n_seq):
        pl.semaphore_signal(barrier, inc=1, device_id={"seq": lax.rem(s + d, n_seq), "chan": c}, device_id_type=MESH_ID)
    for other in (pc, py):
        pl.semaphore_signal(barrier, inc=1, device_id={"seq": s, "chan": other}, device_id_type=MESH_ID)
    for other in range(n_chan):
        @pl.when(jnp.logical_or(z != c, other != c))
        def _():
            pl.semaphore_signal(barrier, inc=1, device_id={"seq": c * GROUP + x, "chan": other}, device_id_type=MESH_ID)
    own_filter = pltpu.make_async_copy(f_ref.at[:, lanes(s, sub)], filt.at[:, lanes(s + 1, sub)], in_sem.at[len(loads)])
    own_filter.start()
    filt[:, :sub] = jnp.zeros((block, sub), filt.dtype)
    for load in loads[:3]:
        load.wait()
    tail = block - 16
    row16 = lax.broadcasted_iota(jnp.int32, (16, width), 0)
    tails = [pltpu.roll(ref[tail:, :].astype(jnp.float32), 2 + 2 * i, 0) for i, ref in enumerate((q_ref, k_ref, v_ref))]
    rim_out[...] = jnp.where(row16 < 2, tails[0], jnp.where(row16 < 4, tails[1], tails[2])).astype(jnp.bfloat16)
    pl.semaphore_wait(barrier, n_seq - 1 + 2 + n_chan - (z == c).astype(jnp.int32))

    rim = remote(rim_out, rim_in, rim_sem.at[0], rim_sem.at[1], lax.rem(s + 1, n_seq), c)
    rim.start()

    def exchange(kind, d, src, dst):
        to = lax.rem(s + d, n_seq)
        return remote(src, dst.at[:, lanes(s + (1 if kind == 0 else 0), sub)], a_send.at[kind, d], a_recv.at[kind, d], to, c)

    order = list(range(1, n_seq))
    sends = []
    for d in order:
        to = lax.rem(s + d, n_seq)
        copy = exchange(0, d, f_ref.at[:, lanes(to, sub)], filt)
        copy.start()
        sends.append(copy)
    loads[3].wait()
    rim.wait()
    row = lax.broadcasted_iota(jnp.int32, (block, sub), 0)
    started = s > 0

    def filtered(ref, stream, here):
        x0 = ref[:, here].astype(jnp.float32)
        edge = jnp.where(started, rim_in[:, here].astype(jnp.float32), 0.0)
        r0, r1 = edge[2 * stream : 2 * stream + 1], edge[2 * stream + 1 : 2 * stream + 2]
        x1 = jnp.where(row == 0, r1, pltpu.roll(x0, 1, 0))
        x2 = jnp.where(row == 0, r0, jnp.where(row == 1, r1, pltpu.roll(x0, 2, 0)))
        t = taps_ref[stream, :, here]
        return t[0:1] * x0 + t[1:2] * x1 + t[2:3] * x2

    w_copies = []
    def send_all(kind, dst, value_of):
        for d in order + [0]:
            here = lanes(lax.rem(s + d, n_seq), sub)
            value = value_of(here).astype(jnp.bfloat16)
            if d == 0:
                dst[:, lanes(s, sub)] = value
            else:
                mine[kind - 1, :, here] = value
                copy = exchange(kind, d, mine.at[kind - 1, :, here], dst)
                copy.start()
                sends.append(copy)

    send_all(1, mix, lambda here: filtered(k_ref, 1, here) * filtered(v_ref, 2, here))
    send_all(2, gate, lambda here: filtered(q_ref, 0, here))
    depth = w_ref.shape[0] // w_sem.shape[1]

    def share_weights(first, last):
        for i in range(first, last):
            at = pl.ds(i * depth, depth)
            copy = remote(w_hbm.at[at, :], w_far.at[at, :], w_sem.at[0, i], w_sem.at[1, i], px, c)
            copy.start()
            w_copies.append(copy)

    share_weights(0, EARLY)
    own_filter.wait()
    loads[5].wait()
    peers = n_seq - 1
    for copy in sends[:peers]:
        copy.wait_recv()
    segments = jnp.concatenate([filt[:, : n_seq * sub], filt[:, sub:]], axis=0)
    spec_g[...] = jnp.dot(fwd_ref[...], segments, preferred_element_type=jnp.float32).astype(jnp.bfloat16).astype(jnp.float32)
    for copy in sends[peers : 2 * peers]:
        copy.wait_recv()
    spec_u[...] = jnp.dot(fwd_ref[:, :block], mix[...], preferred_element_type=jnp.float32)

    def strip(r, carry):
        at = pl.ds(pl.multiple_of(r * 8, 8), 8)
        under = pl.ds(pl.multiple_of(block + r * 8, 8), 8)
        first = lax.broadcasted_iota(jnp.int32, (8, sub), 0) + r * 8 == 0
        part_of = [slice(b * sub, (b + 1) * sub) for b in range(n_seq)]
        u_re = [spec_u[at, here] for here in part_of]
        u_im = [spec_u[under, here] for here in part_of]
        g_re = [spec_g[at, here] for here in part_of]
        g_im = [spec_g[under, here] for here in part_of]
        g_no = [jnp.where(first, 0.0, im) for im in g_im]
        g_on = [jnp.where(first, im, re) for re, im in zip(g_re, g_im)]
        for b in range(n_seq):
            total_re = g_re[0] * u_re[b] - g_no[0] * u_im[b]
            total_im = g_on[0] * u_im[b] + g_no[0] * u_re[b]
            for m in range(1, b + 1):
                total_re += g_re[m] * u_re[b - m] - g_no[m] * u_im[b - m]
                total_im += g_on[m] * u_im[b - m] + g_no[m] * u_re[b - m]
            acc[at, part_of[b]] = total_re
            acc[under, part_of[b]] = total_im
        return carry

    lax.fori_loop(0, block // 8, strip, 0)
    loads[4].wait()
    loads[6].wait()
    conv = jnp.dot(inv_ref[...], acc[...].astype(jnp.bfloat16), preferred_element_type=jnp.float32)
    acc[:block, :] = conv
    for copy in sends[2 * peers :]:
        copy.wait_recv()
    gain = skip_ref[:, lanes(s, sub)]
    x_copies, up_copies, dn_copies = [], {}, {}
    top = z == lines - 1
    bottom = z == 0

    def along(p, h, up):
        slot = jnp.clip(z - (h - 1), 0, lines - 1) if up else jnp.clip(z + (h - 1), 0, lines - 1)
        piece = rows.at[pl.ds(p * block, block), lanes(slot, wide)]
        to = jnp.minimum(z + 1, lines - 1) if up else jnp.maximum(z - 1, 0)
        send, recv = (up_send, up_recv) if up else (dn_send, dn_recv)
        return remote(piece, piece, send.at[p, h - 1], recv.at[p, h - 1], to * GROUP + x, c)

    early = range(NOW)
    late = range(NOW, lines)

    def start_half(p, owner):
        piece = rows.at[pl.ds(p * block, block), lanes(owner, sub)]
        for up, blocked, to in ((True, top, jnp.minimum(z + 1, lines - 1)), (False, bottom, jnp.maximum(z - 1, 0))):
            @pl.when(jnp.logical_not(blocked))
            def _():
                send, recv = (up_send, up_recv) if up else (dn_send, dn_recv)
                remote(piece, piece, send.at[p, 0], recv.at[p, 0], to * GROUP + x, c).start()

    for p in range(lines):
        for e in range(GROUP):
            here = slice(p * wide + e * sub, p * wide + (e + 1) * sub)
            value = gate[:, here].astype(jnp.float32) * (acc[:block, here] + gain * mix[:, here].astype(jnp.float32))
            gated[e] = value.astype(jnp.bfloat16)
        half_out[p] = gated[1 - x]
        rows[pl.ds(p * block, block), lanes(s, sub)] = gated[x]
        copy = remote(half_out.at[p], rows.at[pl.ds(p * block, block), lanes(s, sub)], x_send.at[p], x_recv.at[p], px, c)
        copy.start()
        x_copies.append(copy)
        if p in early:
            start_half(p, s)
    r1, r2 = {}, {}
    half, quarter = block // 2, block // 4
    loads[7].wait()

    def columns(e):
        return lanes(x if e == 0 else 1 - x, cols)

    def stage_one(u):
        e, p = u // lines, u % lines
        if e == 1 and p == 0:
            for copy in w_copies:
                copy.wait_recv()
        lhs = rows[pl.ds(p * block, block), :]
        part[u] = jnp.dot(lhs, (w_ref if e == 0 else w_far)[...], preferred_element_type=jnp.float32)
        away = pl.ds(pl.multiple_of((1 - core) * half, half), half)
        r1_out[u] = part[u, away, :].astype(jnp.bfloat16)
        r1[u] = remote(r1_out.at[u], r1_in.at[u], r1_sem.at[0, u], r1_sem.at[1, u], s, pc)
        r1[u].start()

    def stage_two(u):
        r1[u].wait_recv()
        away = pl.multiple_of((1 - y) * quarter, quarter)
        base = pl.multiple_of(core * half, half)
        r2_out[u] = (part[u, pl.ds(base + away, quarter), :] + r1_in[u, pl.ds(away, quarter), :].astype(jnp.float32)).astype(jnp.bfloat16)
        r2[u] = remote(r2_out.at[u], r2_in.at[u], r2_sem.at[0, u], r2_sem.at[1, u], s, py)
        r2[u].start()

    strip_at = pl.ds(pl.multiple_of((core * 2 + y) * quarter, quarter), quarter)

    def last_copy(u):
        e, p = u // lines, u % lines
        return remote(r3_out.at[u], out_ref.at[strip_at, columns(e)], o_send.at[u], o_recv.at[c, e], p * GROUP + x, z)

    def own_copy(u):
        return pltpu.make_async_copy(r3_out.at[u], out_ref.at[strip_at, columns(u // lines)], o_send.at[u])

    def stage_three(u):
        e, p = u // lines, u % lines
        r2[u].wait_recv()
        near = pl.multiple_of(y * quarter, quarter)
        base = pl.multiple_of(core * half, half)
        value = (
            part[u, pl.ds(base + near, quarter), :]
            + r1_in[u, pl.ds(near, quarter), :].astype(jnp.float32)
            + r2_in[u].astype(jnp.float32)
        ).astype(jnp.bfloat16)
        own = jnp.logical_and(z == c, z == p)
        r3_out[u] = value

        @pl.when(own)
        def _():
            own_copy(u).start()

        @pl.when(jnp.logical_not(own))
        def _():
            last_copy(u).start()

    def begin(batch):
        for p in batch:
            if p in late:
                start_half(p, s)
            x_copies[p].wait_recv()
            start_half(p, px)

    def relay(batch, h):
        for p in batch:
            for up, blocked, reach in ((True, top, z >= h), (False, bottom, z + h < lines)):
                @pl.when(reach)
                def _():
                    slot = z - h if up else z + h
                    piece = rows.at[pl.ds(p * block, block), lanes(slot, wide)]
                    recv = (up_recv if up else dn_recv).at[p, h - 1]
                    remote(piece, piece, (up_send if up else dn_send).at[p, h - 1], recv, s, c).wait_recv()

                if h < lines - 1:
                    @pl.when(jnp.logical_and(reach, jnp.logical_not(blocked)))
                    def _():
                        along(p, h + 1, up).start()


    def near_units(batch):
        return list(batch)

    def far_units(batch):
        return [lines + p for p in batch]

    def run(stage, batch):
        for u in batch:
            stage(u)

    def out_wait():
        for other in range(n_chan):
            strip_of = ((other % 2) * 2 + other // 2) * quarter

            @pl.when(jnp.logical_or(z != c, other != c))
            def _():
                for e in range(GROUP):
                    piece = out_ref.at[pl.ds(strip_of, quarter), columns(e)]
                    remote(r3_out.at[0], piece, o_send.at[0], o_recv.at[other, e], s, c).wait_recv()

    def send_wait(waited):
        for i, group in enumerate((sends, w_copies, x_copies, list(r1.values()), list(r2.values()))):
            if i not in waited:
                for copy in group:
                    copy.wait_send()
        for p in range(lines):
            for h in range(1, lines):
                for up, blocked, reach in ((True, top, z >= h - 1), (False, bottom, z + h - 1 < lines)):
                    @pl.when(jnp.logical_and(reach, jnp.logical_not(blocked)))
                    def _():
                        along(p, h, up).wait_send()

            own = jnp.logical_and(z == c, z == p)

            @pl.when(own)
            def _():
                for e in range(GROUP):
                    own_copy(e * lines + p).wait()

            @pl.when(jnp.logical_not(own))
            def _():
                for e in range(GROUP):
                    last_copy(e * lines + p).wait_send()

    waited = set()
    for act in SCHEDULE:
        kind, p = act[0], int(act[1])
        if kind == "b":
            begin([p])
        elif kind == "r":
            relay([p], int(act[2]))
        elif kind == "w":
            share_weights(p, int(act[2]))
        elif kind == "q":
            for copy in (sends, w_copies, x_copies, list(r1.values()), list(r2.values()))[p]:
                copy.wait_send()
            waited.add(p)
        else:
            stage = {"1": stage_one, "2": stage_two, "3": stage_three}[kind]
            stage(p if act[2] == "n" else lines + p)
    out_wait()
    send_wait(waited)

def fused(n_seq, n_chan, query_in, key_in, value_in, short_taps, long_filter, skip_gain, out_weight):
    block, width = query_in.shape
    sub = width // n_seq
    lines = n_seq // GROUP
    cols = out_weight.shape[1]
    count = 2 * block
    forward, inverse = packed_tables(block)
    bf16, f32 = jnp.bfloat16, jnp.float32
    dma = pltpu.SemaphoreType.DMA
    pieces = 8
    units = GROUP * lines
    return pl.pallas_call(
        functools.partial(kernel, n_seq, n_chan),
        out_shape=jax.ShapeDtypeStruct((block, GROUP * cols), bf16),
        in_specs=[pl.BlockSpec(memory_space=pl.ANY)] * 9,
        out_specs=pl.BlockSpec(memory_space=pl.ANY),
        scratch_shapes=[
            pltpu.VMEM((block, width), bf16),
            pltpu.VMEM((block, width), bf16),
            pltpu.VMEM((block, width), bf16),
            pltpu.VMEM(short_taps.shape, f32),
            pltpu.VMEM((1, width), f32),
            pltpu.VMEM((width, cols), bf16),
            pltpu.VMEM(forward.shape, bf16),
            pltpu.VMEM(inverse.shape, bf16),
            dma((9,)),
            pltpu.VMEM((2, block, width), bf16),
            pltpu.VMEM((16, width), bf16),
            pltpu.VMEM((16, width), bf16),
            pltpu.VMEM((block, n_seq * sub), bf16),
            pltpu.VMEM((block, (n_seq + 1) * sub), bf16),
            pltpu.VMEM((block, n_seq * sub), bf16),
            pltpu.VMEM((count, n_seq * sub), f32),
            pltpu.VMEM((count, n_seq * sub), f32),
            pltpu.VMEM((count, n_seq * sub), f32),
            pltpu.VMEM((GROUP, block, sub), bf16),
            pltpu.VMEM((lines, block, sub), bf16),
            pltpu.VMEM((lines * block, width), bf16),
            pltpu.VMEM((width, cols), bf16),
            pltpu.VMEM((units, block, cols), f32),
            pltpu.VMEM((units, block // 2, cols), bf16),
            pltpu.VMEM((units, block // 2, cols), bf16),
            pltpu.VMEM((units, block // 4, cols), bf16),
            pltpu.VMEM((units, block // 4, cols), bf16),
            pltpu.VMEM((units, block // 4, cols), bf16),
            dma((3, n_seq)),
            dma((3, n_seq)),
            dma((2,)),
            dma((2, pieces)),
            dma((lines,)),
            dma((lines,)),
            dma((lines, lines - 1)),
            dma((lines, lines - 1)),
            dma((lines, lines - 1)),
            dma((lines, lines - 1)),
            dma((2, units)),
            dma((2, units)),
            dma((units,)),
            dma((n_chan, GROUP)),
        ],
        compiler_params=pltpu.CompilerParams(collective_id=0, has_side_effects=True, vmem_limit_bytes=60 * 2**20),
    )(
        query_in, key_in, value_in, short_taps, long_filter, skip_gain.reshape(1, width), out_weight,
        forward, inverse,
    )


def solution(mesh):
    in_specs = (
        P("seq", "chan"),
        P("seq", "chan"),
        P("seq", "chan"),
        P(None, None, "chan"),
        P("seq", "chan"),
        P("chan"),
        P("chan", "seq"),
    )
    out_specs = P("seq", "chan")
    n_seq, n_chan = mesh.shape["seq"], mesh.shape["chan"]

    def device_part(*args):
        width, cols = args[0].shape[1], args[-1].shape[1]
        fits = n_chan == 4 and n_seq == GROUP * n_chan and width % (128 * n_seq) == 0 and cols % 128 == 0
        if fits and args[0].shape[0] % 128 == 0:
            return fused(n_seq, n_chan, *args)
        return body(*args)

    return jax.shard_map(device_part, mesh=mesh, in_specs=in_specs, out_specs=out_specs, check_vma=False)
```

```python
import functools
import math

import jax
import jax.numpy as jnp
import numpy as np
from jax import lax
from jax.experimental import pallas as pl
from jax.experimental.pallas import tpu as pltpu
from jax.sharding import PartitionSpec as P


def passed_along(value, axis, steps):
    count = lax.axis_size(axis)
    first, last = (max(0, -steps), min(count, count - steps))
    return lax.ppermute(value, axis, [(source, source + steps) for source in range(first, last)])


def broadcast(array, axis, root):
    mine = lax.axis_index(axis) == root
    return lax.psum(jnp.where(mine, array, jnp.zeros_like(array)), axis)


def dft_tables(length):
    count = 2 * length
    ramp = jnp.arange(count, dtype=jnp.int32)
    product = ramp[:, None] * ramp[None, :] % count
    angle = product.astype(jnp.float32) * (2.0 * math.pi / count)
    return (jnp.cos(angle), jnp.sin(angle))


def short_conv(rim, stream, taps):
    whole = jnp.concatenate([rim, stream], axis=0).astype(jnp.float32)
    return taps[0] * whole[2:] + taps[1] * whole[1:-1] + taps[2] * whole[:-2]


def spectrum(signal, cos_part, sin_part):
    real = jnp.einsum("nk,nc->kc", cos_part, signal, preferred_element_type=jnp.float32)
    imag = -jnp.einsum("nk,nc->kc", sin_part, signal, preferred_element_type=jnp.float32)
    return (real, imag)


def filter_spectrum(earlier, current, cos_part, sin_part):
    segment = jnp.concatenate([earlier, current], axis=0)
    real, imag = spectrum(segment, cos_part, sin_part)
    real16 = lax.optimization_barrier(real.astype(jnp.bfloat16))
    imag16 = lax.optimization_barrier(imag.astype(jnp.bfloat16))
    return (real16, imag16)


def invert(acc_re, acc_im, inv_cos, inv_sin):
    first = jnp.einsum("kt,...kc->...tc", inv_cos, acc_re, precision=lax.Precision.HIGHEST)
    return first - jnp.einsum("kt,...kc->...tc", inv_sin, acc_im, precision=lax.Precision.HIGHEST)


def body(query_in, key_in, value_in, short_taps, long_filter, skip_gain, out_weight):
    block = query_in.shape[0]
    width = query_in.shape[1]
    count = 2 * block
    rims = passed_along((query_in[-2:], key_in[-2:], value_in[-2:]), "seq", 1)
    gating = short_conv(rims[0], query_in, short_taps[0])
    keyed = short_conv(rims[1], key_in, short_taps[1])
    valued = short_conv(rims[2], value_in, short_taps[2])
    mixed = (keyed * valued).astype(jnp.bfloat16)
    cos_full, sin_full = dft_tables(block)
    fwd_cos = cos_full.astype(jnp.bfloat16)
    fwd_sin = sin_full.astype(jnp.bfloat16)
    inv_cos = cos_full[:, block:] / count
    inv_sin = sin_full[:, block:] / count
    empty = jnp.zeros((count, width), jnp.float32)

    def lag_spectrum(step_index, earlier):
        current = broadcast(long_filter, "seq", step_index)
        g_re, g_im = filter_spectrum(earlier, current, fwd_cos, fwd_sin)
        return (g_re, g_im, current)

    def one_round(step_index, carry):
        moving, earlier, acc_re, acc_im = carry
        g_re, g_im, earlier = lag_spectrum(step_index, earlier)
        g_re = g_re.astype(jnp.float32)
        g_im = g_im.astype(jnp.float32)
        u_re, u_im = spectrum(moving, fwd_cos[:block], fwd_sin[:block])
        acc_re = acc_re + g_re * u_re - g_im * u_im
        acc_im = acc_im + g_re * u_im + g_im * u_re
        moving = passed_along(moving, "seq", 1)
        return (moving, earlier, acc_re, acc_im)

    start_filter = jnp.zeros((block, width), jnp.bfloat16)
    final = lax.fori_loop(0, lax.axis_size("seq"), one_round, (mixed, start_filter, empty, empty))
    conv = invert(final[2], final[3], inv_cos, inv_sin)
    gated = (gating * (conv + skip_gain * mixed.astype(jnp.float32))).astype(jnp.bfloat16)
    partial_out = jnp.dot(
        gated,
        lax.all_gather(out_weight, "seq", axis=1, tiled=True),
        preferred_element_type=jnp.float32,
    )
    return lax.psum_scatter(
        partial_out.astype(jnp.bfloat16), "chan", scatter_dimension=1, tiled=True
    )


MESH_ID = pl.DeviceIdType.MESH
GROUP = 2
EARLY = 3
PIECES = 8
NOW = 4
SCHEDULE = ('b0', 'b1', 'w38', 'r01', 'b2', 'r11', 'r02', 'b3', 'r21', 'r12', 'r03', '10n', 'r31', 'r22', '20n', 'r13', '11n', 'r32', '30n', '21n', 'r23', '12n', '31n', '22n', '10f', '11f', '12f', 'r33', '13n', '13f', '32n', '20f', '21f', '22f', '23n', '23f', '30f', '31f', '32f', '33n', '33f')


def packed_tables(block):
    count = 2 * block
    ramp = np.arange(count)
    angle = (ramp[:, None] * ramp[None, :] % count) * (2.0 * math.pi / count)
    cosine, sine = np.cos(angle), np.sin(angle)
    forward = np.concatenate([cosine[:block], cosine[block : block + 1], -sine[1:block]], axis=0)
    weight = np.full((block, 1), 2.0)
    weight[0] = 1.0
    inverse = np.concatenate(
        [weight * cosine[:block, block:], cosine[block : block + 1, block:], -2.0 * sine[1:block, block:]], axis=0
    ) / count
    return jnp.asarray(forward, jnp.bfloat16), jnp.asarray(inverse.T, jnp.float32).astype(jnp.bfloat16)


def remote(src, dst, send, recv, seq, chan):
    return pltpu.make_async_remote_copy(
        src_ref=src, dst_ref=dst, send_sem=send, recv_sem=recv, device_id={"seq": seq, "chan": chan}, device_id_type=MESH_ID
    )


def kernel(
    n_seq, n_chan, q_hbm, k_hbm, v_hbm, taps_hbm, f_ref, skip_hbm, w_hbm, fwd_hbm, inv_hbm, out_ref,
    qkv_ref, taps_ref, skip_ref, w_ref, fwd_ref, inv_ref, in_sem,
    mine, rim_out, rim_in, mix, filt, gate, spec_u, spec_g, acc, gated, half_out, rows, w_far, part, r1_out, r1_in,
    r2_out, r2_in, r3_out,
    a_send, a_recv, rim_sem, w_sem, x_send, x_recv, z_send, up_recv, dn_recv, r_send, r1_recv, r2_recv, o_recv,
):
    s, c = lax.axis_index("seq"), lax.axis_index("chan")
    block, width = f_ref.shape
    for i, src in enumerate((q_hbm, k_hbm, v_hbm)):
        pltpu.make_async_copy(src, qkv_ref.at[i], in_sem.at[0]).start()
    loads = [
        pltpu.make_async_copy(src, dst, in_sem.at[1 + i])
        for i, (src, dst) in enumerate((
            (taps_hbm, taps_ref), (skip_hbm, skip_ref), (fwd_hbm, fwd_ref), (inv_hbm, inv_ref), (w_hbm, w_ref),
        ))
    ]
    for load in loads:
        load.start()
    lines = n_seq // GROUP
    z, x = s // GROUP, s % GROUP
    y, core = c // 2, c % 2
    sub = width // n_seq
    wide = GROUP * sub
    cols = w_ref.shape[1]
    px, pc, py = z * GROUP + (1 - x), y * 2 + (1 - core), (1 - y) * 2 + core

    def lanes(index, size):
        return pl.ds(pl.multiple_of(index * size, size), size)

    barrier = pltpu.get_barrier_semaphore()
    for d in range(1, n_seq):
        pl.semaphore_signal(barrier, inc=1, device_id={"seq": lax.rem(s + d, n_seq), "chan": c}, device_id_type=MESH_ID)
    for other in (pc, py):
        pl.semaphore_signal(barrier, inc=1, device_id={"seq": s, "chan": other}, device_id_type=MESH_ID)
    for other in range(n_chan):
        @pl.when(jnp.logical_or(z != c, other != c))
        def _():
            pl.semaphore_signal(barrier, inc=1, device_id={"seq": c * GROUP + x, "chan": other}, device_id_type=MESH_ID)
    own_filter = pltpu.make_async_copy(f_ref.at[:, lanes(s, sub)], filt.at[:, lanes(s + 1, sub)], in_sem.at[1 + len(loads)])
    own_filter.start()
    filt[:, :sub] = jnp.zeros((block, sub), filt.dtype)
    pltpu.make_async_copy(qkv_ref, qkv_ref, in_sem.at[0]).wait()
    tail = block - 16
    row16 = lax.broadcasted_iota(jnp.int32, (16, width), 0)
    tails = [pltpu.roll(ref[tail:, :].astype(jnp.float32), 2 + 2 * i, 0) for i, ref in enumerate(qkv_ref.at[j] for j in range(3))]
    rim_out[...] = jnp.where(row16 < 2, tails[0], jnp.where(row16 < 4, tails[1], tails[2])).astype(jnp.bfloat16)
    pl.semaphore_wait(barrier, n_seq - 1 + 2 + n_chan - (z == c).astype(jnp.int32))

    rim = remote(rim_out, rim_in, rim_sem.at[0], rim_sem.at[1], lax.rem(s + 1, n_seq), c)
    rim.start()

    def exchange(kind, d, src, dst):
        to = lax.rem(s + d, n_seq)
        return remote(src, dst.at[:, lanes(s + (1 if kind == 0 else 0), sub)], a_send.at[min(kind, 1)], a_recv.at[kind], to, c)

    order = list(range(1, n_seq))
    for d in order:
        to = lax.rem(s + d, n_seq)
        copy = exchange(0, d, f_ref.at[:, lanes(to, sub)], filt)
        copy.start()
    loads[0].wait()
    rim.wait()
    row = lax.broadcasted_iota(jnp.int32, (block, sub), 0)
    started = s > 0

    def filtered(stream, here):
        x0 = qkv_ref[stream, :, here].astype(jnp.float32)
        edge = jnp.where(started, rim_in[:, here].astype(jnp.float32), 0.0)
        r0, r1 = edge[2 * stream : 2 * stream + 1], edge[2 * stream + 1 : 2 * stream + 2]
        x1 = jnp.where(row == 0, r1, pltpu.roll(x0, 1, 0))
        x2 = jnp.where(row == 0, r0, jnp.where(row == 1, r1, pltpu.roll(x0, 2, 0)))
        t = taps_ref[stream, :, here]
        return t[0:1] * x0 + t[1:2] * x1 + t[2:3] * x2

    def send_all(kind, dst, value_of):
        for d in order + [0]:
            here = lanes(lax.rem(s + d, n_seq), sub)
            value = value_of(here).astype(jnp.bfloat16)
            if d == 0:
                dst[:, lanes(s, sub)] = value
            else:
                mine[kind - 1, :, here] = value
                copy = exchange(kind, d, mine.at[kind - 1, :, here], dst)
                copy.start()

    send_all(1, mix, lambda here: filtered(1, here) * filtered(2, here))
    send_all(2, gate, lambda here: filtered(0, here))
    depth = w_ref.shape[0] // PIECES

    def share_weights(first, last):
        for i in range(first, last):
            at = pl.ds(i * depth, depth)
            remote(w_hbm.at[at, :], w_far.at[at, :], w_sem.at[0], w_sem.at[1], px, c).start()

    share_weights(0, EARLY)
    own_filter.wait()
    loads[2].wait()
    peers = slice(0, (n_seq - 1) * sub)

    def arrival(kind):
        share = mine.at[0, :, peers]
        return remote(share, share, a_send.at[0], a_recv.at[kind], s, c)

    arrival(0).wait_recv()
    segments = jnp.concatenate([filt[:, : n_seq * sub], filt[:, sub:]], axis=0)
    spec_g[...] = jnp.dot(fwd_ref[...], segments, preferred_element_type=jnp.float32).astype(jnp.bfloat16).astype(jnp.float32)
    arrival(1).wait_recv()
    spec_u[...] = jnp.dot(fwd_ref[:, :block], mix[...], preferred_element_type=jnp.float32)

    def strip(r, carry):
        at = pl.ds(pl.multiple_of(r * 8, 8), 8)
        under = pl.ds(pl.multiple_of(block + r * 8, 8), 8)
        first = lax.broadcasted_iota(jnp.int32, (8, sub), 0) + r * 8 == 0
        part_of = [slice(b * sub, (b + 1) * sub) for b in range(n_seq)]
        u_re = [spec_u[at, here] for here in part_of]
        u_im = [spec_u[under, here] for here in part_of]
        g_re = [spec_g[at, here] for here in part_of]
        g_im = [spec_g[under, here] for here in part_of]
        g_no = [jnp.where(first, 0.0, im) for im in g_im]
        g_on = [jnp.where(first, im, re) for re, im in zip(g_re, g_im)]
        for b in range(n_seq):
            total_re = g_re[0] * u_re[b] - g_no[0] * u_im[b]
            total_im = g_on[0] * u_im[b] + g_no[0] * u_re[b]
            for m in range(1, b + 1):
                total_re += g_re[m] * u_re[b - m] - g_no[m] * u_im[b - m]
                total_im += g_on[m] * u_im[b - m] + g_no[m] * u_re[b - m]
            acc[at, part_of[b]] = total_re
            acc[under, part_of[b]] = total_im
        return carry

    lax.fori_loop(0, block // 8, strip, 0)
    loads[1].wait()
    loads[3].wait()
    conv = jnp.dot(inv_ref[...], acc[...].astype(jnp.bfloat16), preferred_element_type=jnp.float32)
    acc[:block, :] = conv
    arrival(2).wait_recv()
    gain = skip_ref[:, lanes(s, sub)]
    x_copies = []
    top = z == lines - 1
    bottom = z == 0

    def along(p, h, up):
        slot = jnp.clip(z - (h - 1), 0, lines - 1) if up else jnp.clip(z + (h - 1), 0, lines - 1)
        piece = rows.at[pl.ds(p * block, block), lanes(slot, wide)]
        to = jnp.minimum(z + 1, lines - 1) if up else jnp.maximum(z - 1, 0)
        send, recv = (z_send.at[0], up_recv) if up else (z_send.at[1], dn_recv)
        return remote(piece, piece, send, recv.at[p, h - 1], to * GROUP + x, c)

    early = range(NOW)
    late = range(NOW, lines)

    def start_half(p, owner):
        piece = rows.at[pl.ds(p * block, block), lanes(owner, sub)]
        for up, blocked, to in ((True, top, jnp.minimum(z + 1, lines - 1)), (False, bottom, jnp.maximum(z - 1, 0))):
            @pl.when(jnp.logical_not(blocked))
            def _():
                send, recv = (z_send.at[0], up_recv) if up else (z_send.at[1], dn_recv)
                remote(piece, piece, send, recv.at[p, 0], to * GROUP + x, c).start()

    for p in range(lines):
        for e in range(GROUP):
            here = slice(p * wide + e * sub, p * wide + (e + 1) * sub)
            value = gate[:, here].astype(jnp.float32) * (acc[:block, here] + gain * mix[:, here].astype(jnp.float32))
            gated[e] = value.astype(jnp.bfloat16)
        half_out[p] = gated[1 - x]
        rows[pl.ds(p * block, block), lanes(s, sub)] = gated[x]
        copy = remote(half_out.at[p], rows.at[pl.ds(p * block, block), lanes(s, sub)], x_send.at[0], x_recv.at[p], px, c)
        copy.start()
        x_copies.append(copy)
        if p in early:
            start_half(p, s)
    r1, r2, far_seen = {}, {}, []
    half, quarter = block // 2, block // 4
    loads[4].wait()

    def columns(e):
        return lanes(x if e == 0 else 1 - x, cols)

    def stage_one(u):
        e, p = u // lines, u % lines
        if e == 1 and not far_seen:
            far_seen.append(u)
            remote(w_hbm, w_far, w_sem.at[0], w_sem.at[1], px, c).wait_recv()
        lhs = rows[pl.ds(p * block, block), :]
        part[u] = jnp.dot(lhs, (w_ref if e == 0 else w_far)[...], preferred_element_type=jnp.float32)
        away = pl.ds(pl.multiple_of((1 - core) * half, half), half)
        r1_out[u] = part[u, away, :].astype(jnp.bfloat16)
        r1[u] = remote(r1_out.at[u], r1_in.at[u], r_send.at[0], r1_recv.at[u], s, pc)
        r1[u].start()

    def stage_two(u):
        r1[u].wait_recv()
        away = pl.multiple_of((1 - y) * quarter, quarter)
        base = pl.multiple_of(core * half, half)
        r2_out[u] = (part[u, pl.ds(base + away, quarter), :] + r1_in[u, pl.ds(away, quarter), :].astype(jnp.float32)).astype(jnp.bfloat16)
        r2[u] = remote(r2_out.at[u], r2_in.at[u], r_send.at[1], r2_recv.at[u], s, py)
        r2[u].start()

    strip_at = pl.ds(pl.multiple_of((core * 2 + y) * quarter, quarter), quarter)

    def last_copy(u):
        e, p = u // lines, u % lines
        return remote(r3_out.at[u], out_ref.at[strip_at, columns(e)], r_send.at[2], o_recv.at[0], p * GROUP + x, z)

    def own_copy(u):
        return pltpu.make_async_copy(r3_out.at[u], out_ref.at[strip_at, columns(u // lines)], r_send.at[2])

    def stage_three(u):
        e, p = u // lines, u % lines
        r2[u].wait_recv()
        near = pl.multiple_of(y * quarter, quarter)
        base = pl.multiple_of(core * half, half)
        value = (
            part[u, pl.ds(base + near, quarter), :]
            + r1_in[u, pl.ds(near, quarter), :].astype(jnp.float32)
            + r2_in[u].astype(jnp.float32)
        ).astype(jnp.bfloat16)
        own = jnp.logical_and(z == c, z == p)
        r3_out[u] = value

        @pl.when(own)
        def _():
            own_copy(u).start()

        @pl.when(jnp.logical_not(own))
        def _():
            last_copy(u).start()

    def begin(batch):
        for p in batch:
            if p in late:
                start_half(p, s)
            x_copies[p].wait_recv()
            start_half(p, px)

    def relay(batch, h):
        for p in batch:
            for up, blocked, reach in ((True, top, z >= h), (False, bottom, z + h < lines)):
                @pl.when(reach)
                def _():
                    slot = z - h if up else z + h
                    piece = rows.at[pl.ds(p * block, block), lanes(slot, wide)]
                    recv = (up_recv if up else dn_recv).at[p, h - 1]
                    remote(piece, piece, z_send.at[0], recv, s, c).wait_recv()

                if h < lines - 1:
                    @pl.when(jnp.logical_and(reach, jnp.logical_not(blocked)))
                    def _():
                        along(p, h + 1, up).start()


    def near_units(batch):
        return list(batch)

    def far_units(batch):
        return [lines + p for p in batch]

    def run(stage, batch):
        for u in batch:
            stage(u)

    def out_wait():
        for local, size in ((False, block), (True, block - quarter)):
            @pl.when((z == c) == local)
            def _():
                landed = out_ref.at[pl.ds(0, size), :]
                remote(landed, landed, r_send.at[2], o_recv.at[0], s, c).wait_recv()

    def send_wait():
        share = mine.at[0, :, peers]
        remote(share, share, a_send.at[0], a_recv.at[0], s, c).wait_send()
        share = mine.at[:, :, peers]
        remote(share, share, a_send.at[1], a_recv.at[0], s, c).wait_send()
        remote(w_hbm, w_far, w_sem.at[0], w_sem.at[1], px, c).wait_send()
        remote(half_out, half_out, x_send.at[0], x_recv.at[0], px, c).wait_send()
        for count in range(1, lines):
            gone = rows.at[:, pl.ds(0, count * wide)]
            for i, here in enumerate((z + 1 == count, lines - z == count)):
                @pl.when(here)
                def _():
                    remote(gone, gone, z_send.at[i], up_recv.at[0, 0], s, c).wait_send()
        for i, done in enumerate((r1_out, r2_out, r3_out)):
            remote(done, done, r_send.at[i], o_recv.at[0], s, c).wait_send()

    for act in SCHEDULE:
        kind, p = act[0], int(act[1])
        if kind == "b":
            begin([p])
        elif kind == "r":
            relay([p], int(act[2]))
        elif kind == "w":
            share_weights(p, int(act[2]))
        else:
            stage = {"1": stage_one, "2": stage_two, "3": stage_three}[kind]
            stage(p if act[2] == "n" else lines + p)
    out_wait()
    send_wait()


def fused(n_seq, n_chan, query_in, key_in, value_in, short_taps, long_filter, skip_gain, out_weight):
    block, width = query_in.shape
    sub = width // n_seq
    lines = n_seq // GROUP
    cols = out_weight.shape[1]
    count = 2 * block
    forward, inverse = packed_tables(block)
    bf16, f32 = jnp.bfloat16, jnp.float32
    dma = pltpu.SemaphoreType.DMA
    units = GROUP * lines
    return pl.pallas_call(
        functools.partial(kernel, n_seq, n_chan),
        out_shape=pltpu.VMEM((block, GROUP * cols), bf16),
        in_specs=[pl.BlockSpec(memory_space=pl.ANY)] * 9,
        out_specs=pl.BlockSpec(memory_space=pltpu.VMEM),
        scratch_shapes=[
            pltpu.VMEM((3, block, width), bf16),
            pltpu.VMEM(short_taps.shape, f32),
            pltpu.VMEM((1, width), f32),
            pltpu.VMEM((width, cols), bf16),
            pltpu.VMEM(forward.shape, bf16),
            pltpu.VMEM(inverse.shape, bf16),
            dma((7,)),
            pltpu.VMEM((2, block, width), bf16),
            pltpu.VMEM((16, width), bf16),
            pltpu.VMEM((16, width), bf16),
            pltpu.VMEM((block, n_seq * sub), bf16),
            pltpu.VMEM((block, (n_seq + 1) * sub), bf16),
            pltpu.VMEM((block, n_seq * sub), bf16),
            pltpu.VMEM((count, n_seq * sub), f32),
            pltpu.VMEM((count, n_seq * sub), f32),
            pltpu.VMEM((count, n_seq * sub), f32),
            pltpu.VMEM((GROUP, block, sub), bf16),
            pltpu.VMEM((lines, block, sub), bf16),
            pltpu.VMEM((lines * block, width), bf16),
            pltpu.VMEM((width, cols), bf16),
            pltpu.VMEM((units, block, cols), f32),
            pltpu.VMEM((units, block // 2, cols), bf16),
            pltpu.VMEM((units, block // 2, cols), bf16),
            pltpu.VMEM((units, block // 4, cols), bf16),
            pltpu.VMEM((units, block // 4, cols), bf16),
            pltpu.VMEM((units, block // 4, cols), bf16),
            dma((2,)),
            dma((3,)),
            dma((2,)),
            dma((2,)),
            dma((1,)),
            dma((lines,)),
            dma((2,)),
            dma((lines, lines - 1)),
            dma((lines, lines - 1)),
            dma((3,)),
            dma((units,)),
            dma((units,)),
            dma((1,)),
        ],
        compiler_params=pltpu.CompilerParams(collective_id=0, has_side_effects=True, vmem_limit_bytes=60 * 2**20),
    )(
        query_in, key_in, value_in, short_taps, long_filter, skip_gain.reshape(1, width), out_weight,
        forward, inverse,
    )


def solution(mesh):
    in_specs = (
        P("seq", "chan"),
        P("seq", "chan"),
        P("seq", "chan"),
        P(None, None, "chan"),
        P("seq", "chan"),
        P("chan"),
        P("chan", "seq"),
    )
    out_specs = P("seq", "chan")
    n_seq, n_chan = mesh.shape["seq"], mesh.shape["chan"]

    def device_part(*args):
        width, cols = args[0].shape[1], args[-1].shape[1]
        fits = n_chan == 4 and n_seq == GROUP * n_chan and width % (128 * n_seq) == 0 and cols % 128 == 0
        if fits and args[0].shape[0] % 128 == 0:
            return fused(n_seq, n_chan, *args)
        return body(*args)

    return jax.shard_map(device_part, mesh=mesh, in_specs=in_specs, out_specs=out_specs, check_vma=False)
```

```python
import functools
import math

import jax
import jax.numpy as jnp
import numpy as np
from jax import lax
from jax.experimental import pallas as pl
from jax.experimental.pallas import tpu as pltpu
from jax.sharding import PartitionSpec as P


def passed_along(value, axis, steps):
    count = lax.axis_size(axis)
    first, last = (max(0, -steps), min(count, count - steps))
    return lax.ppermute(value, axis, [(source, source + steps) for source in range(first, last)])


def broadcast(array, axis, root):
    mine = lax.axis_index(axis) == root
    return lax.psum(jnp.where(mine, array, jnp.zeros_like(array)), axis)


def dft_tables(length):
    count = 2 * length
    ramp = jnp.arange(count, dtype=jnp.int32)
    product = ramp[:, None] * ramp[None, :] % count
    angle = product.astype(jnp.float32) * (2.0 * math.pi / count)
    return (jnp.cos(angle), jnp.sin(angle))


def short_conv(rim, stream, taps):
    whole = jnp.concatenate([rim, stream], axis=0).astype(jnp.float32)
    return taps[0] * whole[2:] + taps[1] * whole[1:-1] + taps[2] * whole[:-2]


def spectrum(signal, cos_part, sin_part):
    real = jnp.einsum("nk,nc->kc", cos_part, signal, preferred_element_type=jnp.float32)
    imag = -jnp.einsum("nk,nc->kc", sin_part, signal, preferred_element_type=jnp.float32)
    return (real, imag)


def filter_spectrum(earlier, current, cos_part, sin_part):
    segment = jnp.concatenate([earlier, current], axis=0)
    real, imag = spectrum(segment, cos_part, sin_part)
    real16 = lax.optimization_barrier(real.astype(jnp.bfloat16))
    imag16 = lax.optimization_barrier(imag.astype(jnp.bfloat16))
    return (real16, imag16)


def invert(acc_re, acc_im, inv_cos, inv_sin):
    first = jnp.einsum("kt,...kc->...tc", inv_cos, acc_re, precision=lax.Precision.HIGHEST)
    return first - jnp.einsum("kt,...kc->...tc", inv_sin, acc_im, precision=lax.Precision.HIGHEST)


def body(query_in, key_in, value_in, short_taps, long_filter, skip_gain, out_weight):
    block = query_in.shape[0]
    width = query_in.shape[1]
    count = 2 * block
    rims = passed_along((query_in[-2:], key_in[-2:], value_in[-2:]), "seq", 1)
    gating = short_conv(rims[0], query_in, short_taps[0])
    keyed = short_conv(rims[1], key_in, short_taps[1])
    valued = short_conv(rims[2], value_in, short_taps[2])
    mixed = (keyed * valued).astype(jnp.bfloat16)
    cos_full, sin_full = dft_tables(block)
    fwd_cos = cos_full.astype(jnp.bfloat16)
    fwd_sin = sin_full.astype(jnp.bfloat16)
    inv_cos = cos_full[:, block:] / count
    inv_sin = sin_full[:, block:] / count
    empty = jnp.zeros((count, width), jnp.float32)

    def lag_spectrum(step_index, earlier):
        current = broadcast(long_filter, "seq", step_index)
        g_re, g_im = filter_spectrum(earlier, current, fwd_cos, fwd_sin)
        return (g_re, g_im, current)

    def one_round(step_index, carry):
        moving, earlier, acc_re, acc_im = carry
        g_re, g_im, earlier = lag_spectrum(step_index, earlier)
        g_re = g_re.astype(jnp.float32)
        g_im = g_im.astype(jnp.float32)
        u_re, u_im = spectrum(moving, fwd_cos[:block], fwd_sin[:block])
        acc_re = acc_re + g_re * u_re - g_im * u_im
        acc_im = acc_im + g_re * u_im + g_im * u_re
        moving = passed_along(moving, "seq", 1)
        return (moving, earlier, acc_re, acc_im)

    start_filter = jnp.zeros((block, width), jnp.bfloat16)
    final = lax.fori_loop(0, lax.axis_size("seq"), one_round, (mixed, start_filter, empty, empty))
    conv = invert(final[2], final[3], inv_cos, inv_sin)
    gated = (gating * (conv + skip_gain * mixed.astype(jnp.float32))).astype(jnp.bfloat16)
    partial_out = jnp.dot(
        gated,
        lax.all_gather(out_weight, "seq", axis=1, tiled=True),
        preferred_element_type=jnp.float32,
    )
    return lax.psum_scatter(
        partial_out.astype(jnp.bfloat16), "chan", scatter_dimension=1, tiled=True
    )


MESH_ID = pl.DeviceIdType.MESH
GROUP = 2
AHEAD = 3
EARLY = 3
MIDDLE = 3
PIECES = (4, 4)
SPLIT = 2
NOW = 4
SCHEDULE = (
    "b0", "b1", "w38", "r01", "b2", "r11", "r02", "b3", "r21", "r12", "r03", "10n", "10f", "r31", "r22", "20n",
    "20f", "r13", "11n", "11f", "r32", "21n", "21f", "r23", "12n", "12f", "30n", "30f", "22n", "22f", "r33",
    "13n", "13h", "10g", "31n", "31f", "11g", "12g", "23n", "23h", "20g", "21g", "22g", "32n", "32f", "33n",
    "33h", "30g", "31g", "32g",
)


def packed_tables(block):
    count = 2 * block
    ramp = np.arange(count)
    angle = (ramp[:, None] * ramp[None, :] % count) * (2.0 * math.pi / count)
    cosine, sine = np.cos(angle), np.sin(angle)
    forward = np.concatenate([cosine[:block], cosine[block : block + 1], -sine[1:block]], axis=0)
    weight = np.full((block, 1), 2.0)
    weight[0] = 1.0
    inverse = np.concatenate(
        [weight * cosine[:block, block:], cosine[block : block + 1, block:], -2.0 * sine[1:block, block:]], axis=0
    ) / count
    return jnp.asarray(forward, jnp.bfloat16), jnp.asarray(inverse.T, jnp.float32).astype(jnp.bfloat16)


def remote(src, dst, send, recv, seq, chan):
    return pltpu.make_async_remote_copy(
        src_ref=src, dst_ref=dst, send_sem=send, recv_sem=recv, device_id={"seq": seq, "chan": chan}, device_id_type=MESH_ID
    )


def kernel(
    n_seq, n_chan, q_hbm, k_hbm, v_hbm, taps_hbm, f_ref, skip_hbm, w_hbm, fwd_hbm, inv_hbm, out_ref,
    qkv_ref, taps_ref, skip_ref, w_ref, fwd_ref, inv_ref, in_sem,
    mine, rim_out, rim_in, mix, filt, gate, spec_u, spec_g, acc, gated, half_out, rows, w_far, part, r1_out, r1_in,
    r2_out, r2_in, r3_out,
    a_send, a_recv, rim_sem, w_sem, x_send, x_recv, z_send, up_recv, dn_recv, r_send, r1_recv, r2_recv, o_recv,
):
    s, c = lax.axis_index("seq"), lax.axis_index("chan")
    block, width = f_ref.shape
    for i, src in enumerate((q_hbm, k_hbm, v_hbm)):
        pltpu.make_async_copy(src, qkv_ref.at[i], in_sem.at[0]).start()
    loads = [
        pltpu.make_async_copy(src, dst, in_sem.at[1 + i])
        for i, (src, dst) in enumerate((
            (taps_hbm, taps_ref), (skip_hbm, skip_ref), (fwd_hbm, fwd_ref), (inv_hbm, inv_ref), (w_hbm, w_ref),
        ))
    ]
    for load in loads:
        load.start()
    lines = n_seq // GROUP
    z, x = s // GROUP, s % GROUP
    y, core = c // 2, c % 2
    sub = width // n_seq
    wide = GROUP * sub
    cols = w_ref.shape[1]
    px, pc, py = z * GROUP + (1 - x), y * 2 + (1 - core), (1 - y) * 2 + core

    def lanes(index, size):
        return pl.ds(pl.multiple_of(index * size, size), size)

    barrier = pltpu.get_barrier_semaphore()
    for d in range(1, n_seq):
        pl.semaphore_signal(barrier, inc=1, device_id={"seq": lax.rem(s + d, n_seq), "chan": c}, device_id_type=MESH_ID)
    for other in (pc, py):
        pl.semaphore_signal(barrier, inc=1, device_id={"seq": s, "chan": other}, device_id_type=MESH_ID)
    for other in range(n_chan):
        @pl.when(jnp.logical_or(z != c, other != c))
        def _():
            pl.semaphore_signal(barrier, inc=1, device_id={"seq": c * GROUP + x, "chan": other}, device_id_type=MESH_ID)
    own_filter = pltpu.make_async_copy(f_ref.at[:, lanes(s, sub)], filt.at[:, lanes(s + 1, sub)], in_sem.at[1 + len(loads)])
    own_filter.start()
    filt[:, :sub] = jnp.zeros((block, sub), filt.dtype)
    pl.semaphore_wait(barrier, n_seq - 1 + 2 + n_chan - (z == c).astype(jnp.int32))

    def exchange(kind, d, src, dst):
        to = lax.rem(s + d, n_seq)
        return remote(src, dst.at[:, lanes(s + (1 if kind == 0 else 0), sub)], a_send.at[min(kind, 1)], a_recv.at[kind], to, c)

    order = list(range(1, n_seq))

    def send_filter(chosen):
        for d in chosen:
            exchange(0, d, f_ref.at[:, lanes(lax.rem(s + d, n_seq), sub)], filt).start()

    send_filter(order[:AHEAD])
    pltpu.make_async_copy(qkv_ref, qkv_ref, in_sem.at[0]).wait()
    tail = block - 16
    row16 = lax.broadcasted_iota(jnp.int32, (16, width), 0)
    tails = [pltpu.roll(ref[tail:, :].astype(jnp.float32), 2 + 2 * i, 0) for i, ref in enumerate(qkv_ref.at[j] for j in range(3))]
    rim_out[...] = jnp.where(row16 < 2, tails[0], jnp.where(row16 < 4, tails[1], tails[2])).astype(jnp.bfloat16)
    rim = remote(rim_out, rim_in, rim_sem.at[0], rim_sem.at[1], lax.rem(s + 1, n_seq), c)
    rim.start()
    send_filter(order[AHEAD:])
    loads[0].wait()
    rim.wait()
    row = lax.broadcasted_iota(jnp.int32, (block, sub), 0)
    started = s > 0

    def filtered(stream, here):
        x0 = qkv_ref[stream, :, here].astype(jnp.float32)
        edge = jnp.where(started, rim_in[:, here].astype(jnp.float32), 0.0)
        r0, r1 = edge[2 * stream : 2 * stream + 1], edge[2 * stream + 1 : 2 * stream + 2]
        x1 = jnp.where(row == 0, r1, pltpu.roll(x0, 1, 0))
        x2 = jnp.where(row == 0, r0, jnp.where(row == 1, r1, pltpu.roll(x0, 2, 0)))
        t = taps_ref[stream, :, here]
        return t[0:1] * x0 + t[1:2] * x1 + t[2:3] * x2

    def send_all(kind, dst, value_of):
        for d in order + [0]:
            here = lanes(lax.rem(s + d, n_seq), sub)
            value = value_of(here).astype(jnp.bfloat16)
            if d == 0:
                dst[:, lanes(s, sub)] = value
            else:
                mine[kind - 1, :, here] = value
                copy = exchange(kind, d, mine.at[kind - 1, :, here], dst)
                copy.start()

    send_all(1, mix, lambda here: filtered(1, here) * filtered(2, here))
    send_all(2, gate, lambda here: filtered(0, here))
    split = cols * SPLIT // 4
    spans = (pl.ds(0, cols), pl.ds(0, split), pl.ds(split, cols - split), pl.ds(0, cols))
    chunks = [(e, r) for e, count in zip((1, 2), PIECES) for r in range(count)]

    def share_weights(first, last):
        for i in range(first, last):
            e, r = chunks[i]
            depth = width // PIECES[e - 1]
            at = (pl.ds(r * depth, depth), spans[e])
            remote(w_hbm.at[at], w_far.at[at], w_sem.at[0], w_sem.at[e], px, c).start()

    share_weights(0, EARLY)
    own_filter.wait()
    loads[2].wait()
    peers = slice(0, (n_seq - 1) * sub)

    def arrival(kind):
        share = mine.at[0, :, peers]
        return remote(share, share, a_send.at[0], a_recv.at[kind], s, c)

    arrival(0).wait_recv()
    segments = jnp.concatenate([filt[:, : n_seq * sub], filt[:, sub:]], axis=0)
    spec_g[...] = jnp.dot(fwd_ref[...], segments, preferred_element_type=jnp.float32).astype(jnp.bfloat16).astype(jnp.float32)
    arrival(1).wait_recv()
    share_weights(EARLY, MIDDLE)
    spec_u[...] = jnp.dot(fwd_ref[:, :block], mix[...], preferred_element_type=jnp.float32)

    def strip(r, carry):
        at = pl.ds(pl.multiple_of(r * 8, 8), 8)
        under = pl.ds(pl.multiple_of(block + r * 8, 8), 8)
        first = lax.broadcasted_iota(jnp.int32, (8, sub), 0) + r * 8 == 0
        part_of = [slice(b * sub, (b + 1) * sub) for b in range(n_seq)]
        u_re = [spec_u[at, here] for here in part_of]
        u_im = [spec_u[under, here] for here in part_of]
        g_re = [spec_g[at, here] for here in part_of]
        g_im = [spec_g[under, here] for here in part_of]
        g_no = [jnp.where(first, 0.0, im) for im in g_im]
        g_on = [jnp.where(first, im, re) for re, im in zip(g_re, g_im)]
        for b in range(n_seq):
            total_re = g_re[0] * u_re[b] - g_no[0] * u_im[b]
            total_im = g_on[0] * u_im[b] + g_no[0] * u_re[b]
            for m in range(1, b + 1):
                total_re += g_re[m] * u_re[b - m] - g_no[m] * u_im[b - m]
                total_im += g_on[m] * u_im[b - m] + g_no[m] * u_re[b - m]
            acc[at, part_of[b]] = total_re
            acc[under, part_of[b]] = total_im
        return carry

    lax.fori_loop(0, block // 8, strip, 0)
    loads[1].wait()
    loads[3].wait()
    conv = jnp.dot(inv_ref[...], acc[...].astype(jnp.bfloat16), preferred_element_type=jnp.float32)
    acc[:block, :] = conv
    arrival(2).wait_recv()
    gain = skip_ref[:, lanes(s, sub)]
    x_copies = []
    top = z == lines - 1
    bottom = z == 0

    def along(p, h, up):
        slot = jnp.clip(z - (h - 1), 0, lines - 1) if up else jnp.clip(z + (h - 1), 0, lines - 1)
        piece = rows.at[pl.ds(p * block, block), lanes(slot, wide)]
        to = jnp.minimum(z + 1, lines - 1) if up else jnp.maximum(z - 1, 0)
        send, recv = (z_send.at[0], up_recv) if up else (z_send.at[1], dn_recv)
        return remote(piece, piece, send, recv.at[p, h - 1], to * GROUP + x, c)

    early = range(NOW)
    late = range(NOW, lines)

    def start_half(p, owner):
        piece = rows.at[pl.ds(p * block, block), lanes(owner, sub)]
        for up, blocked, to in ((True, top, jnp.minimum(z + 1, lines - 1)), (False, bottom, jnp.maximum(z - 1, 0))):
            @pl.when(jnp.logical_not(blocked))
            def _():
                send, recv = (z_send.at[0], up_recv) if up else (z_send.at[1], dn_recv)
                remote(piece, piece, send, recv.at[p, 0], to * GROUP + x, c).start()

    for p in range(lines):
        for e in range(GROUP):
            here = slice(p * wide + e * sub, p * wide + (e + 1) * sub)
            value = gate[:, here].astype(jnp.float32) * (acc[:block, here] + gain * mix[:, here].astype(jnp.float32))
            gated[e] = value.astype(jnp.bfloat16)
        half_out[p] = gated[1 - x]
        rows[pl.ds(p * block, block), lanes(s, sub)] = gated[x]
        copy = remote(half_out.at[p], rows.at[pl.ds(p * block, block), lanes(s, sub)], x_send.at[0], x_recv.at[p], px, c)
        copy.start()
        x_copies.append(copy)
        if p in early:
            start_half(p, s)
    r1, r2, far_seen = {}, {}, []
    half, quarter = block // 2, block // 4
    loads[4].wait()

    def columns(e):
        first = split if e == 2 else 0
        return pl.ds(pl.multiple_of((x if e == 0 else 1 - x) * cols + first, 128), spans[e].size)

    def held(ref, p, e, where=slice(None)):
        return ref.at[p + min(e, 1) * lines, where, spans[e]]

    def place(p, e):
        return min(e, 2) * lines + p

    def stage_one(p, e):
        for i in ((), (1,), (2,), (1, 2))[e]:
            if i not in far_seen:
                far_seen.append(i)
                whole = w_far.at[:, spans[i]]
                remote(whole, whole, w_sem.at[0], w_sem.at[i], px, c).wait_recv()
        lhs = rows[pl.ds(p * block, block), :]
        weight = w_ref[...] if e == 0 else w_far[:, spans[e]]
        held(part, p, e)[...] = jnp.dot(lhs, weight, preferred_element_type=jnp.float32)
        away = pl.ds(pl.multiple_of((1 - core) * half, half), half)
        held(r1_out, p, e)[...] = held(part, p, e, away)[...].astype(jnp.bfloat16)
        r1[p, e] = remote(held(r1_out, p, e), held(r1_in, p, e), r_send.at[0], r1_recv.at[place(p, e)], s, pc)
        r1[p, e].start()

    def stage_two(p, e):
        r1[p, e].wait_recv()
        away = pl.multiple_of((1 - y) * quarter, quarter)
        base = pl.multiple_of(core * half, half)
        held(r2_out, p, e)[...] = (
            held(part, p, e, pl.ds(base + away, quarter))[...]
            + held(r1_in, p, e, pl.ds(away, quarter))[...].astype(jnp.float32)
        ).astype(jnp.bfloat16)
        r2[p, e] = remote(held(r2_out, p, e), held(r2_in, p, e), r_send.at[1], r2_recv.at[place(p, e)], s, py)
        r2[p, e].start()

    strip_at = pl.ds(pl.multiple_of((core * 2 + y) * quarter, quarter), quarter)

    def last_copy(p, e):
        return remote(held(r3_out, p, e), out_ref.at[strip_at, columns(e)], r_send.at[2], o_recv.at[0], p * GROUP + x, z)

    def stage_three(p, e):
        r2[p, e].wait_recv()
        near = pl.multiple_of(y * quarter, quarter)
        base = pl.multiple_of(core * half, half)
        held(r3_out, p, e)[...] = (
            held(part, p, e, pl.ds(base + near, quarter))[...]
            + held(r1_in, p, e, pl.ds(near, quarter))[...].astype(jnp.float32)
            + held(r2_in, p, e)[...].astype(jnp.float32)
        ).astype(jnp.bfloat16)
        own = jnp.logical_and(z == c, z == p)

        @pl.when(own)
        def _():
            pltpu.make_async_copy(held(r3_out, p, e), out_ref.at[strip_at, columns(e)], r_send.at[2]).start()

        @pl.when(jnp.logical_not(own))
        def _():
            last_copy(p, e).start()

    def begin(batch):
        for p in batch:
            if p in late:
                start_half(p, s)
            x_copies[p].wait_recv()
            start_half(p, px)

    def relay(batch, h):
        for p in batch:
            for up, blocked, reach in ((True, top, z >= h), (False, bottom, z + h < lines)):
                @pl.when(reach)
                def _():
                    slot = z - h if up else z + h
                    piece = rows.at[pl.ds(p * block, block), lanes(slot, wide)]
                    recv = (up_recv if up else dn_recv).at[p, h - 1]
                    remote(piece, piece, z_send.at[0], recv, s, c).wait_recv()

                if h < lines - 1:
                    @pl.when(jnp.logical_and(reach, jnp.logical_not(blocked)))
                    def _():
                        along(p, h + 1, up).start()


    def out_wait():
        for local, size in ((False, block), (True, block - quarter)):
            @pl.when((z == c) == local)
            def _():
                landed = out_ref.at[pl.ds(0, size), :]
                remote(landed, landed, r_send.at[2], o_recv.at[0], s, c).wait_recv()

    def send_wait():
        share = mine.at[0, :, peers]
        remote(share, share, a_send.at[0], a_recv.at[0], s, c).wait_send()
        share = mine.at[:, :, peers]
        remote(share, share, a_send.at[1], a_recv.at[0], s, c).wait_send()
        remote(w_hbm, w_far, w_sem.at[0], w_sem.at[1], px, c).wait_send()
        remote(half_out, half_out, x_send.at[0], x_recv.at[0], px, c).wait_send()
        for count in range(1, lines):
            gone = rows.at[:, pl.ds(0, count * wide)]
            for i, here in enumerate((z + 1 == count, lines - z == count)):
                @pl.when(here)
                def _():
                    remote(gone, gone, z_send.at[i], up_recv.at[0, 0], s, c).wait_send()
        for i, done in enumerate((r1_out, r2_out, r3_out)):
            remote(done, done, r_send.at[i], o_recv.at[0], s, c).wait_send()

    for act in SCHEDULE:
        kind, p = act[0], int(act[1])
        if kind == "b":
            begin([p])
        elif kind == "r":
            relay([p], int(act[2]))
        elif kind == "w":
            share_weights(p, int(act[2], 16))
        else:
            stage = {"1": stage_one, "2": stage_two, "3": stage_three}[kind]
            stage(p, "nfgh".index(act[2]))
    out_wait()
    send_wait()


def fused(n_seq, n_chan, query_in, key_in, value_in, short_taps, long_filter, skip_gain, out_weight):
    block, width = query_in.shape
    sub = width // n_seq
    lines = n_seq // GROUP
    cols = out_weight.shape[1]
    count = 2 * block
    forward, inverse = packed_tables(block)
    bf16, f32 = jnp.bfloat16, jnp.float32
    dma = pltpu.SemaphoreType.DMA
    units = GROUP * lines
    return pl.pallas_call(
        functools.partial(kernel, n_seq, n_chan),
        out_shape=pltpu.VMEM((block, GROUP * cols), bf16),
        in_specs=[pl.BlockSpec(memory_space=pl.ANY)] * 9,
        out_specs=pl.BlockSpec(memory_space=pltpu.VMEM),
        scratch_shapes=[
            pltpu.VMEM((3, block, width), bf16),
            pltpu.VMEM(short_taps.shape, f32),
            pltpu.VMEM((1, width), f32),
            pltpu.VMEM((width, cols), bf16),
            pltpu.VMEM(forward.shape, bf16),
            pltpu.VMEM(inverse.shape, bf16),
            dma((7,)),
            pltpu.VMEM((2, block, width), bf16),
            pltpu.VMEM((16, width), bf16),
            pltpu.VMEM((16, width), bf16),
            pltpu.VMEM((block, n_seq * sub), bf16),
            pltpu.VMEM((block, (n_seq + 1) * sub), bf16),
            pltpu.VMEM((block, n_seq * sub), bf16),
            pltpu.VMEM((count, n_seq * sub), f32),
            pltpu.VMEM((count, n_seq * sub), f32),
            pltpu.VMEM((count, n_seq * sub), f32),
            pltpu.VMEM((GROUP, block, sub), bf16),
            pltpu.VMEM((lines, block, sub), bf16),
            pltpu.VMEM((lines * block, width), bf16),
            pltpu.VMEM((width, cols), bf16),
            pltpu.VMEM((units, block, cols), f32),
            pltpu.VMEM((units, block // 2, cols), bf16),
            pltpu.VMEM((units, block // 2, cols), bf16),
            pltpu.VMEM((units, block // 4, cols), bf16),
            pltpu.VMEM((units, block // 4, cols), bf16),
            pltpu.VMEM((units, block // 4, cols), bf16),
            dma((2,)),
            dma((3,)),
            dma((2,)),
            dma((3,)),
            dma((1,)),
            dma((lines,)),
            dma((2,)),
            dma((lines, lines - 1)),
            dma((lines, lines - 1)),
            dma((3,)),
            dma((3 * lines,)),
            dma((3 * lines,)),
            dma((1,)),
        ],
        compiler_params=pltpu.CompilerParams(collective_id=0, has_side_effects=True, vmem_limit_bytes=60 * 2**20),
    )(
        query_in, key_in, value_in, short_taps, long_filter, skip_gain.reshape(1, width), out_weight,
        forward, inverse,
    )


def solution(mesh):
    in_specs = (
        P("seq", "chan"),
        P("seq", "chan"),
        P("seq", "chan"),
        P(None, None, "chan"),
        P("seq", "chan"),
        P("chan"),
        P("chan", "seq"),
    )
    out_specs = P("seq", "chan")
    n_seq, n_chan = mesh.shape["seq"], mesh.shape["chan"]

    def device_part(*args):
        width, cols = args[0].shape[1], args[-1].shape[1]
        fits = n_chan == 4 and n_seq == GROUP * n_chan and width % (128 * n_seq) == 0 and cols % 128 == 0
        if fits and args[0].shape[0] % 128 == 0:
            return fused(n_seq, n_chan, *args)
        return body(*args)

    return jax.shard_map(device_part, mesh=mesh, in_specs=in_specs, out_specs=out_specs, check_vma=False)
```

```python
import functools
import math

import jax
import jax.numpy as jnp
import numpy as np
from jax import lax
from jax.experimental import pallas as pl
from jax.experimental.pallas import tpu as pltpu
from jax.sharding import PartitionSpec as P


def passed_along(value, axis, steps):
    count = lax.axis_size(axis)
    first, last = (max(0, -steps), min(count, count - steps))
    return lax.ppermute(value, axis, [(source, source + steps) for source in range(first, last)])


def broadcast(array, axis, root):
    mine = lax.axis_index(axis) == root
    return lax.psum(jnp.where(mine, array, jnp.zeros_like(array)), axis)


def dft_tables(length):
    count = 2 * length
    ramp = jnp.arange(count, dtype=jnp.int32)
    product = ramp[:, None] * ramp[None, :] % count
    angle = product.astype(jnp.float32) * (2.0 * math.pi / count)
    return (jnp.cos(angle), jnp.sin(angle))


def short_conv(rim, stream, taps):
    whole = jnp.concatenate([rim, stream], axis=0).astype(jnp.float32)
    return taps[0] * whole[2:] + taps[1] * whole[1:-1] + taps[2] * whole[:-2]


def spectrum(signal, cos_part, sin_part):
    real = jnp.einsum("nk,nc->kc", cos_part, signal, preferred_element_type=jnp.float32)
    imag = -jnp.einsum("nk,nc->kc", sin_part, signal, preferred_element_type=jnp.float32)
    return (real, imag)


def filter_spectrum(earlier, current, cos_part, sin_part):
    segment = jnp.concatenate([earlier, current], axis=0)
    real, imag = spectrum(segment, cos_part, sin_part)
    real16 = lax.optimization_barrier(real.astype(jnp.bfloat16))
    imag16 = lax.optimization_barrier(imag.astype(jnp.bfloat16))
    return (real16, imag16)


def invert(acc_re, acc_im, inv_cos, inv_sin):
    first = jnp.einsum("kt,...kc->...tc", inv_cos, acc_re, precision=lax.Precision.HIGHEST)
    return first - jnp.einsum("kt,...kc->...tc", inv_sin, acc_im, precision=lax.Precision.HIGHEST)


def body(query_in, key_in, value_in, short_taps, long_filter, skip_gain, out_weight):
    block = query_in.shape[0]
    width = query_in.shape[1]
    count = 2 * block
    rims = passed_along((query_in[-2:], key_in[-2:], value_in[-2:]), "seq", 1)
    gating = short_conv(rims[0], query_in, short_taps[0])
    keyed = short_conv(rims[1], key_in, short_taps[1])
    valued = short_conv(rims[2], value_in, short_taps[2])
    mixed = (keyed * valued).astype(jnp.bfloat16)
    cos_full, sin_full = dft_tables(block)
    fwd_cos = cos_full.astype(jnp.bfloat16)
    fwd_sin = sin_full.astype(jnp.bfloat16)
    inv_cos = cos_full[:, block:] / count
    inv_sin = sin_full[:, block:] / count
    empty = jnp.zeros((count, width), jnp.float32)

    def lag_spectrum(step_index, earlier):
        current = broadcast(long_filter, "seq", step_index)
        g_re, g_im = filter_spectrum(earlier, current, fwd_cos, fwd_sin)
        return (g_re, g_im, current)

    def one_round(step_index, carry):
        moving, earlier, acc_re, acc_im = carry
        g_re, g_im, earlier = lag_spectrum(step_index, earlier)
        g_re = g_re.astype(jnp.float32)
        g_im = g_im.astype(jnp.float32)
        u_re, u_im = spectrum(moving, fwd_cos[:block], fwd_sin[:block])
        acc_re = acc_re + g_re * u_re - g_im * u_im
        acc_im = acc_im + g_re * u_im + g_im * u_re
        moving = passed_along(moving, "seq", 1)
        return (moving, earlier, acc_re, acc_im)

    start_filter = jnp.zeros((block, width), jnp.bfloat16)
    final = lax.fori_loop(0, lax.axis_size("seq"), one_round, (mixed, start_filter, empty, empty))
    conv = invert(final[2], final[3], inv_cos, inv_sin)
    gated = (gating * (conv + skip_gain * mixed.astype(jnp.float32))).astype(jnp.bfloat16)
    partial_out = jnp.dot(
        gated,
        lax.all_gather(out_weight, "seq", axis=1, tiled=True),
        preferred_element_type=jnp.float32,
    )
    return lax.psum_scatter(
        partial_out.astype(jnp.bfloat16), "chan", scatter_dimension=1, tiled=True
    )


MESH_ID = pl.DeviceIdType.MESH
GROUP = 2
AHEAD = 3
EARLY = 3
MIDDLE = 3
PIECES = (4, 4)
SPLIT = 2
NOW = 4
TURN = (0, 1, 2, 3)
SCHEDULE = (
    "b0", "b1", "w38", "r01", "b2", "r11", "r02", "b3", "r21", "r12", "r03", "10n", "10f", "r31", "r22", "20n",
    "20f", "r13", "11n", "11f", "r32", "21n", "21f", "r23", "12n", "12f", "30n", "30f", "22n", "22f", "r33",
    "13n", "10g", "31n", "31f", "11g", "23n", "13h", "12g", "20g", "21g", "23h", "22g", "32n", "32f", "33n",
    "30g", "31g", "33h", "32g",
)


def packed_tables(block):
    count = 2 * block
    ramp = np.arange(count)
    angle = (ramp[:, None] * ramp[None, :] % count) * (2.0 * math.pi / count)
    cosine, sine = np.cos(angle), np.sin(angle)
    forward = np.concatenate([cosine[:block], cosine[block : block + 1], -sine[1:block]], axis=0)
    weight = np.full((block, 1), 2.0)
    weight[0] = 1.0
    inverse = np.concatenate(
        [weight * cosine[:block, block:], cosine[block : block + 1, block:], -2.0 * sine[1:block, block:]], axis=0
    ) / count
    return jnp.asarray(forward, jnp.bfloat16), jnp.asarray(inverse.T, jnp.float32).astype(jnp.bfloat16)


def remote(src, dst, send, recv, seq, chan):
    return pltpu.make_async_remote_copy(
        src_ref=src, dst_ref=dst, send_sem=send, recv_sem=recv, device_id={"seq": seq, "chan": chan}, device_id_type=MESH_ID
    )


def kernel(
    n_seq, n_chan, q_hbm, k_hbm, v_hbm, taps_hbm, f_ref, skip_hbm, w_hbm, fwd_hbm, inv_hbm, out_ref,
    qkv_ref, taps_ref, skip_ref, w_ref, fwd_ref, inv_ref, in_sem,
    mine, rim_out, rim_in, mix, filt, gate, spec_u, spec_g, acc, gated, half_out, rows, w_far, part, r1_out, r1_in,
    r2_out, r2_in, r3_out,
    a_send, a_recv, rim_sem, w_sem, x_send, x_recv, z_send, up_recv, dn_recv, r_send, r1_recv, r2_recv, o_recv,
):
    s, c = lax.axis_index("seq"), lax.axis_index("chan")
    block, width = f_ref.shape
    for i, src in enumerate((q_hbm, k_hbm, v_hbm)):
        pltpu.make_async_copy(src, qkv_ref.at[i], in_sem.at[0]).start()
    loads = [
        pltpu.make_async_copy(src, dst, in_sem.at[1 + i])
        for i, (src, dst) in enumerate((
            (taps_hbm, taps_ref), (skip_hbm, skip_ref), (fwd_hbm, fwd_ref), (inv_hbm, inv_ref), (w_hbm, w_ref),
        ))
    ]
    for load in loads:
        load.start()
    lines = n_seq // GROUP
    z, x = s // GROUP, s % GROUP
    y, core = c // 2, c % 2
    sub = width // n_seq
    wide = GROUP * sub
    cols = w_ref.shape[1]
    px, pc, py = z * GROUP + (1 - x), y * 2 + (1 - core), (1 - y) * 2 + core

    def lanes(index, size):
        return pl.ds(pl.multiple_of(index * size, size), size)

    barrier = pltpu.get_barrier_semaphore()
    for d in range(1, n_seq):
        pl.semaphore_signal(barrier, inc=1, device_id={"seq": lax.rem(s + d, n_seq), "chan": c}, device_id_type=MESH_ID)
    for other in (pc, py):
        pl.semaphore_signal(barrier, inc=1, device_id={"seq": s, "chan": other}, device_id_type=MESH_ID)
    for other in range(n_chan):
        @pl.when(jnp.logical_or(z != c, other != c))
        def _():
            pl.semaphore_signal(barrier, inc=1, device_id={"seq": c * GROUP + x, "chan": other}, device_id_type=MESH_ID)
    own_filter = pltpu.make_async_copy(f_ref.at[:, lanes(s, sub)], filt.at[:, lanes(s + 1, sub)], in_sem.at[1 + len(loads)])
    own_filter.start()
    filt[:, :sub] = jnp.zeros((block, sub), filt.dtype)
    pl.semaphore_wait(barrier, n_seq - 1 + 2 + n_chan - (z == c).astype(jnp.int32))

    def partner(d):
        return lax.rem(s + d, n_seq)

    def exchange(kind, d, src, dst):
        to = partner(d)
        return remote(src, dst.at[:, lanes(s + (1 if kind == 0 else 0), sub)], a_send.at[min(kind, 1)], a_recv.at[kind], to, c)

    order = list(range(1, n_seq))

    def send_filter(chosen):
        for d in chosen:
            exchange(0, d, f_ref.at[:, lanes(partner(d), sub)], filt).start()

    send_filter(order[:AHEAD])
    pltpu.make_async_copy(qkv_ref, qkv_ref, in_sem.at[0]).wait()
    tail = block - 16
    row16 = lax.broadcasted_iota(jnp.int32, (16, width), 0)
    tails = [pltpu.roll(ref[tail:, :].astype(jnp.float32), 2 + 2 * i, 0) for i, ref in enumerate(qkv_ref.at[j] for j in range(3))]
    rim_out[...] = jnp.where(row16 < 2, tails[0], jnp.where(row16 < 4, tails[1], tails[2])).astype(jnp.bfloat16)
    rim = remote(rim_out, rim_in, rim_sem.at[0], rim_sem.at[1], lax.rem(s + 1, n_seq), c)

    @pl.when(s < n_seq - 1)
    def _():
        rim.start()

    send_filter(order[AHEAD:])
    loads[0].wait()

    @pl.when(s < n_seq - 1)
    def _():
        rim.wait_send()

    @pl.when(s > 0)
    def _():
        rim.wait_recv()

    row = lax.broadcasted_iota(jnp.int32, (block, sub), 0)
    started = s > 0

    def filtered(stream, here):
        x0 = qkv_ref[stream, :, here].astype(jnp.float32)
        edge = jnp.where(started, rim_in[:, here].astype(jnp.float32), 0.0)
        r0, r1 = edge[2 * stream : 2 * stream + 1], edge[2 * stream + 1 : 2 * stream + 2]
        x1 = jnp.where(row == 0, r1, pltpu.roll(x0, 1, 0))
        x2 = jnp.where(row == 0, r0, jnp.where(row == 1, r1, pltpu.roll(x0, 2, 0)))
        t = taps_ref[stream, :, here]
        return t[0:1] * x0 + t[1:2] * x1 + t[2:3] * x2

    def send_all(kind, dst, value_of):
        for d in order + [0]:
            here = lanes(partner(d), sub)
            value = value_of(here).astype(jnp.bfloat16)
            if d == 0:
                dst[:, lanes(s, sub)] = value
            else:
                mine[kind - 1, :, here] = value
                copy = exchange(kind, d, mine.at[kind - 1, :, here], dst)
                copy.start()

    send_all(1, mix, lambda here: filtered(1, here) * filtered(2, here))
    send_all(2, gate, lambda here: filtered(0, here))
    split = cols * SPLIT // 4
    spans = (pl.ds(0, cols), pl.ds(0, split), pl.ds(split, cols - split), pl.ds(0, cols))
    chunks = [(e, r) for e, count in zip((1, 2), PIECES) for r in range(count)]

    def share_weights(first, last):
        for i in range(first, last):
            e, r = chunks[i]
            depth = width // PIECES[e - 1]
            at = (pl.ds(r * depth, depth), spans[e])
            remote(w_hbm.at[at], w_far.at[at], w_sem.at[0], w_sem.at[e], px, c).start()

    share_weights(0, EARLY)
    own_filter.wait()
    loads[2].wait()
    peers = slice(0, (n_seq - 1) * sub)

    def arrival(kind):
        share = mine.at[0, :, peers]
        return remote(share, share, a_send.at[0], a_recv.at[kind], s, c)

    arrival(0).wait_recv()
    segments = jnp.concatenate([filt[:, : n_seq * sub], filt[:, sub:]], axis=0)
    spec_g[...] = jnp.dot(fwd_ref[...], segments, preferred_element_type=jnp.float32).astype(jnp.bfloat16).astype(jnp.float32)
    arrival(1).wait_recv()
    share_weights(EARLY, MIDDLE)
    spec_u[...] = jnp.dot(fwd_ref[:, :block], mix[...], preferred_element_type=jnp.float32)

    def strip(r, carry):
        at = pl.ds(pl.multiple_of(r * 8, 8), 8)
        under = pl.ds(pl.multiple_of(block + r * 8, 8), 8)
        first = lax.broadcasted_iota(jnp.int32, (8, sub), 0) + r * 8 == 0
        part_of = [slice(b * sub, (b + 1) * sub) for b in range(n_seq)]
        u_re = [spec_u[at, here] for here in part_of]
        u_im = [spec_u[under, here] for here in part_of]
        g_re = [spec_g[at, here] for here in part_of]
        g_im = [spec_g[under, here] for here in part_of]
        g_no = [jnp.where(first, 0.0, im) for im in g_im]
        g_on = [jnp.where(first, im, re) for re, im in zip(g_re, g_im)]
        for b in range(n_seq):
            total_re = g_re[0] * u_re[b] - g_no[0] * u_im[b]
            total_im = g_on[0] * u_im[b] + g_no[0] * u_re[b]
            for m in range(1, b + 1):
                total_re += g_re[m] * u_re[b - m] - g_no[m] * u_im[b - m]
                total_im += g_on[m] * u_im[b - m] + g_no[m] * u_re[b - m]
            acc[at, part_of[b]] = total_re
            acc[under, part_of[b]] = total_im
        return carry

    lax.fori_loop(0, block // 8, strip, 0)
    loads[1].wait()
    loads[3].wait()
    conv = jnp.dot(inv_ref[...], acc[...].astype(jnp.bfloat16), preferred_element_type=jnp.float32)
    acc[:block, :] = conv
    arrival(2).wait_recv()
    gain = skip_ref[:, lanes(s, sub)]
    x_copies = {}
    top = z == lines - 1
    bottom = z == 0

    def along(p, h, up):
        slot = jnp.clip(z - (h - 1), 0, lines - 1) if up else jnp.clip(z + (h - 1), 0, lines - 1)
        piece = rows.at[pl.ds(p * block, block), lanes(slot, wide)]
        to = jnp.minimum(z + 1, lines - 1) if up else jnp.maximum(z - 1, 0)
        send, recv = (z_send.at[0], up_recv) if up else (z_send.at[1], dn_recv)
        return remote(piece, piece, send, recv.at[p, h - 1], to * GROUP + x, c)

    early = range(NOW)
    late = range(NOW, lines)

    def start_half(p, owner):
        piece = rows.at[pl.ds(p * block, block), lanes(owner, sub)]
        for up, blocked, to in ((True, top, jnp.minimum(z + 1, lines - 1)), (False, bottom, jnp.maximum(z - 1, 0))):
            @pl.when(jnp.logical_not(blocked))
            def _():
                send, recv = (z_send.at[0], up_recv) if up else (z_send.at[1], dn_recv)
                remote(piece, piece, send, recv.at[p, 0], to * GROUP + x, c).start()

    for p in TURN:
        for e in range(GROUP):
            here = slice(p * wide + e * sub, p * wide + (e + 1) * sub)
            value = gate[:, here].astype(jnp.float32) * (acc[:block, here] + gain * mix[:, here].astype(jnp.float32))
            gated[e] = value.astype(jnp.bfloat16)
        half_out[p] = gated[1 - x]
        rows[pl.ds(p * block, block), lanes(s, sub)] = gated[x]
        copy = remote(half_out.at[p], rows.at[pl.ds(p * block, block), lanes(s, sub)], x_send.at[0], x_recv.at[p], px, c)
        copy.start()
        x_copies[p] = copy
        if p in early:
            start_half(p, s)
    r1, r2, far_seen = {}, {}, []
    half, quarter = block // 2, block // 4
    loads[4].wait()

    def columns(e):
        first = split if e == 2 else 0
        return pl.ds(pl.multiple_of((x if e == 0 else 1 - x) * cols + first, 128), spans[e].size)

    def held(ref, p, e, where=slice(None)):
        return ref.at[p + min(e, 1) * lines, where, spans[e]]

    def place(p, e):
        return min(e, 2) * lines + p

    def stage_one(p, e):
        for i in ((), (1,), (2,), (1, 2))[e]:
            if i not in far_seen:
                far_seen.append(i)
                whole = w_far.at[:, spans[i]]
                remote(whole, whole, w_sem.at[0], w_sem.at[i], px, c).wait_recv()
        lhs = rows[pl.ds(p * block, block), :]
        weight = w_ref[...] if e == 0 else w_far[:, spans[e]]
        held(part, p, e)[...] = jnp.dot(lhs, weight, preferred_element_type=jnp.float32)
        away = pl.ds(pl.multiple_of((1 - core) * half, half), half)
        held(r1_out, p, e)[...] = held(part, p, e, away)[...].astype(jnp.bfloat16)
        r1[p, e] = remote(held(r1_out, p, e), held(r1_in, p, e), r_send.at[0], r1_recv.at[place(p, e)], s, pc)
        r1[p, e].start()

    def stage_two(p, e):
        r1[p, e].wait_recv()
        away = pl.multiple_of((1 - y) * quarter, quarter)
        base = pl.multiple_of(core * half, half)
        held(r2_out, p, e)[...] = (
            held(part, p, e, pl.ds(base + away, quarter))[...]
            + held(r1_in, p, e, pl.ds(away, quarter))[...].astype(jnp.float32)
        ).astype(jnp.bfloat16)
        r2[p, e] = remote(held(r2_out, p, e), held(r2_in, p, e), r_send.at[1], r2_recv.at[place(p, e)], s, py)
        r2[p, e].start()

    strip_at = pl.ds(pl.multiple_of((core * 2 + y) * quarter, quarter), quarter)

    def last_copy(p, e):
        return remote(held(r3_out, p, e), out_ref.at[strip_at, columns(e)], r_send.at[2], o_recv.at[0], p * GROUP + x, z)

    def stage_three(p, e):
        r2[p, e].wait_recv()
        near = pl.multiple_of(y * quarter, quarter)
        base = pl.multiple_of(core * half, half)
        held(r3_out, p, e)[...] = (
            held(part, p, e, pl.ds(base + near, quarter))[...]
            + held(r1_in, p, e, pl.ds(near, quarter))[...].astype(jnp.float32)
            + held(r2_in, p, e)[...].astype(jnp.float32)
        ).astype(jnp.bfloat16)
        own = jnp.logical_and(z == c, z == p)

        @pl.when(own)
        def _():
            pltpu.make_async_copy(held(r3_out, p, e), out_ref.at[strip_at, columns(e)], r_send.at[2]).start()

        @pl.when(jnp.logical_not(own))
        def _():
            last_copy(p, e).start()

    def begin(batch):
        for p in batch:
            if p in late:
                start_half(p, s)
            x_copies[p].wait_recv()
            start_half(p, px)

    def relay(batch, h):
        for p in batch:
            for up, blocked, reach in ((True, top, z >= h), (False, bottom, z + h < lines)):
                @pl.when(reach)
                def _():
                    slot = z - h if up else z + h
                    piece = rows.at[pl.ds(p * block, block), lanes(slot, wide)]
                    recv = (up_recv if up else dn_recv).at[p, h - 1]
                    remote(piece, piece, z_send.at[0], recv, s, c).wait_recv()

                if h < lines - 1:
                    @pl.when(jnp.logical_and(reach, jnp.logical_not(blocked)))
                    def _():
                        along(p, h + 1, up).start()


    def out_wait():
        for local, size in ((False, block), (True, block - quarter)):
            @pl.when((z == c) == local)
            def _():
                landed = out_ref.at[pl.ds(0, size), :]
                remote(landed, landed, r_send.at[2], o_recv.at[0], s, c).wait_recv()

    def send_wait():
        share = mine.at[0, :, peers]
        remote(share, share, a_send.at[0], a_recv.at[0], s, c).wait_send()
        share = mine.at[:, :, peers]
        remote(share, share, a_send.at[1], a_recv.at[0], s, c).wait_send()
        remote(w_hbm, w_far, w_sem.at[0], w_sem.at[1], px, c).wait_send()
        remote(half_out, half_out, x_send.at[0], x_recv.at[0], px, c).wait_send()
        for count in range(1, lines):
            gone = rows.at[:, pl.ds(0, count * wide)]
            for i, here in enumerate((z + 1 == count, lines - z == count)):
                @pl.when(here)
                def _():
                    remote(gone, gone, z_send.at[i], up_recv.at[0, 0], s, c).wait_send()
        for i, done in enumerate((r1_out, r2_out, r3_out)):
            remote(done, done, r_send.at[i], o_recv.at[0], s, c).wait_send()

    for act in SCHEDULE:
        kind, p = act[0], int(act[1])
        if kind != "w":
            p = TURN[p]
        if kind == "b":
            begin([p])
        elif kind == "r":
            relay([p], int(act[2]))
        elif kind == "w":
            share_weights(p, int(act[2], 16))
        else:
            stage = {"1": stage_one, "2": stage_two, "3": stage_three}[kind]
            stage(p, "nfgh".index(act[2]))
    out_wait()
    send_wait()


def fused(n_seq, n_chan, query_in, key_in, value_in, short_taps, long_filter, skip_gain, out_weight):
    block, width = query_in.shape
    sub = width // n_seq
    lines = n_seq // GROUP
    cols = out_weight.shape[1]
    count = 2 * block
    forward, inverse = packed_tables(block)
    bf16, f32 = jnp.bfloat16, jnp.float32
    dma = pltpu.SemaphoreType.DMA
    units = GROUP * lines
    return pl.pallas_call(
        functools.partial(kernel, n_seq, n_chan),
        out_shape=pltpu.VMEM((block, GROUP * cols), bf16),
        in_specs=[pl.BlockSpec(memory_space=pl.ANY)] * 9,
        out_specs=pl.BlockSpec(memory_space=pltpu.VMEM),
        scratch_shapes=[
            pltpu.VMEM((3, block, width), bf16),
            pltpu.VMEM(short_taps.shape, f32),
            pltpu.VMEM((1, width), f32),
            pltpu.VMEM((width, cols), bf16),
            pltpu.VMEM(forward.shape, bf16),
            pltpu.VMEM(inverse.shape, bf16),
            dma((7,)),
            pltpu.VMEM((2, block, width), bf16),
            pltpu.VMEM((16, width), bf16),
            pltpu.VMEM((16, width), bf16),
            pltpu.VMEM((block, n_seq * sub), bf16),
            pltpu.VMEM((block, (n_seq + 1) * sub), bf16),
            pltpu.VMEM((block, n_seq * sub), bf16),
            pltpu.VMEM((count, n_seq * sub), f32),
            pltpu.VMEM((count, n_seq * sub), f32),
            pltpu.VMEM((count, n_seq * sub), f32),
            pltpu.VMEM((GROUP, block, sub), bf16),
            pltpu.VMEM((lines, block, sub), bf16),
            pltpu.VMEM((lines * block, width), bf16),
            pltpu.VMEM((width, cols), bf16),
            pltpu.VMEM((units, block, cols), f32),
            pltpu.VMEM((units, block // 2, cols), bf16),
            pltpu.VMEM((units, block // 2, cols), bf16),
            pltpu.VMEM((units, block // 4, cols), bf16),
            pltpu.VMEM((units, block // 4, cols), bf16),
            pltpu.VMEM((units, block // 4, cols), bf16),
            dma((2,)),
            dma((3,)),
            dma((2,)),
            dma((3,)),
            dma((1,)),
            dma((lines,)),
            dma((2,)),
            dma((lines, lines - 1)),
            dma((lines, lines - 1)),
            dma((3,)),
            dma((3 * lines,)),
            dma((3 * lines,)),
            dma((1,)),
        ],
        compiler_params=pltpu.CompilerParams(collective_id=0, has_side_effects=True, vmem_limit_bytes=60 * 2**20),
    )(
        query_in, key_in, value_in, short_taps, long_filter, skip_gain.reshape(1, width), out_weight,
        forward, inverse,
    )


def solution(mesh):
    in_specs = (
        P("seq", "chan"),
        P("seq", "chan"),
        P("seq", "chan"),
        P(None, None, "chan"),
        P("seq", "chan"),
        P("chan"),
        P("chan", "seq"),
    )
    out_specs = P("seq", "chan")
    n_seq, n_chan = mesh.shape["seq"], mesh.shape["chan"]

    def device_part(*args):
        width, cols = args[0].shape[1], args[-1].shape[1]
        fits = n_chan == 4 and n_seq == GROUP * n_chan and width % (128 * n_seq) == 0 and cols % 128 == 0
        if fits and args[0].shape[0] % 128 == 0:
            return fused(n_seq, n_chan, *args)
        return body(*args)

    return jax.shard_map(device_part, mesh=mesh, in_specs=in_specs, out_specs=out_specs, check_vma=False)
```

```python
import functools
import math

import jax
import jax.numpy as jnp
import numpy as np
from jax import lax
from jax.experimental import pallas as pl
from jax.experimental.pallas import tpu as pltpu
from jax.sharding import PartitionSpec as P


def passed_along(value, axis, steps):
    count = lax.axis_size(axis)
    first, last = (max(0, -steps), min(count, count - steps))
    return lax.ppermute(value, axis, [(source, source + steps) for source in range(first, last)])


def broadcast(array, axis, root):
    mine = lax.axis_index(axis) == root
    return lax.psum(jnp.where(mine, array, jnp.zeros_like(array)), axis)


def dft_tables(length):
    count = 2 * length
    ramp = jnp.arange(count, dtype=jnp.int32)
    product = ramp[:, None] * ramp[None, :] % count
    angle = product.astype(jnp.float32) * (2.0 * math.pi / count)
    return (jnp.cos(angle), jnp.sin(angle))


def short_conv(rim, stream, taps):
    whole = jnp.concatenate([rim, stream], axis=0).astype(jnp.float32)
    return taps[0] * whole[2:] + taps[1] * whole[1:-1] + taps[2] * whole[:-2]


def spectrum(signal, cos_part, sin_part):
    real = jnp.einsum("nk,nc->kc", cos_part, signal, preferred_element_type=jnp.float32)
    imag = -jnp.einsum("nk,nc->kc", sin_part, signal, preferred_element_type=jnp.float32)
    return (real, imag)


def filter_spectrum(earlier, current, cos_part, sin_part):
    segment = jnp.concatenate([earlier, current], axis=0)
    real, imag = spectrum(segment, cos_part, sin_part)
    real16 = lax.optimization_barrier(real.astype(jnp.bfloat16))
    imag16 = lax.optimization_barrier(imag.astype(jnp.bfloat16))
    return (real16, imag16)


def invert(acc_re, acc_im, inv_cos, inv_sin):
    first = jnp.einsum("kt,...kc->...tc", inv_cos, acc_re, precision=lax.Precision.HIGHEST)
    return first - jnp.einsum("kt,...kc->...tc", inv_sin, acc_im, precision=lax.Precision.HIGHEST)


def body(query_in, key_in, value_in, short_taps, long_filter, skip_gain, out_weight):
    block = query_in.shape[0]
    width = query_in.shape[1]
    count = 2 * block
    rims = passed_along((query_in[-2:], key_in[-2:], value_in[-2:]), "seq", 1)
    gating = short_conv(rims[0], query_in, short_taps[0])
    keyed = short_conv(rims[1], key_in, short_taps[1])
    valued = short_conv(rims[2], value_in, short_taps[2])
    mixed = (keyed * valued).astype(jnp.bfloat16)
    cos_full, sin_full = dft_tables(block)
    fwd_cos = cos_full.astype(jnp.bfloat16)
    fwd_sin = sin_full.astype(jnp.bfloat16)
    inv_cos = cos_full[:, block:] / count
    inv_sin = sin_full[:, block:] / count
    empty = jnp.zeros((count, width), jnp.float32)

    def lag_spectrum(step_index, earlier):
        current = broadcast(long_filter, "seq", step_index)
        g_re, g_im = filter_spectrum(earlier, current, fwd_cos, fwd_sin)
        return (g_re, g_im, current)

    def one_round(step_index, carry):
        moving, earlier, acc_re, acc_im = carry
        g_re, g_im, earlier = lag_spectrum(step_index, earlier)
        g_re = g_re.astype(jnp.float32)
        g_im = g_im.astype(jnp.float32)
        u_re, u_im = spectrum(moving, fwd_cos[:block], fwd_sin[:block])
        acc_re = acc_re + g_re * u_re - g_im * u_im
        acc_im = acc_im + g_re * u_im + g_im * u_re
        moving = passed_along(moving, "seq", 1)
        return (moving, earlier, acc_re, acc_im)

    start_filter = jnp.zeros((block, width), jnp.bfloat16)
    final = lax.fori_loop(0, lax.axis_size("seq"), one_round, (mixed, start_filter, empty, empty))
    conv = invert(final[2], final[3], inv_cos, inv_sin)
    gated = (gating * (conv + skip_gain * mixed.astype(jnp.float32))).astype(jnp.bfloat16)
    partial_out = jnp.dot(
        gated,
        lax.all_gather(out_weight, "seq", axis=1, tiled=True),
        preferred_element_type=jnp.float32,
    )
    return lax.psum_scatter(
        partial_out.astype(jnp.bfloat16), "chan", scatter_dimension=1, tiled=True
    )


MESH_ID = pl.DeviceIdType.MESH
GROUP = 2
AHEAD = 3
EARLY = 3
MIDDLE = 3
PIECES = (4, 4)
SPLIT = 2
NOW = 4
TURN = (0, 1, 2, 3)
SCHEDULE = (
    "b0", "b1", "b2", "w38", "b3", "r01", "r11", "r02", "r21", "r12", "r03", "r31", "10n", "10f", "r22", "r13",
    "20n", "20f", "11n", "11f", "r32", "21n", "21f", "r23", "12n", "12f", "30n", "30f", "22n", "22f", "r33",
    "13n", "10g", "31n", "31f", "11g", "23n", "13h", "12g", "20g", "21g", "23h", "22g", "32n", "32f", "33n",
    "30g", "31g", "33h", "32g",
)


def packed_tables(block):
    count = 2 * block
    ramp = np.arange(count)
    angle = (ramp[:, None] * ramp[None, :] % count) * (2.0 * math.pi / count)
    cosine, sine = np.cos(angle), np.sin(angle)
    forward = np.concatenate([cosine[:block], cosine[block : block + 1], -sine[1:block]], axis=0)
    weight = np.full((block, 1), 2.0)
    weight[0] = 1.0
    inverse = np.concatenate(
        [weight * cosine[:block, block:], cosine[block : block + 1, block:], -2.0 * sine[1:block, block:]], axis=0
    ) / count
    return jnp.asarray(forward, jnp.bfloat16), jnp.asarray(inverse.T, jnp.float32).astype(jnp.bfloat16)


def remote(src, dst, send, recv, seq, chan):
    return pltpu.make_async_remote_copy(
        src_ref=src, dst_ref=dst, send_sem=send, recv_sem=recv, device_id={"seq": seq, "chan": chan}, device_id_type=MESH_ID
    )


def kernel(
    n_seq, n_chan, q_hbm, k_hbm, v_hbm, taps_hbm, f_ref, skip_hbm, w_hbm, fwd_hbm, inv_hbm, out_ref,
    qkv_ref, taps_ref, skip_ref, w_ref, fwd_ref, inv_ref, in_sem,
    mine, rim_out, rim_in, mix, filt, gate, spec_u, spec_g, acc, gated, half_out, rows, w_far, part, r1_out, r1_in,
    r2_out, r2_in, r3_out,
    a_send, a_recv, rim_sem, w_sem, x_send, x_recv, z_send, up_recv, dn_recv, r_send, r1_recv, r2_recv, o_recv,
):
    s, c = lax.axis_index("seq"), lax.axis_index("chan")
    block, width = f_ref.shape
    for i, src in enumerate((q_hbm, k_hbm, v_hbm)):
        pltpu.make_async_copy(src, qkv_ref.at[i], in_sem.at[0]).start()
    loads = [
        pltpu.make_async_copy(src, dst, in_sem.at[1 + i])
        for i, (src, dst) in enumerate((
            (taps_hbm, taps_ref), (skip_hbm, skip_ref), (fwd_hbm, fwd_ref), (inv_hbm, inv_ref), (w_hbm, w_ref),
        ))
    ]
    for load in loads:
        load.start()
    lines = n_seq // GROUP
    z, x = s // GROUP, s % GROUP
    y, core = c // 2, c % 2
    sub = width // n_seq
    wide = GROUP * sub
    cols = w_ref.shape[1]
    px, pc, py = z * GROUP + (1 - x), y * 2 + (1 - core), (1 - y) * 2 + core

    def lanes(index, size):
        return pl.ds(pl.multiple_of(index * size, size), size)

    barrier = pltpu.get_barrier_semaphore()
    for d in range(1, n_seq):
        pl.semaphore_signal(barrier, inc=1, device_id={"seq": lax.rem(s + d, n_seq), "chan": c}, device_id_type=MESH_ID)
    for other in (pc, py):
        pl.semaphore_signal(barrier, inc=1, device_id={"seq": s, "chan": other}, device_id_type=MESH_ID)
    for other in range(n_chan):
        @pl.when(jnp.logical_or(z != c, other != c))
        def _():
            pl.semaphore_signal(barrier, inc=1, device_id={"seq": c * GROUP + x, "chan": other}, device_id_type=MESH_ID)
    own_filter = pltpu.make_async_copy(f_ref.at[:, lanes(s, sub)], filt.at[:, lanes(s + 1, sub)], in_sem.at[1 + len(loads)])
    own_filter.start()
    filt[:, :sub] = jnp.zeros((block, sub), filt.dtype)
    pl.semaphore_wait(barrier, n_seq - 1 + 2 + n_chan - (z == c).astype(jnp.int32))

    def partner(d):
        return lax.rem(s + d, n_seq)

    def exchange(kind, d, src, dst):
        to = partner(d)
        return remote(src, dst.at[:, lanes(s + (1 if kind == 0 else 0), sub)], a_send.at[min(kind, 1)], a_recv.at[kind], to, c)

    order = list(range(1, n_seq))

    def send_filter(chosen):
        for d in chosen:
            exchange(0, d, f_ref.at[:, lanes(partner(d), sub)], filt).start()

    send_filter(order[:AHEAD])
    pltpu.make_async_copy(qkv_ref, qkv_ref, in_sem.at[0]).wait()
    tail = block - 16
    row16 = lax.broadcasted_iota(jnp.int32, (16, width), 0)
    tails = [pltpu.roll(ref[tail:, :].astype(jnp.float32), 2 + 2 * i, 0) for i, ref in enumerate(qkv_ref.at[j] for j in range(3))]
    rim_out[...] = jnp.where(row16 < 2, tails[0], jnp.where(row16 < 4, tails[1], tails[2])).astype(jnp.bfloat16)
    rim = remote(rim_out, rim_in, rim_sem.at[0], rim_sem.at[1], lax.rem(s + 1, n_seq), c)

    @pl.when(s < n_seq - 1)
    def _():
        rim.start()

    send_filter(order[AHEAD:])
    loads[0].wait()

    @pl.when(s < n_seq - 1)
    def _():
        rim.wait_send()

    @pl.when(s > 0)
    def _():
        rim.wait_recv()

    row = lax.broadcasted_iota(jnp.int32, (block, sub), 0)
    started = s > 0

    def filtered(stream, here):
        x0 = qkv_ref[stream, :, here].astype(jnp.float32)
        edge = jnp.where(started, rim_in[:, here].astype(jnp.float32), 0.0)
        r0, r1 = edge[2 * stream : 2 * stream + 1], edge[2 * stream + 1 : 2 * stream + 2]
        x1 = jnp.where(row == 0, r1, pltpu.roll(x0, 1, 0))
        x2 = jnp.where(row == 0, r0, jnp.where(row == 1, r1, pltpu.roll(x0, 2, 0)))
        t = taps_ref[stream, :, here]
        return t[0:1] * x0 + t[1:2] * x1 + t[2:3] * x2

    def send_all(kind, dst, value_of):
        for d in order + [0]:
            here = lanes(partner(d), sub)
            value = value_of(here).astype(jnp.bfloat16)
            if d == 0:
                dst[:, lanes(s, sub)] = value
            else:
                mine[kind - 1, :, here] = value
                copy = exchange(kind, d, mine.at[kind - 1, :, here], dst)
                copy.start()

    send_all(1, mix, lambda here: filtered(1, here) * filtered(2, here))
    send_all(2, gate, lambda here: filtered(0, here))
    split = cols * SPLIT // 4
    spans = (pl.ds(0, cols), pl.ds(0, split), pl.ds(split, cols - split), pl.ds(0, cols))
    chunks = [(e, r) for e, count in zip((1, 2), PIECES) for r in range(count)]

    def share_weights(first, last):
        for i in range(first, last):
            e, r = chunks[i]
            depth = width // PIECES[e - 1]
            at = (pl.ds(r * depth, depth), spans[e])
            remote(w_hbm.at[at], w_far.at[at], w_sem.at[0], w_sem.at[e], px, c).start()

    share_weights(0, EARLY)
    own_filter.wait()
    loads[2].wait()
    peers = slice(0, (n_seq - 1) * sub)

    def arrival(kind):
        share = mine.at[0, :, peers]
        return remote(share, share, a_send.at[0], a_recv.at[kind], s, c)

    arrival(0).wait_recv()
    segments = jnp.concatenate([filt[:, : n_seq * sub], filt[:, sub:]], axis=0)
    spec_g[...] = jnp.dot(fwd_ref[...], segments, preferred_element_type=jnp.float32).astype(jnp.bfloat16).astype(jnp.float32)
    arrival(1).wait_recv()
    share_weights(EARLY, MIDDLE)
    spec_u[...] = jnp.dot(fwd_ref[:, :block], mix[...], preferred_element_type=jnp.float32)

    def strip(r, carry):
        at = pl.ds(pl.multiple_of(r * 8, 8), 8)
        under = pl.ds(pl.multiple_of(block + r * 8, 8), 8)
        first = lax.broadcasted_iota(jnp.int32, (8, sub), 0) + r * 8 == 0
        part_of = [slice(b * sub, (b + 1) * sub) for b in range(n_seq)]
        u_re = [spec_u[at, here] for here in part_of]
        u_im = [spec_u[under, here] for here in part_of]
        g_re = [spec_g[at, here] for here in part_of]
        g_im = [spec_g[under, here] for here in part_of]
        g_no = [jnp.where(first, 0.0, im) for im in g_im]
        g_on = [jnp.where(first, im, re) for re, im in zip(g_re, g_im)]
        for b in range(n_seq):
            total_re = g_re[0] * u_re[b] - g_no[0] * u_im[b]
            total_im = g_on[0] * u_im[b] + g_no[0] * u_re[b]
            for m in range(1, b + 1):
                total_re += g_re[m] * u_re[b - m] - g_no[m] * u_im[b - m]
                total_im += g_on[m] * u_im[b - m] + g_no[m] * u_re[b - m]
            acc[at, part_of[b]] = total_re
            acc[under, part_of[b]] = total_im
        return carry

    lax.fori_loop(0, block // 8, strip, 0)
    loads[1].wait()
    loads[3].wait()
    conv = jnp.dot(inv_ref[...], acc[...].astype(jnp.bfloat16), preferred_element_type=jnp.float32)
    acc[:block, :] = conv
    arrival(2).wait_recv()
    gain = skip_ref[:, lanes(s, sub)]
    x_copies = {}
    top = z == lines - 1
    bottom = z == 0

    def along(p, h, up):
        slot = jnp.clip(z - (h - 1), 0, lines - 1) if up else jnp.clip(z + (h - 1), 0, lines - 1)
        piece = rows.at[pl.ds(p * block, block), lanes(slot, wide)]
        to = jnp.minimum(z + 1, lines - 1) if up else jnp.maximum(z - 1, 0)
        send, recv = (z_send.at[0], up_recv) if up else (z_send.at[1], dn_recv)
        return remote(piece, piece, send, recv.at[p, h - 1], to * GROUP + x, c)

    early = range(NOW)
    late = range(NOW, lines)

    def start_half(p, owner):
        piece = rows.at[pl.ds(p * block, block), lanes(owner, sub)]
        for up, blocked, to in ((True, top, jnp.minimum(z + 1, lines - 1)), (False, bottom, jnp.maximum(z - 1, 0))):
            @pl.when(jnp.logical_not(blocked))
            def _():
                send, recv = (z_send.at[0], up_recv) if up else (z_send.at[1], dn_recv)
                remote(piece, piece, send, recv.at[p, 0], to * GROUP + x, c).start()

    for p in TURN:
        for e in range(GROUP):
            here = slice(p * wide + e * sub, p * wide + (e + 1) * sub)
            value = gate[:, here].astype(jnp.float32) * (acc[:block, here] + gain * mix[:, here].astype(jnp.float32))
            gated[e] = value.astype(jnp.bfloat16)
        half_out[p] = gated[1 - x]
        rows[pl.ds(p * block, block), lanes(s, sub)] = gated[x]
        copy = remote(half_out.at[p], rows.at[pl.ds(p * block, block), lanes(s, sub)], x_send.at[0], x_recv.at[p], px, c)
        copy.start()
        x_copies[p] = copy
        if p in early:
            start_half(p, s)
    r1, r2, far_seen = {}, {}, []
    half, quarter = block // 2, block // 4
    loads[4].wait()

    def columns(e):
        first = split if e == 2 else 0
        return pl.ds(pl.multiple_of((x if e == 0 else 1 - x) * cols + first, 128), spans[e].size)

    def held(ref, p, e, where=slice(None)):
        return ref.at[p + min(e, 1) * lines, where, spans[e]]

    def place(p, e):
        return min(e, 2) * lines + p

    def stage_one(p, e):
        for i in ((), (1,), (2,), (1, 2))[e]:
            if i not in far_seen:
                far_seen.append(i)
                whole = w_far.at[:, spans[i]]
                remote(whole, whole, w_sem.at[0], w_sem.at[i], px, c).wait_recv()
        lhs = rows[pl.ds(p * block, block), :]
        weight = w_ref[...] if e == 0 else w_far[:, spans[e]]
        held(part, p, e)[...] = jnp.dot(lhs, weight, preferred_element_type=jnp.float32)
        away = pl.ds(pl.multiple_of((1 - core) * half, half), half)
        held(r1_out, p, e)[...] = held(part, p, e, away)[...].astype(jnp.bfloat16)
        r1[p, e] = remote(held(r1_out, p, e), held(r1_in, p, e), r_send.at[0], r1_recv.at[place(p, e)], s, pc)
        r1[p, e].start()

    def stage_two(p, e):
        r1[p, e].wait_recv()
        away = pl.multiple_of((1 - y) * quarter, quarter)
        base = pl.multiple_of(core * half, half)
        held(r2_out, p, e)[...] = (
            held(part, p, e, pl.ds(base + away, quarter))[...]
            + held(r1_in, p, e, pl.ds(away, quarter))[...].astype(jnp.float32)
        ).astype(jnp.bfloat16)
        r2[p, e] = remote(held(r2_out, p, e), held(r2_in, p, e), r_send.at[1], r2_recv.at[place(p, e)], s, py)
        r2[p, e].start()

    strip_at = pl.ds(pl.multiple_of((core * 2 + y) * quarter, quarter), quarter)

    def last_copy(p, e):
        return remote(held(r3_out, p, e), out_ref.at[strip_at, columns(e)], r_send.at[2], o_recv.at[0], p * GROUP + x, z)

    def stage_three(p, e):
        r2[p, e].wait_recv()
        near = pl.multiple_of(y * quarter, quarter)
        base = pl.multiple_of(core * half, half)
        held(r3_out, p, e)[...] = (
            held(part, p, e, pl.ds(base + near, quarter))[...]
            + held(r1_in, p, e, pl.ds(near, quarter))[...].astype(jnp.float32)
            + held(r2_in, p, e)[...].astype(jnp.float32)
        ).astype(jnp.bfloat16)
        own = jnp.logical_and(z == c, z == p)

        @pl.when(own)
        def _():
            pltpu.make_async_copy(held(r3_out, p, e), out_ref.at[strip_at, columns(e)], r_send.at[2]).start()

        @pl.when(jnp.logical_not(own))
        def _():
            last_copy(p, e).start()

    def begin(batch):
        for p in batch:
            if p in late:
                start_half(p, s)
            x_copies[p].wait_recv()
            start_half(p, px)

    def relay(batch, h):
        for p in batch:
            for up, blocked, reach in ((True, top, z >= h), (False, bottom, z + h < lines)):
                @pl.when(reach)
                def _():
                    slot = z - h if up else z + h
                    piece = rows.at[pl.ds(p * block, block), lanes(slot, wide)]
                    recv = (up_recv if up else dn_recv).at[p, h - 1]
                    remote(piece, piece, z_send.at[0], recv, s, c).wait_recv()

                if h < lines - 1:
                    @pl.when(jnp.logical_and(reach, jnp.logical_not(blocked)))
                    def _():
                        along(p, h + 1, up).start()


    def out_wait():
        for local, size in ((False, block), (True, block - quarter)):
            @pl.when((z == c) == local)
            def _():
                landed = out_ref.at[pl.ds(0, size), :]
                remote(landed, landed, r_send.at[2], o_recv.at[0], s, c).wait_recv()

    def send_wait():
        share = mine.at[0, :, peers]
        remote(share, share, a_send.at[0], a_recv.at[0], s, c).wait_send()
        share = mine.at[:, :, peers]
        remote(share, share, a_send.at[1], a_recv.at[0], s, c).wait_send()
        remote(w_hbm, w_far, w_sem.at[0], w_sem.at[1], px, c).wait_send()
        remote(half_out, half_out, x_send.at[0], x_recv.at[0], px, c).wait_send()
        for count in range(1, lines):
            gone = rows.at[:, pl.ds(0, count * wide)]
            for i, here in enumerate((z + 1 == count, lines - z == count)):
                @pl.when(here)
                def _():
                    remote(gone, gone, z_send.at[i], up_recv.at[0, 0], s, c).wait_send()
        for i, done in enumerate((r1_out, r2_out, r3_out)):
            remote(done, done, r_send.at[i], o_recv.at[0], s, c).wait_send()

    for act in SCHEDULE:
        kind, p = act[0], int(act[1])
        if kind != "w":
            p = TURN[p]
        if kind == "b":
            begin([p])
        elif kind == "r":
            relay([p], int(act[2]))
        elif kind == "w":
            share_weights(p, int(act[2], 16))
        else:
            stage = {"1": stage_one, "2": stage_two, "3": stage_three}[kind]
            stage(p, "nfgh".index(act[2]))
    out_wait()
    send_wait()


def fused(n_seq, n_chan, query_in, key_in, value_in, short_taps, long_filter, skip_gain, out_weight):
    block, width = query_in.shape
    sub = width // n_seq
    lines = n_seq // GROUP
    cols = out_weight.shape[1]
    count = 2 * block
    forward, inverse = packed_tables(block)
    bf16, f32 = jnp.bfloat16, jnp.float32
    dma = pltpu.SemaphoreType.DMA
    units = GROUP * lines
    return pl.pallas_call(
        functools.partial(kernel, n_seq, n_chan),
        out_shape=pltpu.VMEM((block, GROUP * cols), bf16),
        in_specs=[pl.BlockSpec(memory_space=pl.ANY)] * 9,
        out_specs=pl.BlockSpec(memory_space=pltpu.VMEM),
        scratch_shapes=[
            pltpu.VMEM((3, block, width), bf16),
            pltpu.VMEM(short_taps.shape, f32),
            pltpu.VMEM((1, width), f32),
            pltpu.VMEM((width, cols), bf16),
            pltpu.VMEM(forward.shape, bf16),
            pltpu.VMEM(inverse.shape, bf16),
            dma((7,)),
            pltpu.VMEM((2, block, width), bf16),
            pltpu.VMEM((16, width), bf16),
            pltpu.VMEM((16, width), bf16),
            pltpu.VMEM((block, n_seq * sub), bf16),
            pltpu.VMEM((block, (n_seq + 1) * sub), bf16),
            pltpu.VMEM((block, n_seq * sub), bf16),
            pltpu.VMEM((count, n_seq * sub), f32),
            pltpu.VMEM((count, n_seq * sub), f32),
            pltpu.VMEM((count, n_seq * sub), f32),
            pltpu.VMEM((GROUP, block, sub), bf16),
            pltpu.VMEM((lines, block, sub), bf16),
            pltpu.VMEM((lines * block, width), bf16),
            pltpu.VMEM((width, cols), bf16),
            pltpu.VMEM((units, block, cols), f32),
            pltpu.VMEM((units, block // 2, cols), bf16),
            pltpu.VMEM((units, block // 2, cols), bf16),
            pltpu.VMEM((units, block // 4, cols), bf16),
            pltpu.VMEM((units, block // 4, cols), bf16),
            pltpu.VMEM((units, block // 4, cols), bf16),
            dma((2,)),
            dma((3,)),
            dma((2,)),
            dma((3,)),
            dma((1,)),
            dma((lines,)),
            dma((2,)),
            dma((lines, lines - 1)),
            dma((lines, lines - 1)),
            dma((3,)),
            dma((3 * lines,)),
            dma((3 * lines,)),
            dma((1,)),
        ],
        compiler_params=pltpu.CompilerParams(collective_id=0, has_side_effects=True, vmem_limit_bytes=60 * 2**20),
    )(
        query_in, key_in, value_in, short_taps, long_filter, skip_gain.reshape(1, width), out_weight,
        forward, inverse,
    )


def solution(mesh):
    in_specs = (
        P("seq", "chan"),
        P("seq", "chan"),
        P("seq", "chan"),
        P(None, None, "chan"),
        P("seq", "chan"),
        P("chan"),
        P("chan", "seq"),
    )
    out_specs = P("seq", "chan")
    n_seq, n_chan = mesh.shape["seq"], mesh.shape["chan"]

    def device_part(*args):
        width, cols = args[0].shape[1], args[-1].shape[1]
        fits = n_chan == 4 and n_seq == GROUP * n_chan and width % (128 * n_seq) == 0 and cols % 128 == 0
        if fits and args[0].shape[0] % 128 == 0:
            return fused(n_seq, n_chan, *args)
        return body(*args)

    return jax.shard_map(device_part, mesh=mesh, in_specs=in_specs, out_specs=out_specs, check_vma=False)
```

```python
import functools
import math

import jax
import jax.numpy as jnp
import numpy as np
from jax import lax
from jax.experimental import pallas as pl
from jax.experimental.pallas import tpu as pltpu
from jax.sharding import PartitionSpec as P


def passed_along(value, axis, steps):
    count = lax.axis_size(axis)
    first, last = (max(0, -steps), min(count, count - steps))
    return lax.ppermute(value, axis, [(source, source + steps) for source in range(first, last)])


def broadcast(array, axis, root):
    mine = lax.axis_index(axis) == root
    return lax.psum(jnp.where(mine, array, jnp.zeros_like(array)), axis)


def dft_tables(length):
    count = 2 * length
    ramp = jnp.arange(count, dtype=jnp.int32)
    product = ramp[:, None] * ramp[None, :] % count
    angle = product.astype(jnp.float32) * (2.0 * math.pi / count)
    return (jnp.cos(angle), jnp.sin(angle))


def short_conv(rim, stream, taps):
    whole = jnp.concatenate([rim, stream], axis=0).astype(jnp.float32)
    return taps[0] * whole[2:] + taps[1] * whole[1:-1] + taps[2] * whole[:-2]


def spectrum(signal, cos_part, sin_part):
    real = jnp.einsum("nk,nc->kc", cos_part, signal, preferred_element_type=jnp.float32)
    imag = -jnp.einsum("nk,nc->kc", sin_part, signal, preferred_element_type=jnp.float32)
    return (real, imag)


def filter_spectrum(earlier, current, cos_part, sin_part):
    segment = jnp.concatenate([earlier, current], axis=0)
    real, imag = spectrum(segment, cos_part, sin_part)
    real16 = lax.optimization_barrier(real.astype(jnp.bfloat16))
    imag16 = lax.optimization_barrier(imag.astype(jnp.bfloat16))
    return (real16, imag16)


def invert(acc_re, acc_im, inv_cos, inv_sin):
    first = jnp.einsum("kt,...kc->...tc", inv_cos, acc_re, precision=lax.Precision.HIGHEST)
    return first - jnp.einsum("kt,...kc->...tc", inv_sin, acc_im, precision=lax.Precision.HIGHEST)


def body(query_in, key_in, value_in, short_taps, long_filter, skip_gain, out_weight):
    block = query_in.shape[0]
    width = query_in.shape[1]
    count = 2 * block
    rims = passed_along((query_in[-2:], key_in[-2:], value_in[-2:]), "seq", 1)
    gating = short_conv(rims[0], query_in, short_taps[0])
    keyed = short_conv(rims[1], key_in, short_taps[1])
    valued = short_conv(rims[2], value_in, short_taps[2])
    mixed = (keyed * valued).astype(jnp.bfloat16)
    cos_full, sin_full = dft_tables(block)
    fwd_cos = cos_full.astype(jnp.bfloat16)
    fwd_sin = sin_full.astype(jnp.bfloat16)
    inv_cos = cos_full[:, block:] / count
    inv_sin = sin_full[:, block:] / count
    empty = jnp.zeros((count, width), jnp.float32)

    def lag_spectrum(step_index, earlier):
        current = broadcast(long_filter, "seq", step_index)
        g_re, g_im = filter_spectrum(earlier, current, fwd_cos, fwd_sin)
        return (g_re, g_im, current)

    def one_round(step_index, carry):
        moving, earlier, acc_re, acc_im = carry
        g_re, g_im, earlier = lag_spectrum(step_index, earlier)
        g_re = g_re.astype(jnp.float32)
        g_im = g_im.astype(jnp.float32)
        u_re, u_im = spectrum(moving, fwd_cos[:block], fwd_sin[:block])
        acc_re = acc_re + g_re * u_re - g_im * u_im
        acc_im = acc_im + g_re * u_im + g_im * u_re
        moving = passed_along(moving, "seq", 1)
        return (moving, earlier, acc_re, acc_im)

    start_filter = jnp.zeros((block, width), jnp.bfloat16)
    final = lax.fori_loop(0, lax.axis_size("seq"), one_round, (mixed, start_filter, empty, empty))
    conv = invert(final[2], final[3], inv_cos, inv_sin)
    gated = (gating * (conv + skip_gain * mixed.astype(jnp.float32))).astype(jnp.bfloat16)
    partial_out = jnp.dot(
        gated,
        lax.all_gather(out_weight, "seq", axis=1, tiled=True),
        preferred_element_type=jnp.float32,
    )
    return lax.psum_scatter(
        partial_out.astype(jnp.bfloat16), "chan", scatter_dimension=1, tiled=True
    )


MESH_ID = pl.DeviceIdType.MESH
GROUP = 2
AHEAD = 3
LEAD = 0
EARLY = 6
MIDDLE = 6
PIECES = (8, 4)
SPLIT = 2
NOW = 4
TURN = (0, 1, 2, 3)
SCHEDULE = (
    "b0", "b1", "b2", "w6C", "b3", "r01", "r11", "r02", "r21", "r12", "r03", "r31", "10n", "10f", "r13", "20n",
    "20f", "11n", "11f", "r22", "r32", "21n", "21f", "r23", "12n", "12f", "30n", "30f", "22n", "22f", "r33",
    "13n", "10g", "31n", "31f", "11g", "23n", "13h", "12g", "20g", "21g", "23h", "22g", "32n", "32f", "33n",
    "30g", "31g", "33h", "32g",
)


def packed_tables(block):
    count = 2 * block
    ramp = np.arange(count)
    angle = (ramp[:, None] * ramp[None, :] % count) * (2.0 * math.pi / count)
    cosine, sine = np.cos(angle), np.sin(angle)
    forward = np.concatenate([cosine[:block], cosine[block : block + 1], -sine[1:block]], axis=0)
    weight = np.full((block, 1), 2.0)
    weight[0] = 1.0
    inverse = np.concatenate(
        [weight * cosine[:block, block:], cosine[block : block + 1, block:], -2.0 * sine[1:block, block:]], axis=0
    ) / count
    return jnp.asarray(forward, jnp.bfloat16), jnp.asarray(inverse.T, jnp.float32).astype(jnp.bfloat16)


def remote(src, dst, send, recv, seq, chan):
    return pltpu.make_async_remote_copy(
        src_ref=src, dst_ref=dst, send_sem=send, recv_sem=recv, device_id={"seq": seq, "chan": chan}, device_id_type=MESH_ID
    )


def kernel(
    n_seq, n_chan, q_hbm, k_hbm, v_hbm, taps_hbm, f_ref, skip_hbm, w_hbm, fwd_hbm, inv_hbm, out_ref,
    qkv_ref, taps_ref, skip_ref, w_ref, fwd_ref, inv_ref, in_sem,
    mine, rim_out, rim_in, mix, filt, gate, spec_u, spec_g, acc, gated, half_out, rows, w_far, part, r1_out, r1_in,
    r2_out, r2_in, r3_out,
    a_send, a_recv, rim_sem, w_sem, x_send, x_recv, z_send, up_recv, dn_recv, r_send, r1_recv, r2_recv, o_recv,
):
    s, c = lax.axis_index("seq"), lax.axis_index("chan")
    block, width = f_ref.shape
    for i, src in enumerate((q_hbm, k_hbm, v_hbm)):
        pltpu.make_async_copy(src, qkv_ref.at[i], in_sem.at[0]).start()
    loads = [
        pltpu.make_async_copy(src, dst, in_sem.at[1 + i])
        for i, (src, dst) in enumerate((
            (taps_hbm, taps_ref), (skip_hbm, skip_ref), (fwd_hbm, fwd_ref), (inv_hbm, inv_ref), (w_hbm, w_ref),
        ))
    ]
    for load in loads:
        load.start()
    lines = n_seq // GROUP
    z, x = s // GROUP, s % GROUP
    y, core = c // 2, c % 2
    sub = width // n_seq
    wide = GROUP * sub
    cols = w_ref.shape[1]
    px, pc, py = z * GROUP + (1 - x), y * 2 + (1 - core), (1 - y) * 2 + core

    def lanes(index, size):
        return pl.ds(pl.multiple_of(index * size, size), size)

    barrier = pltpu.get_barrier_semaphore()
    for d in range(1, n_seq):
        pl.semaphore_signal(barrier, inc=1, device_id={"seq": lax.rem(s + d, n_seq), "chan": c}, device_id_type=MESH_ID)
    for other in (pc, py):
        pl.semaphore_signal(barrier, inc=1, device_id={"seq": s, "chan": other}, device_id_type=MESH_ID)
    for other in range(n_chan):
        @pl.when(jnp.logical_or(z != c, other != c))
        def _():
            pl.semaphore_signal(barrier, inc=1, device_id={"seq": c * GROUP + x, "chan": other}, device_id_type=MESH_ID)
    own_filter = pltpu.make_async_copy(f_ref.at[:, lanes(s, sub)], filt.at[:, lanes(s + 1, sub)], in_sem.at[1 + len(loads)])
    own_filter.start()
    filt[:, :sub] = jnp.zeros((block, sub), filt.dtype)
    pl.semaphore_wait(barrier, n_seq - 1 + 2 + n_chan - (z == c).astype(jnp.int32))

    def partner(d):
        return lax.rem(s + d, n_seq)

    def exchange(kind, d, src, dst):
        to = partner(d)
        return remote(src, dst.at[:, lanes(s + (1 if kind == 0 else 0), sub)], a_send.at[min(kind, 1)], a_recv.at[kind], to, c)

    order = list(range(1, n_seq))

    def send_filter(chosen):
        for d in chosen:
            exchange(0, d, f_ref.at[:, lanes(partner(d), sub)], filt).start()

    send_filter(order[:AHEAD])
    pltpu.make_async_copy(qkv_ref, qkv_ref, in_sem.at[0]).wait()
    tail = block - 16
    row16 = lax.broadcasted_iota(jnp.int32, (16, width), 0)
    tails = [pltpu.roll(ref[tail:, :].astype(jnp.float32), 2 + 2 * i, 0) for i, ref in enumerate(qkv_ref.at[j] for j in range(3))]
    rim_out[...] = jnp.where(row16 < 2, tails[0], jnp.where(row16 < 4, tails[1], tails[2])).astype(jnp.bfloat16)
    rim = remote(rim_out, rim_in, rim_sem.at[0], rim_sem.at[1], lax.rem(s + 1, n_seq), c)

    @pl.when(s < n_seq - 1)
    def _():
        rim.start()

    send_filter(order[AHEAD:])

    split = cols * SPLIT // 4
    spans = (pl.ds(0, cols), pl.ds(0, split), pl.ds(split, cols - split), pl.ds(0, cols))
    chunks = [(e, r) for e, count in zip((1, 2), PIECES) for r in range(count)]

    def share_weights(first, last):
        for i in range(first, last):
            e, r = chunks[i]
            depth = width // PIECES[e - 1]
            at = (pl.ds(r * depth, depth), spans[e])
            remote(w_hbm.at[at], w_far.at[at], w_sem.at[0], w_sem.at[e], px, c).start()

    share_weights(0, LEAD)
    loads[0].wait()

    @pl.when(s < n_seq - 1)
    def _():
        rim.wait_send()

    @pl.when(s > 0)
    def _():
        rim.wait_recv()

    row = lax.broadcasted_iota(jnp.int32, (block, sub), 0)
    started = s > 0

    def filtered(stream, here):
        x0 = qkv_ref[stream, :, here].astype(jnp.float32)
        edge = jnp.where(started, rim_in[:, here].astype(jnp.float32), 0.0)
        r0, r1 = edge[2 * stream : 2 * stream + 1], edge[2 * stream + 1 : 2 * stream + 2]
        x1 = jnp.where(row == 0, r1, pltpu.roll(x0, 1, 0))
        x2 = jnp.where(row == 0, r0, jnp.where(row == 1, r1, pltpu.roll(x0, 2, 0)))
        t = taps_ref[stream, :, here]
        return t[0:1] * x0 + t[1:2] * x1 + t[2:3] * x2

    def send_all(kind, dst, value_of):
        for d in order + [0]:
            here = lanes(partner(d), sub)
            value = value_of(here).astype(jnp.bfloat16)
            if d == 0:
                dst[:, lanes(s, sub)] = value
            else:
                mine[kind - 1, :, here] = value
                copy = exchange(kind, d, mine.at[kind - 1, :, here], dst)
                copy.start()

    send_all(1, mix, lambda here: filtered(1, here) * filtered(2, here))
    send_all(2, gate, lambda here: filtered(0, here))
    share_weights(LEAD, EARLY)
    own_filter.wait()
    loads[2].wait()
    peers = slice(0, (n_seq - 1) * sub)

    def arrival(kind):
        share = mine.at[0, :, peers]
        return remote(share, share, a_send.at[0], a_recv.at[kind], s, c)

    arrival(0).wait_recv()
    segments = jnp.concatenate([filt[:, : n_seq * sub], filt[:, sub:]], axis=0)
    spec_g[...] = jnp.dot(fwd_ref[...], segments, preferred_element_type=jnp.float32).astype(jnp.bfloat16).astype(jnp.float32)
    arrival(1).wait_recv()
    share_weights(EARLY, MIDDLE)
    spec_u[...] = jnp.dot(fwd_ref[:, :block], mix[...], preferred_element_type=jnp.float32)

    def strip(r, carry):
        at = pl.ds(pl.multiple_of(r * 8, 8), 8)
        under = pl.ds(pl.multiple_of(block + r * 8, 8), 8)
        first = lax.broadcasted_iota(jnp.int32, (8, sub), 0) + r * 8 == 0
        part_of = [slice(b * sub, (b + 1) * sub) for b in range(n_seq)]
        u_re = [spec_u[at, here] for here in part_of]
        u_im = [spec_u[under, here] for here in part_of]
        g_re = [spec_g[at, here] for here in part_of]
        g_im = [spec_g[under, here] for here in part_of]
        g_no = [jnp.where(first, 0.0, im) for im in g_im]
        g_on = [jnp.where(first, im, re) for re, im in zip(g_re, g_im)]
        for b in range(n_seq):
            total_re = g_re[0] * u_re[b] - g_no[0] * u_im[b]
            total_im = g_on[0] * u_im[b] + g_no[0] * u_re[b]
            for m in range(1, b + 1):
                total_re += g_re[m] * u_re[b - m] - g_no[m] * u_im[b - m]
                total_im += g_on[m] * u_im[b - m] + g_no[m] * u_re[b - m]
            acc[at, part_of[b]] = total_re
            acc[under, part_of[b]] = total_im
        return carry

    lax.fori_loop(0, block // 8, strip, 0)
    loads[1].wait()
    loads[3].wait()
    conv = jnp.dot(inv_ref[...], acc[...].astype(jnp.bfloat16), preferred_element_type=jnp.float32)
    gain = jnp.concatenate([skip_ref[:, lanes(s, sub)]] * n_seq, axis=1)
    acc[:block, :] = conv + gain * mix[...].astype(jnp.float32)
    arrival(2).wait_recv()
    x_copies = {}
    top = z == lines - 1
    bottom = z == 0

    def along(p, h, up):
        slot = jnp.clip(z - (h - 1), 0, lines - 1) if up else jnp.clip(z + (h - 1), 0, lines - 1)
        piece = rows.at[pl.ds(p * block, block), lanes(slot, wide)]
        to = jnp.minimum(z + 1, lines - 1) if up else jnp.maximum(z - 1, 0)
        send, recv = (z_send.at[0], up_recv) if up else (z_send.at[1], dn_recv)
        return remote(piece, piece, send, recv.at[p, h - 1], to * GROUP + x, c)

    early = range(NOW)
    late = range(NOW, lines)

    def start_half(p, owner):
        piece = rows.at[pl.ds(p * block, block), lanes(owner, sub)]
        for up, blocked, to in ((True, top, jnp.minimum(z + 1, lines - 1)), (False, bottom, jnp.maximum(z - 1, 0))):
            @pl.when(jnp.logical_not(blocked))
            def _():
                send, recv = (z_send.at[0], up_recv) if up else (z_send.at[1], dn_recv)
                remote(piece, piece, send, recv.at[p, 0], to * GROUP + x, c).start()

    for p in TURN:
        for e in range(GROUP):
            here = slice(p * wide + e * sub, p * wide + (e + 1) * sub)
            value = gate[:, here].astype(jnp.float32) * acc[:block, here]
            gated[e] = value.astype(jnp.bfloat16)
        half_out[p] = gated[1 - x]
        rows[pl.ds(p * block, block), lanes(s, sub)] = gated[x]
        copy = remote(half_out.at[p], rows.at[pl.ds(p * block, block), lanes(s, sub)], x_send.at[0], x_recv.at[p], px, c)
        copy.start()
        x_copies[p] = copy
        if p in early:
            start_half(p, s)
    r1, r2, far_seen = {}, {}, []
    half, quarter = block // 2, block // 4
    loads[4].wait()

    def columns(e):
        first = split if e == 2 else 0
        return pl.ds(pl.multiple_of((x if e == 0 else 1 - x) * cols + first, 128), spans[e].size)

    def held(ref, p, e, where=slice(None)):
        return ref.at[p + min(e, 1) * lines, where, spans[e]]

    def place(p, e):
        return min(e, 2) * lines + p

    def stage_one(p, e):
        for i in ((), (1,), (2,), (1, 2))[e]:
            if i not in far_seen:
                far_seen.append(i)
                whole = w_far.at[:, spans[i]]
                remote(whole, whole, w_sem.at[0], w_sem.at[i], px, c).wait_recv()
        lhs = rows[pl.ds(p * block, block), :]
        weight = w_ref[...] if e == 0 else w_far[:, spans[e]]
        held(part, p, e)[...] = jnp.dot(lhs, weight, preferred_element_type=jnp.float32)
        away = pl.ds(pl.multiple_of((1 - core) * half, half), half)
        held(r1_out, p, e)[...] = held(part, p, e, away)[...].astype(jnp.bfloat16)
        r1[p, e] = remote(held(r1_out, p, e), held(r1_in, p, e), r_send.at[0], r1_recv.at[place(p, e)], s, pc)
        r1[p, e].start()

    def stage_two(p, e):
        r1[p, e].wait_recv()
        away = pl.multiple_of((1 - y) * quarter, quarter)
        base = pl.multiple_of(core * half, half)
        held(r2_out, p, e)[...] = (
            held(part, p, e, pl.ds(base + away, quarter))[...]
            + held(r1_in, p, e, pl.ds(away, quarter))[...].astype(jnp.float32)
        ).astype(jnp.bfloat16)
        r2[p, e] = remote(held(r2_out, p, e), held(r2_in, p, e), r_send.at[1], r2_recv.at[place(p, e)], s, py)
        r2[p, e].start()

    strip_at = pl.ds(pl.multiple_of((core * 2 + y) * quarter, quarter), quarter)

    def last_copy(p, e):
        return remote(held(r3_out, p, e), out_ref.at[strip_at, columns(e)], r_send.at[2], o_recv.at[0], p * GROUP + x, z)

    def stage_three(p, e):
        r2[p, e].wait_recv()
        near = pl.multiple_of(y * quarter, quarter)
        base = pl.multiple_of(core * half, half)
        held(r3_out, p, e)[...] = (
            held(part, p, e, pl.ds(base + near, quarter))[...]
            + held(r1_in, p, e, pl.ds(near, quarter))[...].astype(jnp.float32)
            + held(r2_in, p, e)[...].astype(jnp.float32)
        ).astype(jnp.bfloat16)
        own = jnp.logical_and(z == c, z == p)

        @pl.when(own)
        def _():
            pltpu.make_async_copy(held(r3_out, p, e), out_ref.at[strip_at, columns(e)], r_send.at[2]).start()

        @pl.when(jnp.logical_not(own))
        def _():
            last_copy(p, e).start()

    def begin(batch):
        for p in batch:
            if p in late:
                start_half(p, s)
            x_copies[p].wait_recv()
            start_half(p, px)

    def relay(batch, h):
        for p in batch:
            for up, blocked, reach in ((True, top, z >= h), (False, bottom, z + h < lines)):
                @pl.when(reach)
                def _():
                    slot = z - h if up else z + h
                    piece = rows.at[pl.ds(p * block, block), lanes(slot, wide)]
                    recv = (up_recv if up else dn_recv).at[p, h - 1]
                    remote(piece, piece, z_send.at[0], recv, s, c).wait_recv()

                if h < lines - 1:
                    @pl.when(jnp.logical_and(reach, jnp.logical_not(blocked)))
                    def _():
                        along(p, h + 1, up).start()


    def out_wait():
        for local, size in ((False, block), (True, block - quarter)):
            @pl.when((z == c) == local)
            def _():
                landed = out_ref.at[pl.ds(0, size), :]
                remote(landed, landed, r_send.at[2], o_recv.at[0], s, c).wait_recv()

    def send_wait():
        share = mine.at[0, :, peers]
        remote(share, share, a_send.at[0], a_recv.at[0], s, c).wait_send()
        share = mine.at[:, :, peers]
        remote(share, share, a_send.at[1], a_recv.at[0], s, c).wait_send()
        remote(w_hbm, w_far, w_sem.at[0], w_sem.at[1], px, c).wait_send()
        remote(half_out, half_out, x_send.at[0], x_recv.at[0], px, c).wait_send()
        for count in range(1, lines):
            gone = rows.at[:, pl.ds(0, count * wide)]
            for i, here in enumerate((z + 1 == count, lines - z == count)):
                @pl.when(here)
                def _():
                    remote(gone, gone, z_send.at[i], up_recv.at[0, 0], s, c).wait_send()
        for i, done in enumerate((r1_out, r2_out, r3_out)):
            remote(done, done, r_send.at[i], o_recv.at[0], s, c).wait_send()

    for act in SCHEDULE:
        kind, p = act[0], int(act[1])
        if kind != "w":
            p = TURN[p]
        if kind == "b":
            begin([p])
        elif kind == "r":
            relay([p], int(act[2]))
        elif kind == "w":
            share_weights(p, int(act[2], 16))
        else:
            stage = {"1": stage_one, "2": stage_two, "3": stage_three}[kind]
            stage(p, "nfgh".index(act[2]))
    out_wait()
    send_wait()


def fused(n_seq, n_chan, query_in, key_in, value_in, short_taps, long_filter, skip_gain, out_weight):
    block, width = query_in.shape
    sub = width // n_seq
    lines = n_seq // GROUP
    cols = out_weight.shape[1]
    count = 2 * block
    forward, inverse = packed_tables(block)
    bf16, f32 = jnp.bfloat16, jnp.float32
    dma = pltpu.SemaphoreType.DMA
    units = GROUP * lines
    return pl.pallas_call(
        functools.partial(kernel, n_seq, n_chan),
        out_shape=pltpu.VMEM((block, GROUP * cols), bf16),
        in_specs=[pl.BlockSpec(memory_space=pl.ANY)] * 9,
        out_specs=pl.BlockSpec(memory_space=pltpu.VMEM),
        scratch_shapes=[
            pltpu.VMEM((3, block, width), bf16),
            pltpu.VMEM(short_taps.shape, f32),
            pltpu.VMEM((1, width), f32),
            pltpu.VMEM((width, cols), bf16),
            pltpu.VMEM(forward.shape, bf16),
            pltpu.VMEM(inverse.shape, bf16),
            dma((7,)),
            pltpu.VMEM((2, block, width), bf16),
            pltpu.VMEM((16, width), bf16),
            pltpu.VMEM((16, width), bf16),
            pltpu.VMEM((block, n_seq * sub), bf16),
            pltpu.VMEM((block, (n_seq + 1) * sub), bf16),
            pltpu.VMEM((block, n_seq * sub), bf16),
            pltpu.VMEM((count, n_seq * sub), f32),
            pltpu.VMEM((count, n_seq * sub), f32),
            pltpu.VMEM((count, n_seq * sub), f32),
            pltpu.VMEM((GROUP, block, sub), bf16),
            pltpu.VMEM((lines, block, sub), bf16),
            pltpu.VMEM((lines * block, width), bf16),
            pltpu.VMEM((width, cols), bf16),
            pltpu.VMEM((units, block, cols), f32),
            pltpu.VMEM((units, block // 2, cols), bf16),
            pltpu.VMEM((units, block // 2, cols), bf16),
            pltpu.VMEM((units, block // 4, cols), bf16),
            pltpu.VMEM((units, block // 4, cols), bf16),
            pltpu.VMEM((units, block // 4, cols), bf16),
            dma((2,)),
            dma((3,)),
            dma((2,)),
            dma((3,)),
            dma((1,)),
            dma((lines,)),
            dma((2,)),
            dma((lines, lines - 1)),
            dma((lines, lines - 1)),
            dma((3,)),
            dma((3 * lines,)),
            dma((3 * lines,)),
            dma((1,)),
        ],
        compiler_params=pltpu.CompilerParams(collective_id=0, has_side_effects=True, vmem_limit_bytes=60 * 2**20),
    )(
        query_in, key_in, value_in, short_taps, long_filter, skip_gain.reshape(1, width), out_weight,
        forward, inverse,
    )


def solution(mesh):
    in_specs = (
        P("seq", "chan"),
        P("seq", "chan"),
        P("seq", "chan"),
        P(None, None, "chan"),
        P("seq", "chan"),
        P("chan"),
        P("chan", "seq"),
    )
    out_specs = P("seq", "chan")
    n_seq, n_chan = mesh.shape["seq"], mesh.shape["chan"]

    def device_part(*args):
        width, cols = args[0].shape[1], args[-1].shape[1]
        fits = n_chan == 4 and n_seq == GROUP * n_chan and width % (128 * n_seq) == 0 and cols % 128 == 0
        if fits and args[0].shape[0] % 128 == 0:
            return fused(n_seq, n_chan, *args)
        return body(*args)

    return jax.shard_map(device_part, mesh=mesh, in_specs=in_specs, out_specs=out_specs, check_vma=False)
```

```python
import functools
import math

import jax
import jax.numpy as jnp
import numpy as np
from jax import lax
from jax.experimental import pallas as pl
from jax.experimental.pallas import tpu as pltpu
from jax.sharding import PartitionSpec as P


def passed_along(value, axis, steps):
    count = lax.axis_size(axis)
    first, last = (max(0, -steps), min(count, count - steps))
    return lax.ppermute(value, axis, [(source, source + steps) for source in range(first, last)])


def broadcast(array, axis, root):
    mine = lax.axis_index(axis) == root
    return lax.psum(jnp.where(mine, array, jnp.zeros_like(array)), axis)


def dft_tables(length):
    count = 2 * length
    ramp = jnp.arange(count, dtype=jnp.int32)
    product = ramp[:, None] * ramp[None, :] % count
    angle = product.astype(jnp.float32) * (2.0 * math.pi / count)
    return (jnp.cos(angle), jnp.sin(angle))


def short_conv(rim, stream, taps):
    whole = jnp.concatenate([rim, stream], axis=0).astype(jnp.float32)
    return taps[0] * whole[2:] + taps[1] * whole[1:-1] + taps[2] * whole[:-2]


def spectrum(signal, cos_part, sin_part):
    real = jnp.einsum("nk,nc->kc", cos_part, signal, preferred_element_type=jnp.float32)
    imag = -jnp.einsum("nk,nc->kc", sin_part, signal, preferred_element_type=jnp.float32)
    return (real, imag)


def filter_spectrum(earlier, current, cos_part, sin_part):
    segment = jnp.concatenate([earlier, current], axis=0)
    real, imag = spectrum(segment, cos_part, sin_part)
    real16 = lax.optimization_barrier(real.astype(jnp.bfloat16))
    imag16 = lax.optimization_barrier(imag.astype(jnp.bfloat16))
    return (real16, imag16)


def invert(acc_re, acc_im, inv_cos, inv_sin):
    first = jnp.einsum("kt,...kc->...tc", inv_cos, acc_re, precision=lax.Precision.HIGHEST)
    return first - jnp.einsum("kt,...kc->...tc", inv_sin, acc_im, precision=lax.Precision.HIGHEST)


def body(query_in, key_in, value_in, short_taps, long_filter, skip_gain, out_weight):
    block = query_in.shape[0]
    width = query_in.shape[1]
    count = 2 * block
    rims = passed_along((query_in[-2:], key_in[-2:], value_in[-2:]), "seq", 1)
    gating = short_conv(rims[0], query_in, short_taps[0])
    keyed = short_conv(rims[1], key_in, short_taps[1])
    valued = short_conv(rims[2], value_in, short_taps[2])
    mixed = (keyed * valued).astype(jnp.bfloat16)
    cos_full, sin_full = dft_tables(block)
    fwd_cos = cos_full.astype(jnp.bfloat16)
    fwd_sin = sin_full.astype(jnp.bfloat16)
    inv_cos = cos_full[:, block:] / count
    inv_sin = sin_full[:, block:] / count
    empty = jnp.zeros((count, width), jnp.float32)

    def lag_spectrum(step_index, earlier):
        current = broadcast(long_filter, "seq", step_index)
        g_re, g_im = filter_spectrum(earlier, current, fwd_cos, fwd_sin)
        return (g_re, g_im, current)

    def one_round(step_index, carry):
        moving, earlier, acc_re, acc_im = carry
        g_re, g_im, earlier = lag_spectrum(step_index, earlier)
        g_re = g_re.astype(jnp.float32)
        g_im = g_im.astype(jnp.float32)
        u_re, u_im = spectrum(moving, fwd_cos[:block], fwd_sin[:block])
        acc_re = acc_re + g_re * u_re - g_im * u_im
        acc_im = acc_im + g_re * u_im + g_im * u_re
        moving = passed_along(moving, "seq", 1)
        return (moving, earlier, acc_re, acc_im)

    start_filter = jnp.zeros((block, width), jnp.bfloat16)
    final = lax.fori_loop(0, lax.axis_size("seq"), one_round, (mixed, start_filter, empty, empty))
    conv = invert(final[2], final[3], inv_cos, inv_sin)
    gated = (gating * (conv + skip_gain * mixed.astype(jnp.float32))).astype(jnp.bfloat16)
    partial_out = jnp.dot(
        gated,
        lax.all_gather(out_weight, "seq", axis=1, tiled=True),
        preferred_element_type=jnp.float32,
    )
    return lax.psum_scatter(
        partial_out.astype(jnp.bfloat16), "chan", scatter_dimension=1, tiled=True
    )


MESH_ID = pl.DeviceIdType.MESH
GROUP = 2
AHEAD = 3
LEAD = 0
EARLY = 6
MIDDLE = 6
PIECES = (8, 4)
SPLIT = 2
NOW = 4
TURN = (0, 1, 2, 3)
SCHEDULE = (
    "b0", "b1", "b2", "w6C", "b3", "r01", "r11", "r02", "r21", "r12", "r03", "r31", "10n", "10f", "r13", "20n",
    "20f", "11n", "11f", "r22", "r32", "21n", "21f", "r23", "12n", "12f", "30n", "30f", "22n", "22f", "r33",
    "13n", "10g", "31n", "31f", "11g", "23n", "13h", "12g", "20g", "21g", "23h", "22g", "32n", "32f", "33n",
    "30g", "31g", "33h", "32g",
)


def packed_tables(block):
    count = 2 * block
    ramp = np.arange(count)
    angle = (ramp[:, None] * ramp[None, :] % count) * (2.0 * math.pi / count)
    cosine, sine = np.cos(angle), np.sin(angle)
    forward = np.concatenate([cosine[:block], cosine[block : block + 1], -sine[1:block]], axis=0)
    weight = np.full((block, 1), 2.0)
    weight[0] = 1.0
    inverse = np.concatenate(
        [weight * cosine[:block, block:], cosine[block : block + 1, block:], -2.0 * sine[1:block, block:]], axis=0
    ) / count
    return jnp.asarray(forward, jnp.bfloat16), jnp.asarray(inverse.T, jnp.float32).astype(jnp.bfloat16)


def remote(src, dst, send, recv, seq, chan):
    return pltpu.make_async_remote_copy(
        src_ref=src, dst_ref=dst, send_sem=send, recv_sem=recv, device_id={"seq": seq, "chan": chan}, device_id_type=MESH_ID
    )


def kernel(
    n_seq, n_chan, q_hbm, k_hbm, v_hbm, taps_hbm, f_ref, skip_hbm, w_hbm, fwd_hbm, inv_hbm, out_ref,
    qkv_ref, taps_ref, skip_ref, w_ref, fwd_ref, inv_ref, in_sem,
    mine, rim_out, rim_in, mix, filt, gate, spec_u, spec_g, acc, gated, half_out, rows, w_far, part, r1_out, r1_in,
    r2_out, r2_in, r3_out,
    a_send, a_recv, rim_sem, w_sem, x_send, x_recv, z_send, up_recv, dn_recv, r_send, r1_recv, r2_recv, o_recv,
):
    s, c = lax.axis_index("seq"), lax.axis_index("chan")
    block, width = f_ref.shape
    for i, src in enumerate((q_hbm, k_hbm, v_hbm)):
        pltpu.make_async_copy(src, qkv_ref.at[i], in_sem.at[0]).start()
    loads = [
        pltpu.make_async_copy(src, dst, in_sem.at[1 + i])
        for i, (src, dst) in enumerate((
            (taps_hbm, taps_ref), (skip_hbm, skip_ref), (fwd_hbm, fwd_ref), (inv_hbm, inv_ref), (w_hbm, w_ref),
        ))
    ]
    for load in loads:
        load.start()
    lines = n_seq // GROUP
    z, x = s // GROUP, s % GROUP
    y, core = c // 2, c % 2
    sub = width // n_seq
    wide = GROUP * sub
    cols = w_ref.shape[1]
    px, pc, py = z * GROUP + (1 - x), y * 2 + (1 - core), (1 - y) * 2 + core

    def lanes(index, size):
        return pl.ds(pl.multiple_of(index * size, size), size)

    barrier = pltpu.get_barrier_semaphore()
    for d in range(1, n_seq):
        pl.semaphore_signal(barrier, inc=1, device_id={"seq": lax.rem(s + d, n_seq), "chan": c}, device_id_type=MESH_ID)
    for other in (pc, py):
        pl.semaphore_signal(barrier, inc=1, device_id={"seq": s, "chan": other}, device_id_type=MESH_ID)
    for other in range(n_chan):
        @pl.when(jnp.logical_or(z != c, other != c))
        def _():
            pl.semaphore_signal(barrier, inc=1, device_id={"seq": c * GROUP + x, "chan": other}, device_id_type=MESH_ID)
    own_filter = pltpu.make_async_copy(f_ref.at[:, lanes(s, sub)], filt.at[:, lanes(s + 1, sub)], in_sem.at[1 + len(loads)])
    own_filter.start()
    filt[:, :sub] = jnp.zeros((block, sub), filt.dtype)
    pl.semaphore_wait(barrier, n_seq - 1 + 2 + n_chan - (z == c).astype(jnp.int32))

    def partner(d):
        return lax.rem(s + d, n_seq)

    def exchange(kind, d, src, dst):
        to = partner(d)
        return remote(src, dst.at[:, lanes(s + (1 if kind == 0 else 0), sub)], a_send.at[min(kind, 1)], a_recv.at[kind], to, c)

    order = list(range(1, n_seq))

    def send_filter(chosen):
        for d in chosen:
            exchange(0, d, f_ref.at[:, lanes(partner(d), sub)], filt).start()

    send_filter(order[:AHEAD])
    pltpu.make_async_copy(qkv_ref, qkv_ref, in_sem.at[0]).wait()
    tail = block - 16
    row16 = lax.broadcasted_iota(jnp.int32, (16, width), 0)
    tails = [pltpu.roll(ref[tail:, :].astype(jnp.float32), 2 + 2 * i, 0) for i, ref in enumerate(qkv_ref.at[j] for j in range(3))]
    rim_out[...] = jnp.where(row16 < 2, tails[0], jnp.where(row16 < 4, tails[1], tails[2])).astype(jnp.bfloat16)
    rim = remote(rim_out, rim_in, rim_sem.at[0], rim_sem.at[1], lax.rem(s + 1, n_seq), c)

    @pl.when(s < n_seq - 1)
    def _():
        rim.start()

    send_filter(order[AHEAD:])

    split = cols * SPLIT // 4
    spans = (pl.ds(0, cols), pl.ds(0, split), pl.ds(split, cols - split), pl.ds(0, cols))
    chunks = [(e, r) for e, count in zip((1, 2), PIECES) for r in range(count)]

    def share_weights(first, last):
        for i in range(first, last):
            e, r = chunks[i]
            depth = width // PIECES[e - 1]
            at = (pl.ds(r * depth, depth), spans[e])
            remote(w_hbm.at[at], w_far.at[at], w_sem.at[0], w_sem.at[e], px, c).start()

    share_weights(0, LEAD)
    loads[0].wait()

    @pl.when(s < n_seq - 1)
    def _():
        rim.wait_send()

    @pl.when(s > 0)
    def _():
        rim.wait_recv()

    row = lax.broadcasted_iota(jnp.int32, (block, sub), 0)
    started = s > 0

    def filtered(stream, here):
        x0 = qkv_ref[stream, :, here].astype(jnp.float32)
        edge = jnp.where(started, rim_in[:, here].astype(jnp.float32), 0.0)
        r0, r1 = edge[2 * stream : 2 * stream + 1], edge[2 * stream + 1 : 2 * stream + 2]
        x1 = jnp.where(row == 0, r1, pltpu.roll(x0, 1, 0))
        x2 = jnp.where(row == 0, r0, jnp.where(row == 1, r1, pltpu.roll(x0, 2, 0)))
        t = taps_ref[stream, :, here]
        return t[0:1] * x0 + t[1:2] * x1 + t[2:3] * x2

    def send_all(kind, dst, value_of):
        for d in order + [0]:
            here = lanes(partner(d), sub)
            value = value_of(here).astype(jnp.bfloat16)
            if d == 0:
                dst[:, lanes(s, sub)] = value
            else:
                mine[kind - 1, :, here] = value
                copy = exchange(kind, d, mine.at[kind - 1, :, here], dst)
                copy.start()

    send_all(1, mix, lambda here: filtered(1, here) * filtered(2, here))
    send_all(2, gate, lambda here: filtered(0, here))
    share_weights(LEAD, EARLY)
    own_filter.wait()
    loads[2].wait()
    peers = slice(0, (n_seq - 1) * sub)

    def arrival(kind):
        share = mine.at[0, :, peers]
        return remote(share, share, a_send.at[0], a_recv.at[kind], s, c)

    arrival(0).wait_recv()
    segments = jnp.concatenate([filt[:, : n_seq * sub], filt[:, sub:]], axis=0)
    spec_g[...] = jnp.dot(fwd_ref[...], segments, preferred_element_type=jnp.float32).astype(jnp.bfloat16).astype(jnp.float32)
    arrival(1).wait_recv()
    share_weights(EARLY, MIDDLE)
    spec_u[...] = jnp.dot(fwd_ref[:, :block], mix[...], preferred_element_type=jnp.float32)

    def strip(r, carry):
        at = pl.ds(pl.multiple_of(r * 8, 8), 8)
        under = pl.ds(pl.multiple_of(block + r * 8, 8), 8)
        first = lax.broadcasted_iota(jnp.int32, (8, sub), 0) + r * 8 == 0
        part_of = [slice(b * sub, (b + 1) * sub) for b in range(n_seq)]
        u_re = [spec_u[at, here] for here in part_of]
        u_im = [spec_u[under, here] for here in part_of]
        g_re = [spec_g[at, here] for here in part_of]
        g_im = [spec_g[under, here] for here in part_of]
        g_no = [jnp.where(first, 0.0, im) for im in g_im]
        g_on = [jnp.where(first, im, re) for re, im in zip(g_re, g_im)]
        for b in range(n_seq):
            total_re = g_re[0] * u_re[b] - g_no[0] * u_im[b]
            total_im = g_on[0] * u_im[b] + g_no[0] * u_re[b]
            for m in range(1, b + 1):
                total_re += g_re[m] * u_re[b - m] - g_no[m] * u_im[b - m]
                total_im += g_on[m] * u_im[b - m] + g_no[m] * u_re[b - m]
            acc[at, part_of[b]] = total_re
            acc[under, part_of[b]] = total_im
        return carry

    lax.fori_loop(0, block // 8, strip, 0)
    loads[1].wait()
    loads[3].wait()
    conv = jnp.dot(inv_ref[...], acc[...].astype(jnp.bfloat16), preferred_element_type=jnp.float32)
    gain = jnp.concatenate([skip_ref[:, lanes(s, sub)]] * n_seq, axis=1)
    acc[:block, :] = conv + gain * mix[...].astype(jnp.float32)
    arrival(2).wait_recv()
    x_copies = {}
    top = z == lines - 1
    bottom = z == 0

    def along(p, h, up):
        slot = jnp.clip(z - (h - 1), 0, lines - 1) if up else jnp.clip(z + (h - 1), 0, lines - 1)
        piece = rows.at[pl.ds(p * block, block), lanes(slot, wide)]
        to = jnp.minimum(z + 1, lines - 1) if up else jnp.maximum(z - 1, 0)
        send, recv = (z_send.at[0], up_recv) if up else (z_send.at[1], dn_recv)
        return remote(piece, piece, send, recv.at[p, h - 1], to * GROUP + x, c)

    early = range(NOW)
    late = range(NOW, lines)

    def start_half(p, owner):
        piece = rows.at[pl.ds(p * block, block), lanes(owner, sub)]
        for up, blocked, to in ((True, top, jnp.minimum(z + 1, lines - 1)), (False, bottom, jnp.maximum(z - 1, 0))):
            @pl.when(jnp.logical_not(blocked))
            def _():
                send, recv = (z_send.at[0], up_recv) if up else (z_send.at[1], dn_recv)
                remote(piece, piece, send, recv.at[p, 0], to * GROUP + x, c).start()

    for p in TURN:
        for e in range(GROUP):
            here = slice(p * wide + e * sub, p * wide + (e + 1) * sub)
            value = gate[:, here].astype(jnp.float32) * acc[:block, here]
            gated[e] = value.astype(jnp.bfloat16)
        half_out[p] = gated[1 - x]
        rows[pl.ds(p * block, block), lanes(s, sub)] = gated[x]
        copy = remote(half_out.at[p], rows.at[pl.ds(p * block, block), lanes(s, sub)], x_send.at[0], x_recv.at[p], px, c)
        copy.start()
        x_copies[p] = copy
    for p in early:
        start_half(p, s)
    r1, r2, far_seen = {}, {}, []
    half, quarter = block // 2, block // 4
    loads[4].wait()

    def columns(e):
        first = split if e == 2 else 0
        return pl.ds(pl.multiple_of((x if e == 0 else 1 - x) * cols + first, 128), spans[e].size)

    def held(ref, p, e, where=slice(None)):
        return ref.at[p + min(e, 1) * lines, where, spans[e]]

    def place(p, e):
        return min(e, 2) * lines + p

    def stage_one(p, e):
        for i in ((), (1,), (2,), (1, 2))[e]:
            if i not in far_seen:
                far_seen.append(i)
                whole = w_far.at[:, spans[i]]
                remote(whole, whole, w_sem.at[0], w_sem.at[i], px, c).wait_recv()
        lhs = rows[pl.ds(p * block, block), :]
        weight = w_ref[...] if e == 0 else w_far[:, spans[e]]
        held(part, p, e)[...] = jnp.dot(lhs, weight, preferred_element_type=jnp.float32)
        away = pl.ds(pl.multiple_of((1 - core) * half, half), half)
        held(r1_out, p, e)[...] = held(part, p, e, away)[...].astype(jnp.bfloat16)
        r1[p, e] = remote(held(r1_out, p, e), held(r1_in, p, e), r_send.at[0], r1_recv.at[place(p, e)], s, pc)
        r1[p, e].start()

    def stage_two(p, e):
        r1[p, e].wait_recv()
        away = pl.multiple_of((1 - y) * quarter, quarter)
        base = pl.multiple_of(core * half, half)
        held(r2_out, p, e)[...] = (
            held(part, p, e, pl.ds(base + away, quarter))[...]
            + held(r1_in, p, e, pl.ds(away, quarter))[...].astype(jnp.float32)
        ).astype(jnp.bfloat16)
        r2[p, e] = remote(held(r2_out, p, e), held(r2_in, p, e), r_send.at[1], r2_recv.at[place(p, e)], s, py)
        r2[p, e].start()

    strip_at = pl.ds(pl.multiple_of((core * 2 + y) * quarter, quarter), quarter)

    def last_copy(p, e):
        return remote(held(r3_out, p, e), out_ref.at[strip_at, columns(e)], r_send.at[2], o_recv.at[0], p * GROUP + x, z)

    def stage_three(p, e):
        r2[p, e].wait_recv()
        near = pl.multiple_of(y * quarter, quarter)
        base = pl.multiple_of(core * half, half)
        held(r3_out, p, e)[...] = (
            held(part, p, e, pl.ds(base + near, quarter))[...]
            + held(r1_in, p, e, pl.ds(near, quarter))[...].astype(jnp.float32)
            + held(r2_in, p, e)[...].astype(jnp.float32)
        ).astype(jnp.bfloat16)
        own = jnp.logical_and(z == c, z == p)

        @pl.when(own)
        def _():
            pltpu.make_async_copy(held(r3_out, p, e), out_ref.at[strip_at, columns(e)], r_send.at[2]).start()

        @pl.when(jnp.logical_not(own))
        def _():
            last_copy(p, e).start()

    def begin(batch):
        for p in batch:
            if p in late:
                start_half(p, s)
            x_copies[p].wait_recv()
            start_half(p, px)

    def relay(batch, h):
        for p in batch:
            for up, blocked, reach in ((True, top, z >= h), (False, bottom, z + h < lines)):
                @pl.when(reach)
                def _():
                    slot = z - h if up else z + h
                    piece = rows.at[pl.ds(p * block, block), lanes(slot, wide)]
                    recv = (up_recv if up else dn_recv).at[p, h - 1]
                    remote(piece, piece, z_send.at[0], recv, s, c).wait_recv()

                if h < lines - 1:
                    @pl.when(jnp.logical_and(reach, jnp.logical_not(blocked)))
                    def _():
                        along(p, h + 1, up).start()


    def out_wait():
        for local, size in ((False, block), (True, block - quarter)):
            @pl.when((z == c) == local)
            def _():
                landed = out_ref.at[pl.ds(0, size), :]
                remote(landed, landed, r_send.at[2], o_recv.at[0], s, c).wait_recv()

    def send_wait():
        share = mine.at[0, :, peers]
        remote(share, share, a_send.at[0], a_recv.at[0], s, c).wait_send()
        share = mine.at[:, :, peers]
        remote(share, share, a_send.at[1], a_recv.at[0], s, c).wait_send()
        remote(w_hbm, w_far, w_sem.at[0], w_sem.at[1], px, c).wait_send()
        remote(half_out, half_out, x_send.at[0], x_recv.at[0], px, c).wait_send()
        for count in range(1, lines):
            gone = rows.at[:, pl.ds(0, count * wide)]
            for i, here in enumerate((z + 1 == count, lines - z == count)):
                @pl.when(here)
                def _():
                    remote(gone, gone, z_send.at[i], up_recv.at[0, 0], s, c).wait_send()
        for i, done in enumerate((r1_out, r2_out, r3_out)):
            remote(done, done, r_send.at[i], o_recv.at[0], s, c).wait_send()

    for act in SCHEDULE:
        kind, p = act[0], int(act[1])
        if kind != "w":
            p = TURN[p]
        if kind == "b":
            begin([p])
        elif kind == "r":
            relay([p], int(act[2]))
        elif kind == "w":
            share_weights(p, int(act[2], 16))
        else:
            stage = {"1": stage_one, "2": stage_two, "3": stage_three}[kind]
            stage(p, "nfgh".index(act[2]))
    out_wait()
    send_wait()


def fused(n_seq, n_chan, query_in, key_in, value_in, short_taps, long_filter, skip_gain, out_weight):
    block, width = query_in.shape
    sub = width // n_seq
    lines = n_seq // GROUP
    cols = out_weight.shape[1]
    count = 2 * block
    forward, inverse = packed_tables(block)
    bf16, f32 = jnp.bfloat16, jnp.float32
    dma = pltpu.SemaphoreType.DMA
    units = GROUP * lines
    return pl.pallas_call(
        functools.partial(kernel, n_seq, n_chan),
        out_shape=pltpu.VMEM((block, GROUP * cols), bf16),
        in_specs=[pl.BlockSpec(memory_space=pl.ANY)] * 9,
        out_specs=pl.BlockSpec(memory_space=pltpu.VMEM),
        scratch_shapes=[
            pltpu.VMEM((3, block, width), bf16),
            pltpu.VMEM(short_taps.shape, f32),
            pltpu.VMEM((1, width), f32),
            pltpu.VMEM((width, cols), bf16),
            pltpu.VMEM(forward.shape, bf16),
            pltpu.VMEM(inverse.shape, bf16),
            dma((7,)),
            pltpu.VMEM((2, block, width), bf16),
            pltpu.VMEM((16, width), bf16),
            pltpu.VMEM((16, width), bf16),
            pltpu.VMEM((block, n_seq * sub), bf16),
            pltpu.VMEM((block, (n_seq + 1) * sub), bf16),
            pltpu.VMEM((block, n_seq * sub), bf16),
            pltpu.VMEM((count, n_seq * sub), f32),
            pltpu.VMEM((count, n_seq * sub), f32),
            pltpu.VMEM((count, n_seq * sub), f32),
            pltpu.VMEM((GROUP, block, sub), bf16),
            pltpu.VMEM((lines, block, sub), bf16),
            pltpu.VMEM((lines * block, width), bf16),
            pltpu.VMEM((width, cols), bf16),
            pltpu.VMEM((units, block, cols), f32),
            pltpu.VMEM((units, block // 2, cols), bf16),
            pltpu.VMEM((units, block // 2, cols), bf16),
            pltpu.VMEM((units, block // 4, cols), bf16),
            pltpu.VMEM((units, block // 4, cols), bf16),
            pltpu.VMEM((units, block // 4, cols), bf16),
            dma((2,)),
            dma((3,)),
            dma((2,)),
            dma((3,)),
            dma((1,)),
            dma((lines,)),
            dma((2,)),
            dma((lines, lines - 1)),
            dma((lines, lines - 1)),
            dma((3,)),
            dma((3 * lines,)),
            dma((3 * lines,)),
            dma((1,)),
        ],
        compiler_params=pltpu.CompilerParams(collective_id=0, has_side_effects=True, vmem_limit_bytes=60 * 2**20),
    )(
        query_in, key_in, value_in, short_taps, long_filter, skip_gain.reshape(1, width), out_weight,
        forward, inverse,
    )


def solution(mesh):
    in_specs = (
        P("seq", "chan"),
        P("seq", "chan"),
        P("seq", "chan"),
        P(None, None, "chan"),
        P("seq", "chan"),
        P("chan"),
        P("chan", "seq"),
    )
    out_specs = P("seq", "chan")
    n_seq, n_chan = mesh.shape["seq"], mesh.shape["chan"]

    def device_part(*args):
        width, cols = args[0].shape[1], args[-1].shape[1]
        fits = n_chan == 4 and n_seq == GROUP * n_chan and width % (128 * n_seq) == 0 and cols % 128 == 0
        if fits and args[0].shape[0] % 128 == 0:
            return fused(n_seq, n_chan, *args)
        return body(*args)

    return jax.shard_map(device_part, mesh=mesh, in_specs=in_specs, out_specs=out_specs, check_vma=False)
```

```python
import functools
import math

import jax
import jax.numpy as jnp
import numpy as np
from jax import lax
from jax.experimental import pallas as pl
from jax.experimental.pallas import tpu as pltpu
from jax.sharding import PartitionSpec as P


def passed_along(value, axis, steps):
    count = lax.axis_size(axis)
    first, last = (max(0, -steps), min(count, count - steps))
    return lax.ppermute(value, axis, [(source, source + steps) for source in range(first, last)])


def broadcast(array, axis, root):
    mine = lax.axis_index(axis) == root
    return lax.psum(jnp.where(mine, array, jnp.zeros_like(array)), axis)


def dft_tables(length):
    count = 2 * length
    ramp = jnp.arange(count, dtype=jnp.int32)
    product = ramp[:, None] * ramp[None, :] % count
    angle = product.astype(jnp.float32) * (2.0 * math.pi / count)
    return (jnp.cos(angle), jnp.sin(angle))


def short_conv(rim, stream, taps):
    whole = jnp.concatenate([rim, stream], axis=0).astype(jnp.float32)
    return taps[0] * whole[2:] + taps[1] * whole[1:-1] + taps[2] * whole[:-2]


def spectrum(signal, cos_part, sin_part):
    real = jnp.einsum("nk,nc->kc", cos_part, signal, preferred_element_type=jnp.float32)
    imag = -jnp.einsum("nk,nc->kc", sin_part, signal, preferred_element_type=jnp.float32)
    return (real, imag)


def filter_spectrum(earlier, current, cos_part, sin_part):
    segment = jnp.concatenate([earlier, current], axis=0)
    real, imag = spectrum(segment, cos_part, sin_part)
    real16 = lax.optimization_barrier(real.astype(jnp.bfloat16))
    imag16 = lax.optimization_barrier(imag.astype(jnp.bfloat16))
    return (real16, imag16)


def invert(acc_re, acc_im, inv_cos, inv_sin):
    first = jnp.einsum("kt,...kc->...tc", inv_cos, acc_re, precision=lax.Precision.HIGHEST)
    return first - jnp.einsum("kt,...kc->...tc", inv_sin, acc_im, precision=lax.Precision.HIGHEST)


def body(query_in, key_in, value_in, short_taps, long_filter, skip_gain, out_weight):
    block = query_in.shape[0]
    width = query_in.shape[1]
    count = 2 * block
    rims = passed_along((query_in[-2:], key_in[-2:], value_in[-2:]), "seq", 1)
    gating = short_conv(rims[0], query_in, short_taps[0])
    keyed = short_conv(rims[1], key_in, short_taps[1])
    valued = short_conv(rims[2], value_in, short_taps[2])
    mixed = (keyed * valued).astype(jnp.bfloat16)
    cos_full, sin_full = dft_tables(block)
    fwd_cos = cos_full.astype(jnp.bfloat16)
    fwd_sin = sin_full.astype(jnp.bfloat16)
    inv_cos = cos_full[:, block:] / count
    inv_sin = sin_full[:, block:] / count
    empty = jnp.zeros((count, width), jnp.float32)

    def lag_spectrum(step_index, earlier):
        current = broadcast(long_filter, "seq", step_index)
        g_re, g_im = filter_spectrum(earlier, current, fwd_cos, fwd_sin)
        return (g_re, g_im, current)

    def one_round(step_index, carry):
        moving, earlier, acc_re, acc_im = carry
        g_re, g_im, earlier = lag_spectrum(step_index, earlier)
        g_re = g_re.astype(jnp.float32)
        g_im = g_im.astype(jnp.float32)
        u_re, u_im = spectrum(moving, fwd_cos[:block], fwd_sin[:block])
        acc_re = acc_re + g_re * u_re - g_im * u_im
        acc_im = acc_im + g_re * u_im + g_im * u_re
        moving = passed_along(moving, "seq", 1)
        return (moving, earlier, acc_re, acc_im)

    start_filter = jnp.zeros((block, width), jnp.bfloat16)
    final = lax.fori_loop(0, lax.axis_size("seq"), one_round, (mixed, start_filter, empty, empty))
    conv = invert(final[2], final[3], inv_cos, inv_sin)
    gated = (gating * (conv + skip_gain * mixed.astype(jnp.float32))).astype(jnp.bfloat16)
    partial_out = jnp.dot(
        gated,
        lax.all_gather(out_weight, "seq", axis=1, tiled=True),
        preferred_element_type=jnp.float32,
    )
    return lax.psum_scatter(
        partial_out.astype(jnp.bfloat16), "chan", scatter_dimension=1, tiled=True
    )


MESH_ID = pl.DeviceIdType.MESH
GROUP = 2
AHEAD = 3
LEAD = 1
EARLY = 6
MIDDLE = 6
PIECES = (8, 4)
SPLIT = 2
NOW = 4
TURN = (0, 1, 2, 3)
SCHEDULE = (
    "b0", "b1", "b2", "w6C", "b3", "r01", "r11", "r02", "r21", "r12", "r03", "r31", "10n", "10f", "r13", "20n",
    "20f", "11n", "11f", "r22", "r32", "21n", "21f", "r23", "12n", "12f", "30n", "30f", "22n", "22f", "r33",
    "13n", "10g", "31n", "31f", "11g", "23n", "13h", "12g", "20g", "21g", "23h", "22g", "32n", "32f", "33n",
    "30g", "31g", "33h", "32g",
)


def packed_tables(block):
    count = 2 * block
    ramp = np.arange(count)
    angle = (ramp[:, None] * ramp[None, :] % count) * (2.0 * math.pi / count)
    cosine, sine = np.cos(angle), np.sin(angle)
    forward = np.concatenate([cosine[:block], cosine[block : block + 1], -sine[1:block]], axis=0)
    weight = np.full((block, 1), 2.0)
    weight[0] = 1.0
    inverse = np.concatenate(
        [weight * cosine[:block, block:], cosine[block : block + 1, block:], -2.0 * sine[1:block, block:]], axis=0
    ) / count
    return jnp.asarray(forward, jnp.bfloat16), jnp.asarray(inverse.T, jnp.float32).astype(jnp.bfloat16)


def remote(src, dst, send, recv, seq, chan):
    return pltpu.make_async_remote_copy(
        src_ref=src, dst_ref=dst, send_sem=send, recv_sem=recv, device_id={"seq": seq, "chan": chan}, device_id_type=MESH_ID
    )


def kernel(
    n_seq, n_chan, q_hbm, k_hbm, v_hbm, taps_hbm, f_ref, skip_hbm, w_hbm, fwd_hbm, inv_hbm, out_ref,
    qkv_ref, taps_ref, skip_ref, w_ref, fwd_ref, inv_ref, in_sem,
    mine, rim_out, rim_in, mix, filt, gate, spec_u, spec_g, acc, gated, half_out, rows, w_far, part, r1_out, r1_in,
    r2_out, r2_in, r3_out,
    a_send, a_recv, rim_sem, w_sem, x_send, x_recv, z_send, up_recv, dn_recv, r_send, r1_recv, r2_recv, o_recv,
):
    s, c = lax.axis_index("seq"), lax.axis_index("chan")
    block, width = f_ref.shape
    for i, src in enumerate((q_hbm, k_hbm, v_hbm)):
        pltpu.make_async_copy(src, qkv_ref.at[i], in_sem.at[0]).start()
    loads = [
        pltpu.make_async_copy(src, dst, in_sem.at[1 + i])
        for i, (src, dst) in enumerate((
            (taps_hbm, taps_ref), (skip_hbm, skip_ref), (fwd_hbm, fwd_ref), (inv_hbm, inv_ref), (w_hbm, w_ref),
        ))
    ]
    for load in loads:
        load.start()
    lines = n_seq // GROUP
    z, x = s // GROUP, s % GROUP
    y, core = c // 2, c % 2
    sub = width // n_seq
    wide = GROUP * sub
    cols = w_ref.shape[1]
    px, pc, py = z * GROUP + (1 - x), y * 2 + (1 - core), (1 - y) * 2 + core

    def lanes(index, size):
        return pl.ds(pl.multiple_of(index * size, size), size)

    barrier = pltpu.get_barrier_semaphore()
    for d in range(1, n_seq):
        pl.semaphore_signal(barrier, inc=1, device_id={"seq": lax.rem(s + d, n_seq), "chan": c}, device_id_type=MESH_ID)
    for other in (pc, py):
        pl.semaphore_signal(barrier, inc=1, device_id={"seq": s, "chan": other}, device_id_type=MESH_ID)
    for other in range(n_chan):
        @pl.when(jnp.logical_or(z != c, other != c))
        def _():
            pl.semaphore_signal(barrier, inc=1, device_id={"seq": c * GROUP + x, "chan": other}, device_id_type=MESH_ID)
    own_filter = pltpu.make_async_copy(f_ref.at[:, lanes(s, sub)], filt.at[:, lanes(s + 1, sub)], in_sem.at[1 + len(loads)])
    own_filter.start()
    filt[:, :sub] = jnp.zeros((block, sub), filt.dtype)
    pl.semaphore_wait(barrier, n_seq - 1 + 2 + n_chan - (z == c).astype(jnp.int32))

    def partner(d):
        return lax.rem(s + d, n_seq)

    def exchange(kind, d, src, dst):
        to = partner(d)
        return remote(src, dst.at[:, lanes(s + (1 if kind == 0 else 0), sub)], a_send.at[min(kind, 1)], a_recv.at[kind], to, c)

    order = list(range(1, n_seq))

    def send_filter(chosen):
        for d in chosen:
            exchange(0, d, f_ref.at[:, lanes(partner(d), sub)], filt).start()

    send_filter(order[:AHEAD])
    pltpu.make_async_copy(qkv_ref, qkv_ref, in_sem.at[0]).wait()
    tail = block - 16
    row16 = lax.broadcasted_iota(jnp.int32, (16, width), 0)
    tails = [pltpu.roll(ref[tail:, :].astype(jnp.float32), 2 + 2 * i, 0) for i, ref in enumerate(qkv_ref.at[j] for j in range(3))]
    rim_out[...] = jnp.where(row16 < 2, tails[0], jnp.where(row16 < 4, tails[1], tails[2])).astype(jnp.bfloat16)
    rim = remote(rim_out, rim_in, rim_sem.at[0], rim_sem.at[1], lax.rem(s + 1, n_seq), c)

    @pl.when(s < n_seq - 1)
    def _():
        rim.start()

    send_filter(order[AHEAD:])

    split = cols * SPLIT // 4
    spans = (pl.ds(0, cols), pl.ds(0, split), pl.ds(split, cols - split), pl.ds(0, cols))
    chunks = [(e, r) for e, count in zip((1, 2), PIECES) for r in range(count)]

    def share_weights(first, last):
        for i in range(first, last):
            e, r = chunks[i]
            depth = width // PIECES[e - 1]
            at = (pl.ds(r * depth, depth), spans[e])
            remote(w_hbm.at[at], w_far.at[at], w_sem.at[0], w_sem.at[e], px, c).start()

    share_weights(0, LEAD)
    loads[0].wait()

    @pl.when(s < n_seq - 1)
    def _():
        rim.wait_send()

    @pl.when(s > 0)
    def _():
        rim.wait_recv()

    row = lax.broadcasted_iota(jnp.int32, (block, sub), 0)
    started = s > 0

    def filtered(stream, here):
        x0 = qkv_ref[stream, :, here].astype(jnp.float32)
        edge = jnp.where(started, rim_in[:, here].astype(jnp.float32), 0.0)
        r0, r1 = edge[2 * stream : 2 * stream + 1], edge[2 * stream + 1 : 2 * stream + 2]
        x1 = jnp.where(row == 0, r1, pltpu.roll(x0, 1, 0))
        x2 = jnp.where(row == 0, r0, jnp.where(row == 1, r1, pltpu.roll(x0, 2, 0)))
        t = taps_ref[stream, :, here]
        return t[0:1] * x0 + t[1:2] * x1 + t[2:3] * x2

    def send_all(kind, dst, value_of):
        for d in order + [0]:
            here = lanes(partner(d), sub)
            value = value_of(here).astype(jnp.bfloat16)
            if d == 0:
                dst[:, lanes(s, sub)] = value
            else:
                mine[kind - 1, :, here] = value
                copy = exchange(kind, d, mine.at[kind - 1, :, here], dst)
                copy.start()

    send_all(1, mix, lambda here: filtered(1, here) * filtered(2, here))
    send_all(2, gate, lambda here: filtered(0, here))
    share_weights(LEAD, EARLY)
    own_filter.wait()
    loads[2].wait()
    peers = slice(0, (n_seq - 1) * sub)

    def arrival(kind):
        share = mine.at[0, :, peers]
        return remote(share, share, a_send.at[0], a_recv.at[kind], s, c)

    arrival(0).wait_recv()
    segments = jnp.concatenate([filt[:, : n_seq * sub], filt[:, sub:]], axis=0)
    spec_g[...] = jnp.dot(fwd_ref[...], segments, preferred_element_type=jnp.float32).astype(jnp.bfloat16).astype(jnp.float32)
    arrival(1).wait_recv()
    share_weights(EARLY, MIDDLE)
    spec_u[...] = jnp.dot(fwd_ref[:, :block], mix[...], preferred_element_type=jnp.float32)

    def strip(r, carry):
        at = pl.ds(pl.multiple_of(r * 8, 8), 8)
        under = pl.ds(pl.multiple_of(block + r * 8, 8), 8)
        first = lax.broadcasted_iota(jnp.int32, (8, sub), 0) + r * 8 == 0
        part_of = [slice(b * sub, (b + 1) * sub) for b in range(n_seq)]
        u_re = [spec_u[at, here] for here in part_of]
        u_im = [spec_u[under, here] for here in part_of]
        g_re = [spec_g[at, here] for here in part_of]
        g_im = [spec_g[under, here] for here in part_of]
        g_no = [jnp.where(first, 0.0, im) for im in g_im]
        g_on = [jnp.where(first, im, re) for re, im in zip(g_re, g_im)]
        for b in range(n_seq):
            total_re = g_re[0] * u_re[b] - g_no[0] * u_im[b]
            total_im = g_on[0] * u_im[b] + g_no[0] * u_re[b]
            for m in range(1, b + 1):
                total_re += g_re[m] * u_re[b - m] - g_no[m] * u_im[b - m]
                total_im += g_on[m] * u_im[b - m] + g_no[m] * u_re[b - m]
            acc[at, part_of[b]] = total_re
            acc[under, part_of[b]] = total_im
        return carry

    lax.fori_loop(0, block // 8, strip, 0)
    loads[1].wait()
    loads[3].wait()
    conv = jnp.dot(inv_ref[...], acc[...].astype(jnp.bfloat16), preferred_element_type=jnp.float32)
    gain = jnp.concatenate([skip_ref[:, lanes(s, sub)]] * n_seq, axis=1)
    acc[:block, :] = conv + gain * mix[...].astype(jnp.float32)
    arrival(2).wait_recv()
    x_copies = {}
    top = z == lines - 1
    bottom = z == 0

    def along(p, h, up):
        slot = jnp.clip(z - (h - 1), 0, lines - 1) if up else jnp.clip(z + (h - 1), 0, lines - 1)
        piece = rows.at[pl.ds(p * block, block), lanes(slot, wide)]
        to = jnp.minimum(z + 1, lines - 1) if up else jnp.maximum(z - 1, 0)
        send, recv = (z_send.at[0], up_recv) if up else (z_send.at[1], dn_recv)
        return remote(piece, piece, send, recv.at[p, h - 1], to * GROUP + x, c)

    early = range(NOW)
    late = range(NOW, lines)

    def start_half(p, owner):
        piece = rows.at[pl.ds(p * block, block), lanes(owner, sub)]
        for up, blocked, to in ((True, top, jnp.minimum(z + 1, lines - 1)), (False, bottom, jnp.maximum(z - 1, 0))):
            @pl.when(jnp.logical_not(blocked))
            def _():
                send, recv = (z_send.at[0], up_recv) if up else (z_send.at[1], dn_recv)
                remote(piece, piece, send, recv.at[p, 0], to * GROUP + x, c).start()

    for p in TURN:
        for e in range(GROUP):
            here = slice(p * wide + e * sub, p * wide + (e + 1) * sub)
            value = gate[:, here].astype(jnp.float32) * acc[:block, here]
            gated[e] = value.astype(jnp.bfloat16)
        half_out[p] = gated[1 - x]
        rows[pl.ds(p * block, block), lanes(s, sub)] = gated[x]
        copy = remote(half_out.at[p], rows.at[pl.ds(p * block, block), lanes(s, sub)], x_send.at[0], x_recv.at[p], px, c)
        copy.start()
        x_copies[p] = copy
    for p in early:
        start_half(p, s)
    r1, r2, far_seen = {}, {}, []
    half, quarter = block // 2, block // 4
    loads[4].wait()

    def columns(e):
        first = split if e == 2 else 0
        return pl.ds(pl.multiple_of((x if e == 0 else 1 - x) * cols + first, 128), spans[e].size)

    def held(ref, p, e, where=slice(None)):
        return ref.at[p + min(e, 1) * lines, where, spans[e]]

    def place(p, e):
        return min(e, 2) * lines + p

    def stage_one(p, e):
        for i in ((), (1,), (2,), (1, 2))[e]:
            if i not in far_seen:
                far_seen.append(i)
                whole = w_far.at[:, spans[i]]
                remote(whole, whole, w_sem.at[0], w_sem.at[i], px, c).wait_recv()
        lhs = rows[pl.ds(p * block, block), :]
        weight = w_ref[...] if e == 0 else w_far[:, spans[e]]
        held(part, p, e)[...] = jnp.dot(lhs, weight, preferred_element_type=jnp.float32)
        away = pl.ds(pl.multiple_of((1 - core) * half, half), half)
        held(r1_out, p, e)[...] = held(part, p, e, away)[...].astype(jnp.bfloat16)
        r1[p, e] = remote(held(r1_out, p, e), held(r1_in, p, e), r_send.at[0], r1_recv.at[place(p, e)], s, pc)
        r1[p, e].start()

    def stage_two(p, e):
        r1[p, e].wait_recv()
        away = pl.multiple_of((1 - y) * quarter, quarter)
        base = pl.multiple_of(core * half, half)
        held(r2_out, p, e)[...] = (
            held(part, p, e, pl.ds(base + away, quarter))[...]
            + held(r1_in, p, e, pl.ds(away, quarter))[...].astype(jnp.float32)
        ).astype(jnp.bfloat16)
        r2[p, e] = remote(held(r2_out, p, e), held(r2_in, p, e), r_send.at[1], r2_recv.at[place(p, e)], s, py)
        r2[p, e].start()

    strip_at = pl.ds(pl.multiple_of((core * 2 + y) * quarter, quarter), quarter)

    def last_copy(p, e):
        return remote(held(r3_out, p, e), out_ref.at[strip_at, columns(e)], r_send.at[2], o_recv.at[0], p * GROUP + x, z)

    def stage_three(p, e):
        r2[p, e].wait_recv()
        near = pl.multiple_of(y * quarter, quarter)
        base = pl.multiple_of(core * half, half)
        held(r3_out, p, e)[...] = (
            held(part, p, e, pl.ds(base + near, quarter))[...]
            + held(r1_in, p, e, pl.ds(near, quarter))[...].astype(jnp.float32)
            + held(r2_in, p, e)[...].astype(jnp.float32)
        ).astype(jnp.bfloat16)
        own = jnp.logical_and(z == c, z == p)

        @pl.when(own)
        def _():
            pltpu.make_async_copy(held(r3_out, p, e), out_ref.at[strip_at, columns(e)], r_send.at[2]).start()

        @pl.when(jnp.logical_not(own))
        def _():
            last_copy(p, e).start()

    def begin(batch):
        for p in batch:
            if p in late:
                start_half(p, s)
            x_copies[p].wait_recv()
            start_half(p, px)

    def relay(batch, h):
        for p in batch:
            for up, blocked, reach in ((True, top, z >= h), (False, bottom, z + h < lines)):
                @pl.when(reach)
                def _():
                    slot = z - h if up else z + h
                    piece = rows.at[pl.ds(p * block, block), lanes(slot, wide)]
                    recv = (up_recv if up else dn_recv).at[p, h - 1]
                    remote(piece, piece, z_send.at[0], recv, s, c).wait_recv()

                if h < lines - 1:
                    @pl.when(jnp.logical_and(reach, jnp.logical_not(blocked)))
                    def _():
                        along(p, h + 1, up).start()


    def out_wait():
        for local, size in ((False, block), (True, block - quarter)):
            @pl.when((z == c) == local)
            def _():
                landed = out_ref.at[pl.ds(0, size), :]
                remote(landed, landed, r_send.at[2], o_recv.at[0], s, c).wait_recv()

    def send_wait():
        share = mine.at[0, :, peers]
        remote(share, share, a_send.at[0], a_recv.at[0], s, c).wait_send()
        share = mine.at[:, :, peers]
        remote(share, share, a_send.at[1], a_recv.at[0], s, c).wait_send()
        remote(w_hbm, w_far, w_sem.at[0], w_sem.at[1], px, c).wait_send()
        remote(half_out, half_out, x_send.at[0], x_recv.at[0], px, c).wait_send()
        for count in range(1, lines):
            gone = rows.at[:, pl.ds(0, count * wide)]
            for i, here in enumerate((z + 1 == count, lines - z == count)):
                @pl.when(here)
                def _():
                    remote(gone, gone, z_send.at[i], up_recv.at[0, 0], s, c).wait_send()
        for i, done in enumerate((r1_out, r2_out, r3_out)):
            remote(done, done, r_send.at[i], o_recv.at[0], s, c).wait_send()

    for act in SCHEDULE:
        kind, p = act[0], int(act[1])
        if kind != "w":
            p = TURN[p]
        if kind == "b":
            begin([p])
        elif kind == "r":
            relay([p], int(act[2]))
        elif kind == "w":
            share_weights(p, int(act[2], 16))
        else:
            stage = {"1": stage_one, "2": stage_two, "3": stage_three}[kind]
            stage(p, "nfgh".index(act[2]))
    out_wait()
    send_wait()


def fused(n_seq, n_chan, query_in, key_in, value_in, short_taps, long_filter, skip_gain, out_weight):
    block, width = query_in.shape
    sub = width // n_seq
    lines = n_seq // GROUP
    cols = out_weight.shape[1]
    count = 2 * block
    forward, inverse = packed_tables(block)
    bf16, f32 = jnp.bfloat16, jnp.float32
    dma = pltpu.SemaphoreType.DMA
    units = GROUP * lines
    return pl.pallas_call(
        functools.partial(kernel, n_seq, n_chan),
        out_shape=pltpu.VMEM((block, GROUP * cols), bf16),
        in_specs=[pl.BlockSpec(memory_space=pl.ANY)] * 9,
        out_specs=pl.BlockSpec(memory_space=pltpu.VMEM),
        scratch_shapes=[
            pltpu.VMEM((3, block, width), bf16),
            pltpu.VMEM(short_taps.shape, f32),
            pltpu.VMEM((1, width), f32),
            pltpu.VMEM((width, cols), bf16),
            pltpu.VMEM(forward.shape, bf16),
            pltpu.VMEM(inverse.shape, bf16),
            dma((7,)),
            pltpu.VMEM((2, block, width), bf16),
            pltpu.VMEM((16, width), bf16),
            pltpu.VMEM((16, width), bf16),
            pltpu.VMEM((block, n_seq * sub), bf16),
            pltpu.VMEM((block, (n_seq + 1) * sub), bf16),
            pltpu.VMEM((block, n_seq * sub), bf16),
            pltpu.VMEM((count, n_seq * sub), f32),
            pltpu.VMEM((count, n_seq * sub), f32),
            pltpu.VMEM((count, n_seq * sub), f32),
            pltpu.VMEM((GROUP, block, sub), bf16),
            pltpu.VMEM((lines, block, sub), bf16),
            pltpu.VMEM((lines * block, width), bf16),
            pltpu.VMEM((width, cols), bf16),
            pltpu.VMEM((units, block, cols), f32),
            pltpu.VMEM((units, block // 2, cols), bf16),
            pltpu.VMEM((units, block // 2, cols), bf16),
            pltpu.VMEM((units, block // 4, cols), bf16),
            pltpu.VMEM((units, block // 4, cols), bf16),
            pltpu.VMEM((units, block // 4, cols), bf16),
            dma((2,)),
            dma((3,)),
            dma((2,)),
            dma((3,)),
            dma((1,)),
            dma((lines,)),
            dma((2,)),
            dma((lines, lines - 1)),
            dma((lines, lines - 1)),
            dma((3,)),
            dma((3 * lines,)),
            dma((3 * lines,)),
            dma((1,)),
        ],
        compiler_params=pltpu.CompilerParams(collective_id=0, has_side_effects=True, vmem_limit_bytes=60 * 2**20),
    )(
        query_in, key_in, value_in, short_taps, long_filter, skip_gain.reshape(1, width), out_weight,
        forward, inverse,
    )


def solution(mesh):
    in_specs = (
        P("seq", "chan"),
        P("seq", "chan"),
        P("seq", "chan"),
        P(None, None, "chan"),
        P("seq", "chan"),
        P("chan"),
        P("chan", "seq"),
    )
    out_specs = P("seq", "chan")
    n_seq, n_chan = mesh.shape["seq"], mesh.shape["chan"]

    def device_part(*args):
        width, cols = args[0].shape[1], args[-1].shape[1]
        fits = n_chan == 4 and n_seq == GROUP * n_chan and width % (128 * n_seq) == 0 and cols % 128 == 0
        if fits and args[0].shape[0] % 128 == 0:
            return fused(n_seq, n_chan, *args)
        return body(*args)

    return jax.shard_map(device_part, mesh=mesh, in_specs=in_specs, out_specs=out_specs, check_vma=False)
```
